32 devices in a mesh: group: 4 (over y, x), dp: 8 (over z, core).
Axes of the slice: x: 2, y: 2, z: 4, core: 2. Of those that a mesh axis runs over, the one named last changes fastest.
Arguments:
- tokens: bfloat16 [128, 320, 1024], P(('group', 'dp')), may hold values from -16 to 16
- keep: int32 [128, 256], P(('group', 'dp')), may hold values from 0 to 1, as said below
- cotangent: bfloat16 [128, 320, 1024], P(('group', 'dp')), may hold values from -6 to 6
- master_matrices: float32 [1024, 8192], P('group'), may hold values from -0.5 to 0.5
- master_down: float32 [4096, 1024], P('group'), may hold values from -0.09375 to 0.09375
- master_vectors: float32 [12, 1024], P(None, 'group'), may hold values from -1 to 2
- first_matrices: float32 [1024, 8192], P('group'), may hold values from -274.230852 to 274.230852
- first_down: float32 [4096, 1024], P('group'), may hold values from -228.52571 to 228.52571
- first_vectors: float32 [12, 1024], P(None, 'group'), may hold values from -457.05142 to 457.05142
- second_matrices: float32 [1024, 8192], P('group'), may hold values from 146.88 to 18800.64
- second_down: float32 [4096, 1024], P('group'), may hold values from 1632 to 13056
- second_vectors: float32 [12, 1024], P(None, 'group'), may hold values from 6528 to 52224
Outputs:
- block_output: bfloat16 [128, 320, 1024], P(('group', 'dp'))
- input_grad: float32 [128, 320, 1024], P(('group', 'dp'))
- new_matrices: float32 [1024, 8192], P('group')
- new_down: float32 [4096, 1024], P('group')
- new_vectors: float32 [12, 1024], P(None, 'group')
- new_first_matrices: float32 [1024, 8192], P('group')
- new_first_down: float32 [4096, 1024], P('group')
- new_first_vectors: float32 [12, 1024], P(None, 'group')
- new_second_matrices: float32 [1024, 8192], P('group')
- new_second_down: float32 [4096, 1024], P('group')
- new_second_vectors: float32 [12, 1024], P(None, 'group')
- copy_matrices: bfloat16 [1024, 8192], P('group')
- copy_down: bfloat16 [4096, 1024], P('group')
- copy_vectors: bfloat16 [12, 1024], P(None, 'group')
- branch_rms: float32 [3], replicated
The draws below stay inside these ranges and needn't reach their ends.
Inputs may be any that keep to these rules, and one draw needn't show every extreme that they name: `keep`: each row keeps between 0 and 77 of its image tokens; some row keeps none and some keeps exactly 77.
All inputs are finite; a program needn't handle non-finite values.
Results may differ from the reference program's by a relative error of at most 0.009.
The reference program's roundings to bfloat16 on the way count: a program that leaves them out, or rounds other values in their place, can miss the bound.
Values may be sent and summed in bfloat16 or wider, within the bound.
A program may use at most 384 MiB of HBM per device.

```python
import math
import jax
import jax.numpy as jnp
from jax import lax

D = 1024
HEADS = 16
HEAD = 64
FF = 4096
BUF = 64
IMG = 256
STEP = 7
L = 320
KEEP_MAX = 77
SEQS = 128
KEPT_ROWS = 13056


def seq_scale(rising):
    position = jnp.arange(SEQS, dtype=jnp.float32) / (SEQS - 1)
    return 1.0 + rising * position


def base_values(key, shape, limit):
    return jnp.clip(jax.random.normal(key, shape, jnp.float32), -limit, limit)


def column_scale(factors):
    column = jnp.arange(4 * D + FF)
    return jnp.where(column < 2 * D, factors[0], jnp.where(column < 3 * D, factors[1], jnp.where(column < 4 * D, factors[2], factors[3])))


def draw_tokens(key, part):
    scales = seq_scale(2.0)
    values = base_values(key, (SEQS, L, D), 4.0)
    return (values * scales[:, None, None]).astype(jnp.bfloat16)


def draw_keep(key, part):
    count_key, order_key = jax.random.split(key)
    counts = jax.random.randint(count_key, (SEQS,), 0, KEEP_MAX + 1)
    counts = counts.at[0].set(0).at[SEQS - 1].set(KEEP_MAX)
    order_keys = jax.random.split(order_key, SEQS)
    rankings = jax.vmap(lambda single: jax.random.permutation(single, IMG))(order_keys)
    return (rankings < counts[:, None]).astype(jnp.int32)


def draw_master_matrices(key, part):
    scales = column_scale((1.4, 1.0, 4.0, 1.0)) / math.sqrt(D)
    values = base_values(key, (D, 4 * D + FF), 4.0)
    return (values * scales[None, :]).astype(jnp.float32)


def draw_master_vectors(key, part):
    row_index = jnp.arange(12)[:, None]
    gain_rows = (row_index == 0) | (row_index == 5)
    base_draw = jnp.clip(jax.random.normal(key, (12, D), jnp.float32), -3.0, 3.0)
    gains = 1.0 + 0.2 * base_draw
    shifts = 0.3 * base_draw
    return jnp.where(gain_rows, gains, shifts).astype(jnp.float32)


def draw_first_matrices(key, part):
    scales = column_scale((0.25, 0.6, 0.15, 0.25)) * math.sqrt(KEPT_ROWS)
    values = base_values(key, (D, 4 * D + FF), 4.0)
    return (values * scales[None, :]).astype(jnp.float32)


def draw_second_matrices(key, part):
    scales = column_scale((0.0625, 0.36, 0.0225, 0.0625)) * KEPT_ROWS
    factor = jnp.exp(jax.random.uniform(key, (D, 4 * D + FF), jnp.float32, math.log(0.5), math.log(4.0)))
    return (factor * scales[None, :]).astype(jnp.float32)


def block_scale(rng, extent, shards, least, top_value):
    level, own = 1.0, jax.random.fold_in(rng, 6)
    for dim, parts in shards:
        draws = jnp.exp(jax.random.uniform(jax.random.fold_in(own, dim), (parts,), jnp.float32, least / len(shards), top_value / len(shards)))
        level = level * jnp.repeat(draws, extent[dim] // parts).reshape([-1 if axis == dim else 1 for axis in range(len(extent))])
    return level


def scatter_about(stream_key, dims, scale, bound, cuts=(), kind=jnp.bfloat16):
    loudness = block_scale(stream_key, dims, cuts, -0.22, 0.18) if cuts else 1.0
    drawn = jax.random.normal(stream_key, dims, jnp.float32) * scale * loudness
    return jnp.minimum(jnp.maximum(drawn, -bound), bound).astype(kind)


def setup_inputs(seed: int = 0) -> dict:
    arg_keys = jax.random.split(jax.random.key(seed), 13)
    tokens = draw_tokens(jax.random.fold_in(arg_keys[12], 71), 0)
    keep = draw_keep(jax.random.fold_in(arg_keys[12], 71), 0)
    cotangent = scatter_about(arg_keys[2], (SEQS, L, D), 1.0, 6.0, ((0, 32),))
    master_matrices = draw_master_matrices(jax.random.fold_in(arg_keys[12], 71), 0)
    master_down = scatter_about(arg_keys[4], (FF, D), FF ** -0.5, 0.09375, ((0, 4),), jnp.float32)
    master_vectors = draw_master_vectors(jax.random.fold_in(arg_keys[12], 71), 0)
    first_matrices = draw_first_matrices(jax.random.fold_in(arg_keys[12], 71), 0)
    first_down = scatter_about(arg_keys[7], (FF, D), (0.5 * KEPT_ROWS ** 0.5), 228.52571, ((0, 4),), jnp.float32)
    first_vectors = scatter_about(arg_keys[8], (12, D), (KEPT_ROWS ** 0.5), 457.05142, ((1, 4),), jnp.float32)
    second_matrices = draw_second_matrices(jax.random.fold_in(arg_keys[12], 71), 0)
    second_down = jnp.clip(jnp.exp(math.log(13056.0) - 2.0794415 * jax.random.uniform(arg_keys[10], (FF, D), jnp.float32) ** block_scale(arg_keys[10], (FF, D), ((0, 4),), -0.2, 0.2)), 1632.0, 13056.0)
    second_vectors = jnp.clip(jnp.exp(math.log(52224.0) - 2.0794415 * jax.random.uniform(arg_keys[11], (12, D), jnp.float32) ** block_scale(arg_keys[11], (12, D), ((1, 4),), -0.2, 0.2)), 6528.0, 52224.0)
    return dict(tokens=tokens, keep=keep, cotangent=cotangent, master_matrices=master_matrices, master_down=master_down, master_vectors=master_vectors, first_matrices=first_matrices, first_down=first_down, first_vectors=first_vectors, second_matrices=second_matrices, second_down=second_down, second_vectors=second_vectors)


norm_epsilon = 1e-06
beta_first = 0.5
beta_second = 0.5
adam_epsilon = 1e-08
rate_matrix = 0.05
rate_vector = 0.3
weight_decay = 0.05
root_half = 0.7071067811865476

@jax.custom_vjp
def low(v):
    return lax.optimization_barrier(v.astype(jnp.bfloat16)).astype(jnp.float32)

@jax.custom_vjp
def low_back(v):
    return v

def low_keep(v):
    return (low(v), None)

def low_pass(kept, grad):
    return (grad,)

def back_keep(v):
    return (v, None)

def back_low(kept, grad):
    return (low(grad),)
low.defvjp(low_keep, low_pass)
low_back.defvjp(back_keep, back_low)

def matmul(left, right):
    return jnp.dot(left, right, preferred_element_type=jnp.float32, precision=lax.Precision.HIGHEST)

def layer_norm(values, gain, shift):
    centre = lax.optimization_barrier(jnp.mean(values, axis=-1, keepdims=True))
    centred = values - centre
    variance = lax.optimization_barrier(jnp.mean(centred * centred, axis=-1, keepdims=True))
    return centred * lax.rsqrt(variance + norm_epsilon) * gain + shift

def gelu_exact(values):
    return 0.5 * values * (1.0 + lax.erf(values * root_half))

def block_forward(token_rows, slots, matrices, down, vectors):
    count_seq, length, features = token_rows.shape
    row_count = count_seq * length
    head_shape = (count_seq, length, HEADS, HEAD)
    inputs = token_rows.reshape(row_count, features)
    slot_mask = slots.reshape(row_count, 1)
    normed_one = low(layer_norm(inputs, vectors[0], vectors[1]))
    qkv_all = matmul(normed_one, matrices[:, :3 * features])
    queries = low(low_back(qkv_all[:, :features] + vectors[2]))
    key_heads = low(low_back(qkv_all[:, features:2 * features]))
    value_heads = low(low_back(qkv_all[:, 2 * features:] + vectors[3]))
    raw = jnp.einsum('sqhd,skhd->shqk', queries.reshape(head_shape), key_heads.reshape(head_shape), precision=lax.Precision.HIGHEST)
    scores = low_back(raw * (1.0 / math.sqrt(HEAD)))
    scores = jnp.where(slots[:, None, None, :] > 0.5, scores, -1e+30)
    row_max = lax.optimization_barrier(jnp.max(scores, axis=-1, keepdims=True))
    exponent = jnp.exp(scores - row_max)
    probs_low = low(exponent / lax.optimization_barrier(jnp.sum(exponent, axis=-1, keepdims=True)))
    attended = jnp.einsum('shqk,skhd->sqhd', probs_low, value_heads.reshape(head_shape), precision=lax.Precision.HIGHEST)
    attended = low(low_back(attended.reshape(row_count, features)))
    branch = low_back(matmul(attended, matrices[:, 3 * features:4 * features]) + vectors[4])
    resid = inputs + branch
    normed_two = low(layer_norm(resid, vectors[5], vectors[6]))
    up_value = low_back(matmul(normed_two, matrices[:, 4 * features:]) + vectors[8:12].reshape(-1))
    activated = low(gelu_exact(up_value))
    mlp_out = low_back(matmul(activated, down) + vectors[7])
    result = ((resid + mlp_out) * slot_mask).reshape(count_seq, length, features)
    squares = jnp.stack([jnp.sum(inputs * inputs * slot_mask), jnp.sum(branch * branch * slot_mask), jnp.sum(mlp_out * mlp_out * slot_mask)])
    return (result, squares)

def adam_step(master, first, second, grad, rate, decay):
    first_new = beta_first * first + (1.0 - beta_first) * grad
    second_new = beta_second * second + (1.0 - beta_second) * grad * grad
    fix_first = 1.0 - beta_first ** STEP
    fix_second = 1.0 - beta_second ** STEP
    update = first_new / fix_first / (jnp.sqrt(second_new / fix_second) + adam_epsilon)
    return (master - rate * (update + decay * master), first_new, second_new)

def reference(tokens, keep, cotangent, master_matrices, master_down, master_vectors, first_matrices, first_down, first_vectors, second_matrices, second_down, second_vectors):
    seq_count = tokens.shape[0]
    block_size = math.gcd(seq_count, 8)
    block_count = seq_count // block_size
    slots = jnp.concatenate([jnp.ones((seq_count, BUF), jnp.float32), keep.astype(jnp.float32)], axis=1)
    token_blocks = tokens.astype(jnp.float32).reshape(block_count, block_size, L, D)
    slot_blocks = slots.reshape(block_count, block_size, L)

    def forward(token_all, matrices, down, vectors):
        low_matrices = low(matrices)
        low_down = low(down)
        low_vectors = low(vectors)

        def block_step(pair):
            return block_forward(pair[0], pair[1], low_matrices, low_down, low_vectors)
        outputs, squares = lax.map(jax.checkpoint(block_step), (token_all, slot_blocks))
        return (outputs, lax.optimization_barrier(jnp.sum(squares, axis=0)))
    outputs, pullback, squares = jax.vjp(forward, token_blocks, master_matrices, master_down, master_vectors, has_aux=True)
    grad_tokens, grad_matrices, grad_down, grad_vectors = pullback(cotangent.astype(jnp.float32).reshape(block_count, block_size, L, D))
    count_kept = jnp.sum(slots)
    branch_rms = jnp.sqrt(squares / (count_kept * D))
    new_matrices, new_first_matrices, new_second_matrices = adam_step(master_matrices, first_matrices, second_matrices, grad_matrices, rate_matrix, weight_decay)
    new_down, new_first_down, new_second_down = adam_step(master_down, first_down, second_down, grad_down, rate_matrix, weight_decay)
    new_vectors, new_first_vectors, new_second_vectors = adam_step(master_vectors, first_vectors, second_vectors, grad_vectors, rate_vector, 0.0)
    return (outputs.reshape(seq_count, L, D).astype(jnp.bfloat16), grad_tokens.reshape(seq_count, L, D), new_matrices, new_down, new_vectors, new_first_matrices, new_first_down, new_first_vectors, new_second_matrices, new_second_down, new_second_vectors, new_matrices.astype(jnp.bfloat16), new_down.astype(jnp.bfloat16), new_vectors.astype(jnp.bfloat16), branch_rms)
```

```python
import functools
import math

import jax
import jax.numpy as jnp
from jax import lax
from jax.experimental import pallas as pl
from jax.experimental.pallas import tpu as pltpu
from jax.sharding import PartitionSpec as P

HEAD = 64
STEP = 7
KEEP_MAX = 77

norm_epsilon = 1e-06
beta_first = 0.5
beta_second = 0.5
adam_epsilon = 1e-08
rate_matrix = 0.05
rate_vector = 0.3
weight_decay = 0.05
root_half = 0.7071067811865476
inverse_root_two_pi = 0.3989422804014327

bf16 = jnp.bfloat16
f32 = jnp.float32
BOTH = ("group", "dp")
VMEM_SPEC = pl.BlockSpec(memory_space=pltpu.VMEM)
SMEM_SPEC = pl.BlockSpec(memory_space=pltpu.SMEM)
ANY_SPEC = pl.BlockSpec(memory_space=pl.ANY)
MIB = 1 << 20


def mm(a, b):
    return jnp.dot(a, b, preferred_element_type=f32)


def mm_nt(a, b):
    return lax.dot_general(a, b, (((1,), (1,)), ((), ())), preferred_element_type=f32)


def mm_tn(a, b):
    return lax.dot_general(a, b, (((0,), (0,)), ((), ())), preferred_element_type=f32)


def sds(shape, dtype):
    return jax.ShapeDtypeStruct(shape, dtype)


def params(mib, **more):
    return pltpu.CompilerParams(vmem_limit_bytes=mib * MIB, **more)


def cost(flops, nbytes):
    return pl.CostEstimate(flops=int(flops), bytes_accessed=int(nbytes), transcendentals=0)


def layer_stats(values):
    centre = jnp.mean(values, axis=-1, keepdims=True)
    centred = values - centre
    variance = jnp.mean(centred * centred, axis=-1, keepdims=True)
    inverse = lax.rsqrt(variance + norm_epsilon)
    return centred * inverse, inverse


def norm_back(grad_normed, normal, inverse, gain):
    scaled = grad_normed * gain
    mean_one = jnp.mean(scaled, axis=-1, keepdims=True)
    mean_two = jnp.mean(scaled * normal, axis=-1, keepdims=True)
    return inverse * (scaled - mean_one - normal * mean_two)


def picker(keep_row, rows):
    image = keep_row.shape[1]
    ahead = lax.broadcasted_iota(jnp.int32, (image, image), 0)
    here = lax.broadcasted_iota(jnp.int32, (image, image), 1)
    upper = jnp.where(ahead <= here, 1.0, 0.0).astype(bf16)
    kept = keep_row.astype(f32)
    place = mm(kept.astype(bf16), upper) - 1.0
    place = jnp.where(kept > 0.5, place, -1.0)
    want = lax.broadcasted_iota(jnp.int32, (rows, image), 0).astype(f32)
    return jnp.where(place == want, 1.0, 0.0).astype(bf16)


def pack_kernel(buf, info, keep, tokens, cot, v0, v1, v2, v3, x_out, em_out, h_out, vec_out, vec):
    step = pl.program_id(0)
    part = v0.shape[1]

    @pl.when(step == 0)
    def _():
        for flip, piece in enumerate((v0, v1, v2, v3)):
            place = pl.multiple_of((info[0] ^ flip) * part, part)
            vec[0:12, pl.ds(place, part)] = piece[...].astype(f32)

    vec_out[...] = vec[...]
    rows = x_out.shape[0]
    pick = picker(keep[0], rows - buf)
    for src, dst in ((tokens, x_out), (cot, em_out)):
        dst[0:buf, :] = src[0, 0:buf, :]
        dst[buf:rows, :] = mm(pick, src[0, buf:, :]).astype(bf16)
    normal, _ = layer_stats(x_out[...].astype(f32))
    h_out[...] = (normal * vec[0:1, :] + vec[1:2, :]).astype(bf16)


def pieces_of(info, e):
    core = info[1] ^ e
    first = core + 1
    second = 3 - first
    group = info[0]
    return core, (group, group ^ first, group ^ second, group ^ 3)


def head_masks():
    lane = lax.broadcasted_iota(jnp.int32, (1, 2 * HEAD), 1)
    low = jnp.where(lane < HEAD, 1.0, 0.0)
    return low.astype(bf16), (1.0 - low).astype(bf16), low > 0.5


def two_heads(x, low, high):
    return jnp.concatenate([x * low, x * high], axis=0)


def pick_heads(both, first):
    rows = both.shape[0] // 2
    return jnp.where(first, both[:rows], both[rows:])


def pair_probs(q_pair, k_pair, count):
    raw = mm_nt(q_pair, k_pair) * (1.0 / math.sqrt(HEAD))
    col = lax.broadcasted_iota(jnp.int32, raw.shape, 1)
    raw = jnp.where(col < count, raw, -1e30)
    top = jnp.max(raw, axis=-1, keepdims=True)
    exponent = jnp.exp(raw - top)
    return exponent / jnp.sum(exponent, axis=-1, keepdims=True)


def fetch_attn(info, pieces, wbuf, sems, start, width):
    copies = []
    for e in range(2):
        _, owners = pieces_of(info, e)
        for k in range(4):
            src = pieces[4 * e + k]
            rows = src.shape[0]
            copies.append(
                pltpu.make_async_copy(
                    src.at[:, pl.ds(start, width)],
                    wbuf.at[e, pl.ds(pl.multiple_of(owners[k] * rows, rows), rows), :],
                    sems.at[e, k],
                )
            )
    for one in copies:
        one.start()
    return copies


def attend_kernel(seqs, *refs):
    info, h1, x, vec = refs[:4]
    pieces = refs[4:12]
    qkv, o, r, h2, stats, wbuf, sems = refs[12:]
    rows = h1.shape[0] // seqs
    d = h1.shape[1]
    half = d // 2
    copies = fetch_attn(info, pieces, wbuf, sems, 0, 4 * half)
    for e in range(2):
        core, _ = pieces_of(info, e)
        for one in copies[4 * e : 4 * e + 4]:
            one.wait()

        @pl.loop(0, 2)
        def _(t):
            near = pl.multiple_of(core * half + t * (half // 2), half // 2)
            for j in range(3):
                w = wbuf[e, :, pl.ds(pl.multiple_of(j * half + t * (half // 2), half // 2), half // 2)]
                got = mm(h1[...], w)
                if j != 1:
                    got = got + vec[2 + j // 2 : 3 + j // 2, pl.ds(near, half // 2)]
                qkv[:, pl.ds(pl.multiple_of(j * d + near, half // 2), half // 2)] = got.astype(bf16)

    low, high, first = head_masks()
    pairs = d // (2 * HEAD)

    @pl.loop(0, seqs * pairs)
    def _(i):
        n, j = i // pairs, i % pairs
        at = pl.ds(pl.multiple_of(n * rows, 16), rows)
        lanes = [pl.ds(pl.multiple_of(j * 2 * HEAD + m * d, 2 * HEAD), 2 * HEAD) for m in range(3)]
        q_pair = two_heads(qkv[at, lanes[0]], low, high)
        probs = pair_probs(q_pair, qkv[at, lanes[1]], info[4 + n]).astype(bf16)
        o[at, lanes[0]] = pick_heads(mm(probs, qkv[at, lanes[2]]), first).astype(bf16)

    for e in range(2):
        core, _ = pieces_of(info, e)

        @pl.loop(0, 2)
        def _(t):
            near = pl.ds(pl.multiple_of(core * half + t * (half // 2), half // 2), half // 2)
            w = wbuf[e, :, pl.ds(pl.multiple_of(3 * half + t * (half // 2), half // 2), half // 2)]
            r[:, near] = mm(o[...], w) + vec[4:5, near]

    stats[...] = jnp.zeros_like(stats)

    @pl.loop(0, seqs)
    def _(n):
        at = pl.ds(pl.multiple_of(n * rows, 16), rows)
        valid = lax.broadcasted_iota(jnp.int32, (rows, 1), 0) < info[4 + n]
        valid = jnp.where(valid, 1.0, 0.0)
        inputs = x[at, :].astype(f32)
        branch = r[at, :]
        resid = inputs + branch
        r[at, :] = resid
        normal, _ = layer_stats(resid)
        h2[at, :] = (normal * vec[5:6, :] + vec[6:7, :]).astype(bf16)
        stats[0:1, :] += jnp.sum(inputs * inputs * valid, axis=0, keepdims=True)
        stats[1:2, :] += jnp.sum(branch * branch * valid, axis=0, keepdims=True)


def feed_kernel(seqs, buf, *refs):
    info, keep, h2, em, r, vec = refs[:6]
    ups, downs = refs[6:14], refs[14:22]
    z_mine, z_yours, u_mine, u_yours, er, ea, out, sums = refs[22:30]
    wup, wdown, m_acc, t_acc, sem_up, sem_down = refs[30:]
    rows = h2.shape[0] // seqs
    d = h2.shape[1]
    strip = wup.shape[2] // 4
    tile = strip // 2
    copies = [[], []]
    for e in range(2):
        _, owners = pieces_of(info, e)
        for k in range(4):
            src = ups[4 * e + k]
            deep = src.shape[0]
            copies[e].append(
                pltpu.make_async_copy(
                    src,
                    wup.at[e, pl.ds(pl.multiple_of(owners[k] * deep, deep), deep), :],
                    sem_up.at[e, k],
                )
            )
            copies[e].append(
                pltpu.make_async_copy(downs[4 * e + k], wdown.at[e, owners[k]], sem_down.at[e, k])
            )
        for one in copies[e]:
            one.start()
    sums[...] = jnp.zeros_like(sums)
    m_acc[...] = jnp.zeros_like(m_acc)
    t_acc[...] = jnp.zeros_like(t_acc)
    for e, z_out, u_out in ((0, z_mine, u_mine), (1, z_yours, u_yours)):
        core, _ = pieces_of(info, e)
        for one in copies[e]:
            one.wait()

        @pl.loop(0, 8)
        def _(i):
            s, t = i // 2, i % 2
            near = pl.ds(pl.multiple_of(i * tile, tile), tile)
            far = (pl.ds(8 + s, 1), pl.ds(pl.multiple_of(core * strip + t * tile, tile), tile))
            w_up = wup[e, :, near]
            w_down = wdown[e, s, pl.ds(pl.multiple_of(t * tile, tile), tile), :]
            u = mm(h2[...], w_up) + vec[far]
            phi = 0.5 * (1.0 + lax.erf(u * root_half))
            z = (u * phi).astype(bf16)
            z_out[:, near] = z
            slope = phi + u * jnp.exp(-0.5 * u * u) * inverse_root_two_pi
            eu = (mm_nt(em[...], w_down) * slope).astype(bf16)
            u_out[:, near] = eu
            m_acc[...] += mm(z, w_down)
            t_acc[...] += mm_nt(eu, w_up)
            sums[far] = jnp.sum(eu.astype(f32), axis=0, keepdims=True)

    @pl.loop(0, seqs)
    def _(n):
        at = pl.ds(pl.multiple_of(n * rows, 16), rows)
        valid = lax.broadcasted_iota(jnp.int32, (rows, 1), 0) < info[4 + n]
        valid = jnp.where(valid, 1.0, 0.0)
        resid = r[at, :]
        m = m_acc[at, :] + vec[7:8, :]
        packed = ((resid + m) * valid).astype(bf16)
        out[n, 0:buf, :] = packed[0:buf]
        pick = picker(keep[n], rows - buf)
        out[n, buf:, :] = mm_tn(pick, packed[buf:]).astype(bf16)
        normal, inverse = layer_stats(resid)
        t = t_acc[at, :]
        low = em[at, :].astype(f32)
        back = low + norm_back(t, normal, inverse, vec[5:6, :])
        er[at, :] = back
        ea_low = back.astype(bf16)
        ea[at, :] = ea_low
        sums[4:5, :] += jnp.sum(ea_low.astype(f32), axis=0, keepdims=True)
        sums[5:6, :] += jnp.sum(t * normal, axis=0, keepdims=True)
        sums[6:7, :] += jnp.sum(t, axis=0, keepdims=True)
        sums[7:8, :] += jnp.sum(low, axis=0, keepdims=True)
        sums[12:13, :] += jnp.sum(m * m * valid, axis=0, keepdims=True)


def back_kernel(seqs, *refs):
    info, ea, qkv = refs[:3]
    pieces = refs[3:11]
    mine, yours, sums, wbuf, eo, sems = refs[11:]
    rows = ea.shape[0] // seqs
    d = ea.shape[1]
    half = d // 2
    copies = fetch_attn(info, pieces, wbuf, sems, 3 * half, half)
    for one in copies:
        one.wait()

    @pl.loop(0, 4)
    def _(s):
        near = pl.ds(pl.multiple_of(s * (d // 4), d // 4), d // 4)
        total = None
        for e in range(2):
            core, _ = pieces_of(info, e)
            part = ea[:, pl.ds(pl.multiple_of(core * half, half), half)]
            got = mm_nt(part, wbuf[e, near, :])
            total = got if total is None else total + got
        eo[:, near] = total.astype(bf16)

    low, high, first = head_masks()
    pairs = half // (2 * HEAD)
    scale = 1.0 / math.sqrt(HEAD)
    sums[...] = jnp.zeros_like(sums)
    for e, dst in ((0, mine), (1, yours)):
        core, _ = pieces_of(info, e)

        @pl.loop(0, seqs * pairs)
        def _(i):
            n, j = i // pairs, i % pairs
            at = pl.ds(pl.multiple_of(n * rows, 16), rows)
            far = core * half + j * 2 * HEAD
            lanes = [pl.ds(pl.multiple_of(far + m * d, 2 * HEAD), 2 * HEAD) for m in range(3)]
            k_pair = qkv[at, lanes[1]]
            q_both = two_heads(qkv[at, lanes[0]], low, high)
            probs = pair_probs(q_both, k_pair, info[4 + n])
            eo_both = two_heads(eo[at, lanes[0]], low, high)
            ep = mm_nt(eo_both, qkv[at, lanes[2]])
            inner = jnp.sum(probs * ep, axis=-1, keepdims=True)
            es = (probs * (ep - inner)).astype(bf16)
            ev = mm_tn(probs.astype(bf16), eo_both).astype(bf16)
            eq = (pick_heads(mm(es, k_pair), first) * scale).astype(bf16)
            ek = (mm_tn(es, q_both) * scale).astype(bf16)
            for m, value in enumerate((eq, ek, ev)):
                dst[at, pl.ds(pl.multiple_of(m * half + j * 2 * HEAD, 2 * HEAD), 2 * HEAD)] = value
            sums[2:3, lanes[0]] += jnp.sum(eq.astype(f32), axis=0, keepdims=True)
            sums[3:4, lanes[0]] += jnp.sum(ev.astype(f32), axis=0, keepdims=True)


def input_kernel(seqs, buf, *refs):
    info, keep, mine, yours, x, er, vec = refs[:7]
    pieces = refs[7:15]
    out, sums, wbuf, t_acc, sems = refs[15:]
    rows = x.shape[0] // seqs
    d = x.shape[1]
    half = d // 2
    copies = fetch_attn(info, pieces, wbuf, sems, 0, 3 * half)
    for one in copies:
        one.wait()

    @pl.loop(0, 4)
    def _(s):
        near = pl.ds(pl.multiple_of(s * (d // 4), d // 4), d // 4)
        t_acc[:, near] = mm_nt(mine[...], wbuf[0, near, :]) + mm_nt(yours[...], wbuf[1, near, :])

    sums[...] = jnp.zeros_like(sums)

    @pl.loop(0, seqs)
    def _(n):
        at = pl.ds(pl.multiple_of(n * rows, 16), rows)
        normal, inverse = layer_stats(x[at, :].astype(f32))
        t = t_acc[at, :]
        grad = er[at, :] + norm_back(t, normal, inverse, vec[0:1, :])
        sums[0:1, :] += jnp.sum(t * normal, axis=0, keepdims=True)
        sums[1:2, :] += jnp.sum(t, axis=0, keepdims=True)
        out[n, 0:buf, :] = grad[0:buf]
        pick = picker(keep[n], rows - buf)
        rest = grad[buf:]
        high = rest.astype(bf16)
        rest = rest - high.astype(f32)
        middle = rest.astype(bf16)
        low = (rest - middle.astype(f32)).astype(bf16)
        out[n, buf:, :] = mm_tn(pick, high) + mm_tn(pick, middle) + mm_tn(pick, low)


def grad_kernel(order, a_own, a_got, b_own, b_got, out):
    left = jnp.concatenate([a_own[...], a_got[...]], axis=0)
    right = jnp.concatenate([b_own[...], b_got[...]], axis=0)
    out[0] = mm_tn(left, right).astype(bf16)


def weight_grad(order, a_own, a_got, b_own, b_got, deep, wide, tile, b_start=0):
    rows = a_own.shape[0]
    blocks = 2
    return pl.pallas_call(
        grad_kernel,
        grid_spec=pltpu.PrefetchScalarGridSpec(
            num_scalar_prefetch=1,
            grid=(blocks, wide // tile),
            in_specs=[pl.BlockSpec((rows, deep), lambda i, j, order: (0, order[i]))] * 2
            + [pl.BlockSpec((rows, tile), lambda i, j, order: (0, order[2] * b_start + j))] * 2,
            out_specs=pl.BlockSpec((1, deep, tile), lambda i, j, order: (i, 0, j)),
        ),
        out_shape=sds((blocks, deep, wide), bf16),
        compiler_params=params(40),
        cost_estimate=cost(4 * rows * deep * wide * blocks, 4 * rows * (deep * 2 + wide)),
    )(order, a_own, a_got, b_own, b_got)


def adam_math(w, f, s, grad, rate, decay):
    first_new = beta_first * f + (1.0 - beta_first) * grad
    second_new = beta_second * s + (1.0 - beta_second) * grad * grad
    fix_first = 1.0 - beta_first**STEP
    fix_second = 1.0 - beta_second**STEP
    update = first_new / fix_first / (jnp.sqrt(second_new / fix_second) + adam_epsilon)
    return w - rate * (update + decay * w), first_new, second_new


def adam_kernel(info, w, f, s, g0, g1, g2, g3, *rest):
    w_out, f_out, s_out, low_out = rest[-4:]
    quarter = pl.program_id(0)
    for k, part in enumerate((g0, g1, g2, g3)):

        @pl.when(quarter == k)
        def _():
            new, first, second = adam_math(
                w[...], f[...], s[...], part[...].astype(f32), rate_matrix, weight_decay
            )
            w_out[...] = new
            f_out[...] = first
            s_out[...] = second
            low_out[...] = new.astype(bf16)


def adam_call(info, state, quarters, block, grid_width, place, grad_place, aliased=None):
    spec = pl.BlockSpec(block, place)
    shape = state[0].shape
    grads = [
        pl.BlockSpec(block, functools.partial(lambda k, i, j, info: grad_place(jnp.where(i == k, j, 0)), k))
        for k in range(4)
    ]
    extra = [] if aliased is None else list(aliased)
    return pl.pallas_call(
        adam_kernel,
        grid_spec=pltpu.PrefetchScalarGridSpec(
            num_scalar_prefetch=1,
            grid=(4, grid_width),
            in_specs=[spec] * 3 + grads + [ANY_SPEC] * len(extra),
            out_specs=[spec] * 4,
        ),
        out_shape=[sds(shape, f32)] * 3 + [sds(shape, bf16)],
        input_output_aliases={8 + k: k for k in range(len(extra))},
        compiler_params=params(40),
        cost_estimate=cost(20 * 4 * grid_width * block[0] * block[1], 28 * 4 * grid_width * block[0] * block[1]),
    )(info, *state, *quarters, *extra)


def cast_kernel(info, src, out):
    out[...] = src[...].astype(bf16)


def half_strips(info, matrix, start, count):
    deep = matrix.shape[0]
    strip = 512
    return pl.pallas_call(
        cast_kernel,
        grid_spec=pltpu.PrefetchScalarGridSpec(
            num_scalar_prefetch=1,
            grid=(count,),
            in_specs=[pl.BlockSpec((deep, strip), lambda j, info: (0, 2 * (start + j) + info[1]))],
            out_specs=pl.BlockSpec((deep, strip), lambda j, info: (0, j)),
        ),
        out_shape=sds((deep, strip * count), bf16),
        compiler_params=params(16),
        cost_estimate=cost(deep * strip * count, 6 * deep * strip * count),
    )(info, matrix)


def half_rows(info, matrix):
    deep, wide = matrix.shape[0] // 2, matrix.shape[1]
    return pl.pallas_call(
        cast_kernel,
        grid_spec=pltpu.PrefetchScalarGridSpec(
            num_scalar_prefetch=1,
            grid=(2,),
            in_specs=[pl.BlockSpec((deep // 2, wide), lambda j, info: (2 * info[1] + j, 0))],
            out_specs=pl.BlockSpec((deep // 2, wide), lambda j, info: (j, 0)),
        ),
        out_shape=sds((deep, wide), bf16),
        compiler_params=params(16),
        cost_estimate=cost(deep * wide, 6 * deep * wide),
    )(info, matrix)


def add_low(a, b):
    return (a.astype(f32) + b.astype(f32)).astype(bf16)


def local(groups, replicas, *args):
    tokens, keep, cot, mats, down, vectors, f_mats, f_down, f_vectors, s_mats, s_down, s_vectors = args
    seqs, length, d = tokens.shape
    image = keep.shape[1]
    buf = length - image
    rows = -(-(buf + KEEP_MAX) // 16) * 16
    total = seqs * rows
    half = d // 2
    group, replica = lax.axis_index("group"), lax.axis_index("dp")
    core, level = replica % 2, (replica // 2) % 2
    counts = buf + jnp.sum(keep, axis=1)
    info = jnp.concatenate([jnp.stack([group, core, level, 0 * core]), counts]).astype(jnp.int32)

    def permute(value, target):
        pairs = []
        for a in range(groups):
            for b in range(replicas):
                to_a, to_b = target(a, b)
                pairs.append((a * replicas + b, to_a * replicas + to_b))
        return lax.ppermute(value, BOTH, pairs)

    hop_one = lambda v: permute(v, lambda a, b: (a ^ (1 + b % 2), b))
    hop_two = lambda v: permute(v, lambda a, b: (a ^ (2 - b % 2), b))
    swap = lambda v: permute(v, lambda a, b: (a, b ^ 1))
    shift = lambda v, bit: permute(v, lambda a, b: (a, b ^ bit))

    low_vectors = vectors.astype(bf16)
    vec_parts = [low_vectors] + [
        permute(low_vectors, functools.partial(lambda flip, a, b: (a ^ flip, b), flip)) for flip in (1, 2, 3)
    ]

    def gather(own):
        one = hop_one(own)
        two = hop_two(own)
        three = hop_two(one)
        mine = [own, one, two, three]
        return mine + [swap(v) for v in mine]

    own_attn = half_strips(info, mats, 0, 4)
    own_up = half_strips(info, mats, 4, 4)
    own_down = half_rows(info, down)
    w_attn = gather(own_attn)
    own_up, own_down, _ = lax.optimization_barrier((own_up, own_down, w_attn[3]))
    w_up = gather(own_up)
    own_down, _ = lax.optimization_barrier((own_down, w_up[3]))
    w_down = gather(own_down)

    keep3 = keep.reshape(seqs, 1, image)
    x, em, h1, vec = pl.pallas_call(
        functools.partial(pack_kernel, buf),
        grid_spec=pltpu.PrefetchScalarGridSpec(
            num_scalar_prefetch=1,
            grid=(seqs,),
            in_specs=[pl.BlockSpec((1, 1, image), lambda n, info: (n, 0, 0))]
            + [pl.BlockSpec((1, length, d), lambda n, info: (n, 0, 0))] * 2
            + [pl.BlockSpec((12, vectors.shape[1]), lambda n, info: (0, 0))] * 4,
            out_specs=[pl.BlockSpec((rows, d), lambda n, info: (n, 0))] * 3
            + [pl.BlockSpec((16, d), lambda n, info: (0, 0))],
            scratch_shapes=[pltpu.VMEM((16, d), f32)],
        ),
        out_shape=[sds((total, d), bf16)] * 3 + [sds((16, d), f32)],
        compiler_params=params(40),
        cost_estimate=cost(8 * total * image * d, 10 * total * d),
    )(info, keep3, tokens, cot, *vec_parts)
    h1_got, em_got = swap(h1), swap(em)

    qkv, o, r, h2, stats = pl.pallas_call(
        functools.partial(attend_kernel, seqs),
        in_specs=[SMEM_SPEC] + [VMEM_SPEC] * 3 + [ANY_SPEC] * 8,
        out_specs=[VMEM_SPEC] * 5,
        out_shape=[
            sds((total, 3 * d), bf16),
            sds((total, d), bf16),
            sds((total, d), f32),
            sds((total, d), bf16),
            sds((8, d), f32),
        ],
        scratch_shapes=[pltpu.VMEM((2, d, 2 * d), bf16), pltpu.SemaphoreType.DMA((2, 4))],
        compiler_params=params(56),
        cost_estimate=cost(2 * total * 4 * d * d * 1.5, 20 * total * d),
    )(info, h1, x, vec, *w_attn)
    o_got, h2_got = swap(o), swap(h2)

    z_mine, z_yours, u_mine, u_yours, er, ea, block_output, sums_feed = pl.pallas_call(
        functools.partial(feed_kernel, seqs, buf),
        in_specs=[SMEM_SPEC] + [VMEM_SPEC] * 5 + [ANY_SPEC] * 16,
        out_specs=[VMEM_SPEC] * 8,
        out_shape=[sds((total, 2 * d), bf16)] * 4
        + [
            sds((total, d), f32),
            sds((total, d), bf16),
            sds((seqs, length, d), bf16),
            sds((16, d), f32),
        ],
        scratch_shapes=[
            pltpu.VMEM((2, d, 2 * d), bf16),
            pltpu.VMEM((2, 4, half, d), bf16),
            pltpu.VMEM((total, d), f32),
            pltpu.VMEM((total, d), f32),
            pltpu.SemaphoreType.DMA((2, 4)),
            pltpu.SemaphoreType.DMA((2, 4)),
        ],
        compiler_params=params(60),
        cost_estimate=cost(2 * total * 16 * d * d, 60 * total * d),
    )(info, keep3, h2, em, r, vec, *w_up, *w_down)

    z_got, u_got, ea_got = swap(z_yours), swap(u_yours), swap(ea)

    first, second = core + 1, 2 - core
    send_order = jnp.stack([group ^ first, group ^ 3, core]).astype(jnp.int32)
    keep_order = jnp.stack([group, group ^ second, core]).astype(jnp.int32)

    def reduce_blocks(make):
        sent = make(send_order)
        got = hop_one(sent)
        kept = make(keep_order)
        kept = add_low(kept, got)
        mine = add_low(kept[0], hop_two(kept[1]))
        deep = mine.shape[0] // 2
        give = lax.dynamic_slice(mine, ((1 - level) * deep, 0), (deep, mine.shape[1]))
        hold = lax.dynamic_slice(mine, (level * deep, 0), (deep, mine.shape[1]))
        hold = add_low(hold, shift(give, 2))
        bit = 4
        while bit < replicas:
            hold = add_low(hold, shift(hold, bit))
            bit *= 2
        other = shift(hold, 2)
        return hold, other, swap(hold), swap(other)

    g_down = reduce_blocks(
        lambda order: weight_grad(order, z_mine, z_got, em, em_got, half, d, half)
    )

    def up_and_out(order):
        return weight_grad(order, h2, h2_got, u_mine, u_got, d // 4, 2 * d, half)

    g_up = reduce_blocks(up_and_out)
    g_out = reduce_blocks(lambda order: weight_grad(order, o, o_got, ea, ea_got, d // 4, half, half, 1))

    e_mine, e_yours, sums_back = pl.pallas_call(
        functools.partial(back_kernel, seqs),
        in_specs=[SMEM_SPEC] + [VMEM_SPEC] * 2 + [ANY_SPEC] * 8,
        out_specs=[VMEM_SPEC] * 3,
        out_shape=[sds((total, 3 * half), bf16)] * 2 + [sds((8, d), f32)],
        scratch_shapes=[
            pltpu.VMEM((2, d, half), bf16),
            pltpu.VMEM((total, d), bf16),
            pltpu.SemaphoreType.DMA((2, 4)),
        ],
        compiler_params=params(48),
        cost_estimate=cost(2 * total * 4 * d * d, 20 * total * d),
    )(info, ea, qkv, *w_attn)
    e_got = swap(e_yours)
    g_qkv = reduce_blocks(
        lambda order: weight_grad(order, h1, h1_got, e_mine, e_got, d // 4, 3 * half, half)
    )

    input_grad, sums_in = pl.pallas_call(
        functools.partial(input_kernel, seqs, buf),
        in_specs=[SMEM_SPEC] + [VMEM_SPEC] * 6 + [ANY_SPEC] * 8,
        out_specs=[VMEM_SPEC] * 2,
        out_shape=[sds((seqs, length, d), f32), sds((8, d), f32)],
        scratch_shapes=[
            pltpu.VMEM((2, d, 3 * half), bf16),
            pltpu.VMEM((total, d), f32),
            pltpu.SemaphoreType.DMA((2, 4)),
        ],
        compiler_params=params(56),
        cost_estimate=cost(2 * total * 3 * d * d, 20 * total * d),
    )(info, keep3, e_mine, e_yours, x, er, vec, *w_attn)

    squares = jnp.stack([jnp.sum(stats[0]), jnp.sum(stats[1]), jnp.sum(sums_feed[12]), jnp.sum(counts).astype(f32)])
    small = jnp.concatenate(
        [
            sums_in[0:2],
            sums_back[2:4],
            sums_feed[4:12],
            jnp.pad(squares.reshape(1, 4), ((0, 3), (0, d - 4))),
        ]
    )
    bit = 1
    while bit < groups:
        small = small + permute(small, functools.partial(lambda flip, a, b: (a ^ flip, b), bit))
        bit *= 2
    bit = 1
    while bit < replicas:
        small = small + shift(small, bit)
        bit *= 2
    branch_rms = jnp.sqrt(small[12, 0:3] / (small[12, 3] * d))
    part = vectors.shape[1]
    grad_vectors = lax.dynamic_slice(small, (0, group * part), (12, part))

    def core_of(k, info):
        return info[1] ^ (k // 2)

    def level_of(k, info):
        return info[2] ^ (k % 2)

    new_down = adam_call(
        info,
        (down, f_down, s_down),
        g_down,
        (down.shape[0] // 4, half),
        2,
        lambda i, j, info: (2 * core_of(i, info) + level_of(i, info), j),
        lambda j: (0, j),
    )

    def adam_mats(quarters, first_strip, strips, previous):
        return adam_call(
            info,
            (mats, f_mats, s_mats),
            quarters,
            (mats.shape[0] // 2, half),
            strips,
            lambda i, j, info: (level_of(i, info), 2 * (first_strip + j) + core_of(i, info)),
            lambda j: (0, j),
            previous,
        )

    new_mats = adam_mats(g_up, 4, 4, None)
    new_mats = adam_mats(g_out, 3, 1, new_mats)
    new_mats = adam_mats(g_qkv, 0, 3, new_mats)
    new_vectors, first_vectors, second_vectors = adam_math(
        vectors, f_vectors, s_vectors, grad_vectors, rate_vector, 0.0
    )
    return (
        block_output,
        input_grad,
        new_mats[0],
        new_down[0],
        new_vectors,
        new_mats[1],
        new_down[1],
        first_vectors,
        new_mats[2],
        new_down[2],
        second_vectors,
        new_mats[3],
        new_down[3],
        new_vectors.astype(bf16),
        branch_rms,
    )


def solution(mesh):
    rows, owned, columns = P(BOTH, None, None), P("group", None), P(None, "group")
    state = (owned, owned, columns)
    return jax.shard_map(
        functools.partial(local, mesh.shape["group"], mesh.shape["dp"]),
        mesh=mesh,
        in_specs=(rows, P(BOTH, None), rows) + state * 3,
        out_specs=(rows, rows) + state * 4 + (P(),),
        check_vma=False,
    )
```

```python
import functools
import math

import jax
import jax.numpy as jnp
from jax import lax
from jax.experimental import pallas as pl
from jax.experimental.pallas import tpu as pltpu
from jax.sharding import PartitionSpec as P

HEAD = 64
STEP = 7
KEEP_MAX = 77

norm_epsilon = 1e-06
beta_first = 0.5
beta_second = 0.5
adam_epsilon = 1e-08
rate_matrix = 0.05
rate_vector = 0.3
weight_decay = 0.05
root_half = 0.7071067811865476
inverse_root_two_pi = 0.3989422804014327

bf16 = jnp.bfloat16
f32 = jnp.float32
BOTH = ("group", "dp")
VMEM_SPEC = pl.BlockSpec(memory_space=pltpu.VMEM)
SMEM_SPEC = pl.BlockSpec(memory_space=pltpu.SMEM)
ANY_SPEC = pl.BlockSpec(memory_space=pl.ANY)
MIB = 1 << 20


def mm(a, b):
    return jnp.dot(a, b, preferred_element_type=f32)


def mm_nt(a, b):
    return lax.dot_general(a, b, (((1,), (1,)), ((), ())), preferred_element_type=f32)


def mm_tn(a, b):
    return lax.dot_general(a, b, (((0,), (0,)), ((), ())), preferred_element_type=f32)


def sds(shape, dtype):
    return jax.ShapeDtypeStruct(shape, dtype)


def params(mib, **more):
    return pltpu.CompilerParams(vmem_limit_bytes=mib * MIB, **more)


def cost(flops, nbytes):
    return pl.CostEstimate(flops=int(flops), bytes_accessed=int(nbytes), transcendentals=0)


def layer_stats(values):
    centre = jnp.mean(values, axis=-1, keepdims=True)
    centred = values - centre
    variance = jnp.mean(centred * centred, axis=-1, keepdims=True)
    inverse = lax.rsqrt(variance + norm_epsilon)
    return centred * inverse, inverse


def norm_back(grad_normed, normal, inverse, gain):
    scaled = grad_normed * gain
    mean_one = jnp.mean(scaled, axis=-1, keepdims=True)
    mean_two = jnp.mean(scaled * normal, axis=-1, keepdims=True)
    return inverse * (scaled - mean_one - normal * mean_two)


def picker(keep_row, rows):
    image = keep_row.shape[1]
    ahead = lax.broadcasted_iota(jnp.int32, (image, image), 0)
    here = lax.broadcasted_iota(jnp.int32, (image, image), 1)
    upper = jnp.where(ahead <= here, 1.0, 0.0).astype(bf16)
    kept = keep_row.astype(f32)
    place = mm(kept.astype(bf16), upper) - 1.0
    place = jnp.where(kept > 0.5, place, -1.0)
    want = lax.broadcasted_iota(jnp.int32, (rows, image), 0).astype(f32)
    return jnp.where(place == want, 1.0, 0.0).astype(bf16)


MESH = pl.DeviceIdType.MESH


def flip(value, bit):
    return value + bit - 2 * bit * ((value // bit) % 2)


class Place:
    def __init__(self):
        self.group, self.replica = lax.axis_index("group"), lax.axis_index("dp")
        self.core, self.level = self.replica % 2, (self.replica // 2) % 2
        one, two = flip(self.group, 1), flip(self.group, 2)
        self.first = (1 - self.core) * one + self.core * two
        self.second = (1 - self.core) * two + self.core * one
        self.third = flip(one, 2)
        self.to_first = (self.first, self.replica)
        self.to_second = (self.second, self.replica)
        self.to_third = (self.third, self.replica)
        self.to_core = (self.group, flip(self.replica, 1))

    def to_bit(self, bit):
        return (self.group, flip(self.replica, bit))

    def meet(self, partners):
        barrier = pltpu.get_barrier_semaphore()
        for partner in partners:
            pl.semaphore_signal(barrier, inc=1, device_id=partner, device_id_type=MESH)
        pl.semaphore_wait(barrier, len(partners))


class Gather:
    def __init__(self, place, own, full, send, recv):
        self.place, self.own, self.full, self.send, self.recv = place, own, full, send, recv
        deep = own.shape[0]
        self.deep, self.strip = deep, 5 * deep // 16
        self.main = deep - self.strip
        self.main_at = place.level * self.strip
        self.strip_at = place.level * self.main

    def block(self, owner, start, size):
        at = pl.multiple_of(owner * self.deep + start, 16)
        return self.full.at[self.place.core, pl.ds(at, size), :]

    def make(self, k, owner, start, size, device):
        view = self.block(owner, start, size)
        return pltpu.make_async_remote_copy(
            src_ref=view, dst_ref=view, send_sem=self.send.at[k], recv_sem=self.recv.at[k],
            device_id=device, device_id_type=MESH,
        )

    def plan(self, k):
        p = self.place
        main, strip, whole = (self.main_at, self.main), (self.strip_at, self.strip), (0, self.deep)
        return (
            (p.group, *main, p.to_first),
            (p.group, *main, p.to_second),
            (p.first, *main, p.to_second),
            (p.first, *strip, p.to_bit(2)),
            (p.second, *strip, p.to_bit(2)),
            (p.third, *strip, p.to_bit(2)),
            (p.group, *whole, p.to_core),
            (p.first, *whole, p.to_core),
            (p.second, *whole, p.to_core),
            (p.third, *whole, p.to_core),
        )[k]

    def start(self, *ks):
        for k in ks:
            owner, at, size, device = self.plan(k)
            if k in (0, 1, 6):
                start = pl.multiple_of(at, 16) if k < 6 else 0
                pltpu.make_async_remote_copy(
                    src_ref=self.own.at[pl.ds(start, size), :], dst_ref=self.block(owner, at, size),
                    send_sem=self.send.at[k], recv_sem=self.recv.at[k], device_id=device, device_id_type=MESH,
                ).start()
            else:
                self.make(k, owner, at, size, device).start()

    def arrived(self, *ks):
        for k in ks:
            self.make(k, *self.plan(k)).wait_recv()

    def sent(self, *ks):
        for k in ks:
            self.make(k, *self.plan(k)).wait_send()

    def step_one(self):
        self.start(0, 1, 6)

    def step_two(self):
        self.arrived(0)
        self.start(2, 3)
        self.arrived(1)
        self.start(4)

    def step_three(self):
        self.arrived(2)
        self.start(5)
        self.arrived(3)
        self.start(7)
        self.arrived(4)
        self.start(8)

    def step_four(self):
        self.arrived(5)
        self.start(9)

    def step_five(self):
        self.arrived(6, 7, 8, 9)
        self.sent(*range(10))


def head_masks():
    lane = lax.broadcasted_iota(jnp.int32, (1, 2 * HEAD), 1)
    low = jnp.where(lane < HEAD, 1.0, 0.0)
    return low.astype(bf16), (1.0 - low).astype(bf16), low > 0.5


def two_heads(x, low, high):
    return jnp.concatenate([x * low, x * high], axis=0)


def pick_heads(both, first):
    rows = both.shape[0] // 2
    return jnp.where(first, both[:rows], both[rows:])


def pair_probs(q_pair, k_pair, count):
    raw = mm_nt(q_pair, k_pair) * (1.0 / math.sqrt(HEAD))
    col = lax.broadcasted_iota(jnp.int32, raw.shape, 1)
    raw = jnp.where(col < count, raw, -1e30)
    top = jnp.max(raw, axis=-1, keepdims=True)
    exponent = jnp.exp(raw - top)
    return exponent / jnp.sum(exponent, axis=-1, keepdims=True)


def fetch(src, buf, sem, start, width):
    copy = pltpu.make_async_copy(src.at[:, :, pl.ds(start, width)], buf, sem)
    copy.start()
    return copy


def attend_kernel(seqs, buf, *refs):
    counts, keep, vectors, mats, down, tokens, cot = refs[:7]
    w_attn, w_up, w_down, x, em, h1, vec, qkv, o, r, h2, stats = refs[7:19]
    wbuf, wide, tall, low_up, low_down, rows_in, parts, send, recv, vec_send, vec_recv, loads, stores, reads = refs[19:]
    rows = h1.shape[0] // seqs
    d = h1.shape[1]
    half = d // 2
    place = Place()
    core = place.core
    deep = mats.shape[0]

    takes = []
    for j in range(8):
        at = pl.ds(pl.multiple_of((2 * j + core) * half, half), half)
        takes.append(
            pltpu.make_async_copy(mats.at[:, at], wide.at[j // 4, :, pl.ds((j % 4) * half, half)], loads.at[j])
        )
    takes.append(
        pltpu.make_async_copy(down.at[pl.ds(pl.multiple_of(core * half, half), half), :], tall, loads.at[8])
    )
    for one in takes:
        one.start()
    reads_in = []
    for n in range(seqs):
        for k, src in enumerate((tokens, cot)):
            reads_in.append(pltpu.make_async_copy(src.at[n], rows_in.at[k, n], reads.at[k, n]))
    for one in reads_in:
        one.start()

    place.meet((place.to_first, place.to_second, place.to_third, place.to_core, place.to_bit(2)))

    part = vectors.shape[1]
    parts[place.group] = jnp.concatenate([vectors[...], jnp.zeros((4, part), f32)], axis=0).astype(bf16)
    for k, partner in enumerate((place.to_first, place.to_second, place.to_third)):
        pltpu.make_async_remote_copy(
            src_ref=parts.at[place.group], dst_ref=parts.at[place.group],
            send_sem=vec_send.at[k], recv_sem=vec_recv.at[k], device_id=partner, device_id_type=MESH,
        ).start()

    for one in takes[:4]:
        one.wait()
    own = wbuf.at[core, pl.ds(pl.multiple_of(place.group * deep, deep), deep), :]
    own[...] = wide[0].astype(bf16)
    attn = Gather(place, own, wbuf, send.at[0], recv.at[0])
    attn.step_one()
    for one in takes[4:]:
        one.wait()
    low_up[...] = wide[1].astype(bf16)
    low_down[...] = tall[...].astype(bf16)
    up = Gather(place, low_up, w_up, send.at[1], recv.at[1])
    downs = Gather(place, low_down, w_down, send.at[2], recv.at[2])
    keep_up = pltpu.make_async_copy(low_up, up.block(place.group, 0, deep), stores.at[0])
    keep_down = pltpu.make_async_copy(low_down, downs.block(place.group, 0, half), stores.at[1])
    keep_up.start()
    keep_down.start()

    for one in reads_in:
        one.wait()

    @pl.loop(0, seqs)
    def _(n):
        at = pl.multiple_of(n * rows, 16)
        pick = picker(keep[n], rows - buf)
        for k, dst in ((0, x), (1, em)):
            dst[pl.ds(at, buf), :] = rows_in[k, n, 0:buf, :]
            dst[pl.ds(pl.multiple_of(at + buf, 16), rows - buf), :] = mm(pick, rows_in[k, n, buf:, :]).astype(bf16)

    attn.step_two()
    for k, partner in enumerate((place.first, place.second, place.third)):
        got = pltpu.make_async_remote_copy(
            src_ref=parts.at[place.group], dst_ref=parts.at[place.group],
            send_sem=vec_send.at[k], recv_sem=vec_recv.at[k], device_id=place.to_first, device_id_type=MESH,
        )
        got.wait()
    vec[...] = jnp.zeros_like(vec)
    for s in range(4):
        vec[:, s * part : (s + 1) * part] = parts[s].astype(f32)

    @pl.loop(0, seqs)
    def _(n):
        at = pl.ds(pl.multiple_of(n * rows, 16), rows)
        normal, _ = layer_stats(x[at, :].astype(f32))
        h1[at, :] = (normal * vec[0:1, :] + vec[1:2, :]).astype(bf16)

    up.step_one()
    attn.step_three()
    attn.step_four()
    attn.step_five()
    keep_attn = pltpu.make_async_copy(wbuf, w_attn, stores.at[2])
    keep_attn.start()

    @pl.loop(0, 4)
    def _(i):
        h, t = i // 2, i % 2
        tile = half // 2
        near = pl.multiple_of(i * tile, tile)
        for j in range(3):
            w = wbuf[h, :, pl.ds(pl.multiple_of(j * half + t * tile, tile), tile)]
            got = mm(h1[...], w)
            if j != 1:
                got = got + vec[2 + j // 2 : 3 + j // 2, pl.ds(near, tile)]
            qkv[:, pl.ds(pl.multiple_of(j * d + near, tile), tile)] = got.astype(bf16)

    up.step_two()
    downs.step_one()
    low, high, first = head_masks()
    pairs = d // (2 * HEAD)
    steps = {
        4: up.step_three,
        8: up.step_four,
        12: downs.step_two,
        20: downs.step_three,
        26: downs.step_four,
    }

    @pl.loop(0, seqs * pairs)
    def _(i):
        for when, step in steps.items():
            pl.when(i == when)(step)
        n, j = i // pairs, i % pairs
        at = pl.ds(pl.multiple_of(n * rows, 16), rows)
        lanes = [pl.ds(pl.multiple_of(j * 2 * HEAD + m * d, 2 * HEAD), 2 * HEAD) for m in range(3)]
        q_pair = two_heads(qkv[at, lanes[0]], low, high)
        probs = pair_probs(q_pair, qkv[at, lanes[1]], counts[n]).astype(bf16)
        o[at, lanes[0]] = pick_heads(mm(probs, qkv[at, lanes[2]]), first).astype(bf16)

    @pl.loop(0, 4)
    def _(i):
        h, t = i // 2, i % 2
        tile = half // 2
        near = pl.ds(pl.multiple_of(i * tile, tile), tile)
        w = wbuf[h, :, pl.ds(pl.multiple_of(3 * half + t * tile, tile), tile)]
        r[:, near] = mm(o[...], w) + vec[4:5, near]

    stats[...] = jnp.zeros_like(stats)

    @pl.loop(0, seqs)
    def _(n):
        at = pl.ds(pl.multiple_of(n * rows, 16), rows)
        valid = lax.broadcasted_iota(jnp.int32, (rows, 1), 0) < counts[n]
        valid = jnp.where(valid, 1.0, 0.0)
        inputs = x[at, :].astype(f32)
        branch = r[at, :]
        resid = inputs + branch
        r[at, :] = resid
        normal, _ = layer_stats(resid)
        h2[at, :] = (normal * vec[5:6, :] + vec[6:7, :]).astype(bf16)
        stats[0:1, :] += jnp.sum(inputs * inputs * valid, axis=0, keepdims=True)
        stats[1:2, :] += jnp.sum(branch * branch * valid, axis=0, keepdims=True)

    up.step_five()
    downs.step_five()
    keep_up.wait()
    keep_down.wait()
    keep_attn.wait()


def feed_kernel(seqs, buf, *refs):
    info, keep, h2, em, r, vec, ups, downs = refs[:8]
    z_mine, z_yours, u_mine, u_yours, er, ea, out, sums = refs[8:16]
    wup, wdown, m_acc, t_acc, sems = refs[16:]
    rows = h2.shape[0] // seqs
    d = h2.shape[1]
    strip = wup.shape[2] // 4
    tile = strip // 2
    copies = []
    for e in range(2):
        core = info[1] ^ e
        copies.append(pltpu.make_async_copy(ups.at[core], wup.at[e], sems.at[e, 0]))
        copies.append(pltpu.make_async_copy(downs.at[core], wdown.at[e], sems.at[e, 1]))
    for one in copies:
        one.start()
    sums[...] = jnp.zeros_like(sums)
    m_acc[...] = jnp.zeros_like(m_acc)
    t_acc[...] = jnp.zeros_like(t_acc)
    for e, z_out, u_out in ((0, z_mine, u_mine), (1, z_yours, u_yours)):
        core = info[1] ^ e
        for one in copies[2 * e : 2 * e + 2]:
            one.wait()

        @pl.loop(0, 8)
        def _(i):
            s, t = i // 2, i % 2
            near = pl.ds(pl.multiple_of(i * tile, tile), tile)
            far = (pl.ds(8 + s, 1), pl.ds(pl.multiple_of(core * strip + t * tile, tile), tile))
            w_up = wup[e, :, near]
            w_down = wdown[e, near, :]
            u = mm(h2[...], w_up) + vec[far]
            phi = 0.5 * (1.0 + lax.erf(u * root_half))
            z = (u * phi).astype(bf16)
            z_out[:, near] = z
            slope = phi + u * jnp.exp(-0.5 * u * u) * inverse_root_two_pi
            eu = (mm_nt(em[...], w_down) * slope).astype(bf16)
            u_out[:, near] = eu
            m_acc[...] += mm(z, w_down)
            t_acc[...] += mm_nt(eu, w_up)
            sums[far] = jnp.sum(eu.astype(f32), axis=0, keepdims=True)

    @pl.loop(0, seqs)
    def _(n):
        at = pl.ds(pl.multiple_of(n * rows, 16), rows)
        valid = lax.broadcasted_iota(jnp.int32, (rows, 1), 0) < info[4 + n]
        valid = jnp.where(valid, 1.0, 0.0)
        resid = r[at, :]
        m = m_acc[at, :] + vec[7:8, :]
        packed = ((resid + m) * valid).astype(bf16)
        out[n, 0:buf, :] = packed[0:buf]
        pick = picker(keep[n], rows - buf)
        out[n, buf:, :] = mm_tn(pick, packed[buf:]).astype(bf16)
        normal, inverse = layer_stats(resid)
        t = t_acc[at, :]
        low = em[at, :].astype(f32)
        back = low + norm_back(t, normal, inverse, vec[5:6, :])
        er[at, :] = back
        ea_low = back.astype(bf16)
        ea[at, :] = ea_low
        sums[4:5, :] += jnp.sum(ea_low.astype(f32), axis=0, keepdims=True)
        sums[5:6, :] += jnp.sum(t * normal, axis=0, keepdims=True)
        sums[6:7, :] += jnp.sum(t, axis=0, keepdims=True)
        sums[7:8, :] += jnp.sum(low, axis=0, keepdims=True)
        sums[12:13, :] += jnp.sum(m * m * valid, axis=0, keepdims=True)


def back_kernel(seqs, *refs):
    info, ea, qkv, w_attn, mine, yours, sums, wbuf, eo, sem = refs
    rows = ea.shape[0] // seqs
    d = ea.shape[1]
    half = d // 2
    fetch(w_attn, wbuf, sem, 3 * half, half).wait()

    @pl.loop(0, 4)
    def _(s):
        near = pl.ds(pl.multiple_of(s * (d // 4), d // 4), d // 4)
        got = mm_nt(ea[:, 0:half], wbuf[0, near, :]) + mm_nt(ea[:, half:], wbuf[1, near, :])
        eo[:, near] = got.astype(bf16)

    low, high, first = head_masks()
    pairs = half // (2 * HEAD)
    scale = 1.0 / math.sqrt(HEAD)
    sums[...] = jnp.zeros_like(sums)
    for e, dst in ((0, mine), (1, yours)):
        core = info[1] ^ e

        @pl.loop(0, seqs * pairs)
        def _(i):
            n, j = i // pairs, i % pairs
            at = pl.ds(pl.multiple_of(n * rows, 16), rows)
            far = core * half + j * 2 * HEAD
            lanes = [pl.ds(pl.multiple_of(far + m * d, 2 * HEAD), 2 * HEAD) for m in range(3)]
            k_pair = qkv[at, lanes[1]]
            q_both = two_heads(qkv[at, lanes[0]], low, high)
            probs = pair_probs(q_both, k_pair, info[4 + n])
            eo_both = two_heads(eo[at, lanes[0]], low, high)
            ep = mm_nt(eo_both, qkv[at, lanes[2]])
            inner = jnp.sum(probs * ep, axis=-1, keepdims=True)
            es = (probs * (ep - inner)).astype(bf16)
            ev = mm_tn(probs.astype(bf16), eo_both).astype(bf16)
            eq = (pick_heads(mm(es, k_pair), first) * scale).astype(bf16)
            ek = (mm_tn(es, q_both) * scale).astype(bf16)
            for m, value in enumerate((eq, ek, ev)):
                dst[at, pl.ds(pl.multiple_of(m * half + j * 2 * HEAD, 2 * HEAD), 2 * HEAD)] = value
            sums[2:3, lanes[0]] += jnp.sum(eq.astype(f32), axis=0, keepdims=True)
            sums[3:4, lanes[0]] += jnp.sum(ev.astype(f32), axis=0, keepdims=True)


def input_kernel(seqs, buf, *refs):
    info, keep, mine, yours, x, er, vec, w_attn, out, sums, wbuf, t_acc, sem = refs
    rows = x.shape[0] // seqs
    d = x.shape[1]
    half = d // 2
    fetch(w_attn, wbuf, sem, 0, 3 * half).wait()
    core = info[1]

    @pl.loop(0, 4)
    def _(s):
        near = pl.ds(pl.multiple_of(s * (d // 4), d // 4), d // 4)
        t_acc[:, near] = mm_nt(mine[...], wbuf[core, near, :]) + mm_nt(yours[...], wbuf[1 - core, near, :])

    sums[...] = jnp.zeros_like(sums)

    @pl.loop(0, seqs)
    def _(n):
        at = pl.ds(pl.multiple_of(n * rows, 16), rows)
        normal, inverse = layer_stats(x[at, :].astype(f32))
        t = t_acc[at, :]
        grad = er[at, :] + norm_back(t, normal, inverse, vec[0:1, :])
        sums[0:1, :] += jnp.sum(t * normal, axis=0, keepdims=True)
        sums[1:2, :] += jnp.sum(t, axis=0, keepdims=True)
        out[n, 0:buf, :] = grad[0:buf]
        pick = picker(keep[n], rows - buf)
        rest = grad[buf:]
        high = rest.astype(bf16)
        rest = rest - high.astype(f32)
        middle = rest.astype(bf16)
        low = (rest - middle.astype(f32)).astype(bf16)
        out[n, buf:, :] = mm_tn(pick, high) + mm_tn(pick, middle) + mm_tn(pick, low)


def grad_kernel(order, a_own, a_got, b_own, b_got, out):
    left = jnp.concatenate([a_own[...], a_got[...]], axis=0)
    right = jnp.concatenate([b_own[...], b_got[...]], axis=0)
    out[0] = mm_tn(left, right).astype(bf16)


def weight_grad(order, a_own, a_got, b_own, b_got, deep, wide, tile, b_start=0):
    rows = a_own.shape[0]
    blocks = 2
    return pl.pallas_call(
        grad_kernel,
        grid_spec=pltpu.PrefetchScalarGridSpec(
            num_scalar_prefetch=1,
            grid=(blocks, wide // tile),
            in_specs=[pl.BlockSpec((rows, deep), lambda i, j, order: (0, order[i]))] * 2
            + [pl.BlockSpec((rows, tile), lambda i, j, order: (0, order[2] * b_start + j))] * 2,
            out_specs=pl.BlockSpec((1, deep, tile), lambda i, j, order: (i, 0, j)),
        ),
        out_shape=sds((blocks, deep, wide), bf16),
        compiler_params=params(40),
        cost_estimate=cost(4 * rows * deep * wide * blocks, 4 * rows * (deep * 2 + wide)),
    )(order, a_own, a_got, b_own, b_got)


def adam_math(w, f, s, grad, rate, decay):
    first_new = beta_first * f + (1.0 - beta_first) * grad
    second_new = beta_second * s + (1.0 - beta_second) * grad * grad
    fix_first = 1.0 - beta_first**STEP
    fix_second = 1.0 - beta_second**STEP
    update = first_new / fix_first / (jnp.sqrt(second_new / fix_second) + adam_epsilon)
    return w - rate * (update + decay * w), first_new, second_new


def adam_kernel(info, w, f, s, g0, g1, g2, g3, *rest):
    w_out, f_out, s_out, low_out = rest[-4:]
    quarter = pl.program_id(0)
    for k, part in enumerate((g0, g1, g2, g3)):

        @pl.when(quarter == k)
        def _():
            new, first, second = adam_math(
                w[...], f[...], s[...], part[...].astype(f32), rate_matrix, weight_decay
            )
            w_out[...] = new
            f_out[...] = first
            s_out[...] = second
            low_out[...] = new.astype(bf16)


def adam_call(info, state, quarters, block, grid_width, place, grad_place, aliased=None):
    spec = pl.BlockSpec(block, place)
    shape = state[0].shape
    grads = [
        pl.BlockSpec(block, functools.partial(lambda k, i, j, info: grad_place(jnp.where(i == k, j, 0)), k))
        for k in range(4)
    ]
    extra = [] if aliased is None else list(aliased)
    return pl.pallas_call(
        adam_kernel,
        grid_spec=pltpu.PrefetchScalarGridSpec(
            num_scalar_prefetch=1,
            grid=(4, grid_width),
            in_specs=[spec] * 3 + grads + [ANY_SPEC] * len(extra),
            out_specs=[spec] * 4,
        ),
        out_shape=[sds(shape, f32)] * 3 + [sds(shape, bf16)],
        input_output_aliases={8 + k: k for k in range(len(extra))},
        compiler_params=params(40),
        cost_estimate=cost(20 * 4 * grid_width * block[0] * block[1], 28 * 4 * grid_width * block[0] * block[1]),
    )(info, *state, *quarters, *extra)


def add_low(a, b):
    return (a.astype(f32) + b.astype(f32)).astype(bf16)


def local(groups, replicas, *args):
    tokens, keep, cot, mats, down, vectors, f_mats, f_down, f_vectors, s_mats, s_down, s_vectors = args
    seqs, length, d = tokens.shape
    image = keep.shape[1]
    buf = length - image
    rows = -(-(buf + KEEP_MAX) // 16) * 16
    total = seqs * rows
    half = d // 2
    group, replica = lax.axis_index("group"), lax.axis_index("dp")
    core, level = replica % 2, (replica // 2) % 2
    counts = buf + jnp.sum(keep, axis=1)
    info = jnp.concatenate([jnp.stack([group, core, level, 0 * core]), counts]).astype(jnp.int32)

    def permute(value, target):
        pairs = []
        for a in range(groups):
            for b in range(replicas):
                to_a, to_b = target(a, b)
                pairs.append((a * replicas + b, to_a * replicas + to_b))
        return lax.ppermute(value, BOTH, pairs)

    hop_one = lambda v: permute(v, lambda a, b: (a ^ (1 + b % 2), b))
    hop_two = lambda v: permute(v, lambda a, b: (a ^ (2 - b % 2), b))
    swap = lambda v: permute(v, lambda a, b: (a, b ^ 1))
    shift = lambda v, bit: permute(v, lambda a, b: (a, b ^ bit))

    keep3 = keep.reshape(seqs, 1, image)
    deep = mats.shape[0]
    w_attn, w_up, w_down, x, em, h1, vec, qkv, o, r, h2, stats = pl.pallas_call(
        functools.partial(attend_kernel, seqs, buf),
        in_specs=[SMEM_SPEC] + [VMEM_SPEC] * 2 + [ANY_SPEC] * 4,
        out_specs=[ANY_SPEC] * 3 + [VMEM_SPEC] * 9,
        out_shape=[
            sds((2, d, 2 * d), bf16),
            sds((2, d, 2 * d), bf16),
            sds((2, 2 * d, d), bf16),
            sds((total, d), bf16),
            sds((total, d), bf16),
            sds((total, d), bf16),
            sds((16, d), f32),
            sds((total, 3 * d), bf16),
            sds((total, d), bf16),
            sds((total, d), f32),
            sds((total, d), bf16),
            sds((8, d), f32),
        ],
        scratch_shapes=[
            pltpu.VMEM((2, d, 2 * d), bf16),
            pltpu.VMEM((2, deep, 2 * d), f32),
            pltpu.VMEM((half, d), f32),
            pltpu.VMEM((deep, 2 * d), bf16),
            pltpu.VMEM((half, d), bf16),
            pltpu.VMEM((2, seqs, length, d), bf16),
            pltpu.VMEM((4, 16, d // 4), bf16),
            pltpu.SemaphoreType.DMA((3, 10)),
            pltpu.SemaphoreType.DMA((3, 10)),
            pltpu.SemaphoreType.DMA((3,)),
            pltpu.SemaphoreType.DMA((3,)),
            pltpu.SemaphoreType.DMA((9,)),
            pltpu.SemaphoreType.DMA((3,)),
            pltpu.SemaphoreType.DMA((2, seqs)),
        ],
        compiler_params=params(60, collective_id=0, has_side_effects=True),
        cost_estimate=cost(2 * total * 4 * d * d * 4, 20 * total * d),
    )(counts.astype(jnp.int32), keep3, vectors, mats, down, tokens, cot)
    h1_got, em_got = swap(h1), swap(em)
    o_got, h2_got = swap(o), swap(h2)

    z_mine, z_yours, u_mine, u_yours, er, ea, block_output, sums_feed = pl.pallas_call(
        functools.partial(feed_kernel, seqs, buf),
        in_specs=[SMEM_SPEC] + [VMEM_SPEC] * 5 + [ANY_SPEC] * 2,
        out_specs=[VMEM_SPEC] * 8,
        out_shape=[sds((total, 2 * d), bf16)] * 4
        + [
            sds((total, d), f32),
            sds((total, d), bf16),
            sds((seqs, length, d), bf16),
            sds((16, d), f32),
        ],
        scratch_shapes=[
            pltpu.VMEM((2, d, 2 * d), bf16),
            pltpu.VMEM((2, 2 * d, d), bf16),
            pltpu.VMEM((total, d), f32),
            pltpu.VMEM((total, d), f32),
            pltpu.SemaphoreType.DMA((2, 2)),
        ],
        compiler_params=params(60),
        cost_estimate=cost(2 * total * 16 * d * d, 60 * total * d),
    )(info, keep3, h2, em, r, vec, w_up, w_down)

    z_got, u_got, ea_got = swap(z_yours), swap(u_yours), swap(ea)

    first, second = core + 1, 2 - core
    send_order = jnp.stack([group ^ first, group ^ 3, core]).astype(jnp.int32)
    keep_order = jnp.stack([group, group ^ second, core]).astype(jnp.int32)

    def reduce_blocks(make):
        sent = make(send_order)
        got = hop_one(sent)
        kept = make(keep_order)
        kept = add_low(kept, got)
        mine = add_low(kept[0], hop_two(kept[1]))
        deep = mine.shape[0] // 2
        give = lax.dynamic_slice(mine, ((1 - level) * deep, 0), (deep, mine.shape[1]))
        hold = lax.dynamic_slice(mine, (level * deep, 0), (deep, mine.shape[1]))
        hold = add_low(hold, shift(give, 2))
        bit = 4
        while bit < replicas:
            hold = add_low(hold, shift(hold, bit))
            bit *= 2
        other = shift(hold, 2)
        return hold, other, swap(hold), swap(other)

    g_down = reduce_blocks(
        lambda order: weight_grad(order, z_mine, z_got, em, em_got, half, d, half)
    )

    def up_and_out(order):
        return weight_grad(order, h2, h2_got, u_mine, u_got, d // 4, 2 * d, half)

    g_up = reduce_blocks(up_and_out)
    g_out = reduce_blocks(lambda order: weight_grad(order, o, o_got, ea, ea_got, d // 4, half, half, 1))

    e_mine, e_yours, sums_back = pl.pallas_call(
        functools.partial(back_kernel, seqs),
        in_specs=[SMEM_SPEC] + [VMEM_SPEC] * 2 + [ANY_SPEC],
        out_specs=[VMEM_SPEC] * 3,
        out_shape=[sds((total, 3 * half), bf16)] * 2 + [sds((8, d), f32)],
        scratch_shapes=[
            pltpu.VMEM((2, d, half), bf16),
            pltpu.VMEM((total, d), bf16),
            pltpu.SemaphoreType.DMA(()),
        ],
        compiler_params=params(48),
        cost_estimate=cost(2 * total * 4 * d * d, 20 * total * d),
    )(info, ea, qkv, w_attn)
    e_got = swap(e_yours)
    g_qkv = reduce_blocks(
        lambda order: weight_grad(order, h1, h1_got, e_mine, e_got, d // 4, 3 * half, half)
    )

    input_grad, sums_in = pl.pallas_call(
        functools.partial(input_kernel, seqs, buf),
        in_specs=[SMEM_SPEC] + [VMEM_SPEC] * 6 + [ANY_SPEC],
        out_specs=[VMEM_SPEC] * 2,
        out_shape=[sds((seqs, length, d), f32), sds((8, d), f32)],
        scratch_shapes=[
            pltpu.VMEM((2, d, 3 * half), bf16),
            pltpu.VMEM((total, d), f32),
            pltpu.SemaphoreType.DMA(()),
        ],
        compiler_params=params(56),
        cost_estimate=cost(2 * total * 3 * d * d, 20 * total * d),
    )(info, keep3, e_mine, e_yours, x, er, vec, w_attn)

    squares = jnp.stack([jnp.sum(stats[0]), jnp.sum(stats[1]), jnp.sum(sums_feed[12]), jnp.sum(counts).astype(f32)])
    small = jnp.concatenate(
        [
            sums_in[0:2],
            sums_back[2:4],
            sums_feed[4:12],
            jnp.pad(squares.reshape(1, 4), ((0, 3), (0, d - 4))),
        ]
    )
    bit = 1
    while bit < groups:
        small = small + permute(small, functools.partial(lambda flip, a, b: (a ^ flip, b), bit))
        bit *= 2
    bit = 1
    while bit < replicas:
        small = small + shift(small, bit)
        bit *= 2
    branch_rms = jnp.sqrt(small[12, 0:3] / (small[12, 3] * d))
    part = vectors.shape[1]
    grad_vectors = lax.dynamic_slice(small, (0, group * part), (12, part))

    def core_of(k, info):
        return info[1] ^ (k // 2)

    def level_of(k, info):
        return info[2] ^ (k % 2)

    new_down = adam_call(
        info,
        (down, f_down, s_down),
        g_down,
        (down.shape[0] // 4, half),
        2,
        lambda i, j, info: (2 * core_of(i, info) + level_of(i, info), j),
        lambda j: (0, j),
    )

    def adam_mats(quarters, first_strip, strips, previous):
        return adam_call(
            info,
            (mats, f_mats, s_mats),
            quarters,
            (mats.shape[0] // 2, half),
            strips,
            lambda i, j, info: (level_of(i, info), 2 * (first_strip + j) + core_of(i, info)),
            lambda j: (0, j),
            previous,
        )

    new_mats = adam_mats(g_up, 4, 4, None)
    new_mats = adam_mats(g_out, 3, 1, new_mats)
    new_mats = adam_mats(g_qkv, 0, 3, new_mats)
    new_vectors, first_vectors, second_vectors = adam_math(
        vectors, f_vectors, s_vectors, grad_vectors, rate_vector, 0.0
    )
    return (
        block_output,
        input_grad,
        new_mats[0],
        new_down[0],
        new_vectors,
        new_mats[1],
        new_down[1],
        first_vectors,
        new_mats[2],
        new_down[2],
        second_vectors,
        new_mats[3],
        new_down[3],
        new_vectors.astype(bf16),
        branch_rms,
    )


def solution(mesh):
    rows, owned, columns = P(BOTH, None, None), P("group", None), P(None, "group")
    state = (owned, owned, columns)
    return jax.shard_map(
        functools.partial(local, mesh.shape["group"], mesh.shape["dp"]),
        mesh=mesh,
        in_specs=(rows, P(BOTH, None), rows) + state * 3,
        out_specs=(rows, rows) + state * 4 + (P(),),
        check_vma=False,
    )
```

```python
import functools
import math

import jax
import jax.numpy as jnp
from jax import lax
from jax.experimental import pallas as pl
from jax.experimental.pallas import tpu as pltpu
from jax.sharding import PartitionSpec as P

HEAD = 64
STEP = 7
KEEP_MAX = 77

norm_epsilon = 1e-06
beta_first = 0.5
beta_second = 0.5
adam_epsilon = 1e-08
rate_matrix = 0.05
rate_vector = 0.3
weight_decay = 0.05
root_half = 0.7071067811865476
inverse_root_two_pi = 0.3989422804014327

bf16 = jnp.bfloat16
f32 = jnp.float32
BOTH = ("group", "dp")
VMEM_SPEC = pl.BlockSpec(memory_space=pltpu.VMEM)
SMEM_SPEC = pl.BlockSpec(memory_space=pltpu.SMEM)
ANY_SPEC = pl.BlockSpec(memory_space=pl.ANY)
MIB = 1 << 20


def mm(a, b):
    return jnp.dot(a, b, preferred_element_type=f32)


def mm_nt(a, b):
    return lax.dot_general(a, b, (((1,), (1,)), ((), ())), preferred_element_type=f32)


def mm_tn(a, b):
    return lax.dot_general(a, b, (((0,), (0,)), ((), ())), preferred_element_type=f32)


def sds(shape, dtype):
    return jax.ShapeDtypeStruct(shape, dtype)


def params(mib, **more):
    return pltpu.CompilerParams(vmem_limit_bytes=mib * MIB, **more)


def cost(flops, nbytes):
    return pl.CostEstimate(flops=int(flops), bytes_accessed=int(nbytes), transcendentals=0)


def layer_stats(values):
    centre = jnp.mean(values, axis=-1, keepdims=True)
    centred = values - centre
    variance = jnp.mean(centred * centred, axis=-1, keepdims=True)
    inverse = lax.rsqrt(variance + norm_epsilon)
    return centred * inverse, inverse


def norm_back(grad_normed, normal, inverse, gain):
    scaled = grad_normed * gain
    mean_one = jnp.mean(scaled, axis=-1, keepdims=True)
    mean_two = jnp.mean(scaled * normal, axis=-1, keepdims=True)
    return inverse * (scaled - mean_one - normal * mean_two)


def picker(keep_row, rows):
    image = keep_row.shape[1]
    ahead = lax.broadcasted_iota(jnp.int32, (image, image), 0)
    here = lax.broadcasted_iota(jnp.int32, (image, image), 1)
    upper = jnp.where(ahead <= here, 1.0, 0.0).astype(bf16)
    kept = keep_row.astype(f32)
    place = mm(kept.astype(bf16), upper) - 1.0
    place = jnp.where(kept > 0.5, place, -1.0)
    want = lax.broadcasted_iota(jnp.int32, (rows, image), 0).astype(f32)
    return jnp.where(place == want, 1.0, 0.0).astype(bf16)


MESH = pl.DeviceIdType.MESH


def flip(value, bit):
    return value + bit - 2 * bit * ((value // bit) % 2)


class Place:
    def __init__(self):
        self.group, self.replica = lax.axis_index("group"), lax.axis_index("dp")
        self.core, self.level = self.replica % 2, (self.replica // 2) % 2
        one, two = flip(self.group, 1), flip(self.group, 2)
        self.first = (1 - self.core) * one + self.core * two
        self.second = (1 - self.core) * two + self.core * one
        self.third = flip(one, 2)
        self.to_first = (self.first, self.replica)
        self.to_second = (self.second, self.replica)
        self.to_third = (self.third, self.replica)
        self.to_core = (self.group, flip(self.replica, 1))

    def to_bit(self, bit):
        return (self.group, flip(self.replica, bit))

    def meet(self, partners):
        barrier = pltpu.get_barrier_semaphore()
        for partner in partners:
            pl.semaphore_signal(barrier, inc=1, device_id=partner, device_id_type=MESH)
        pl.semaphore_wait(barrier, len(partners))


class Gather:
    def __init__(self, place, own, full, send, recv):
        self.place, self.own, self.full, self.send, self.recv = place, own, full, send, recv
        deep = own.shape[0]
        self.deep, self.strip = deep, 5 * deep // 16
        self.main = deep - self.strip
        self.main_at = place.level * self.strip
        self.strip_at = place.level * self.main

    def block(self, owner, start, size):
        at = pl.multiple_of(owner * self.deep + start, 16)
        return self.full.at[self.place.core, pl.ds(at, size), :]

    def make(self, k, owner, start, size, device):
        view = self.block(owner, start, size)
        return pltpu.make_async_remote_copy(
            src_ref=view, dst_ref=view, send_sem=self.send.at[k], recv_sem=self.recv.at[k],
            device_id=device, device_id_type=MESH,
        )

    def plan(self, k):
        p = self.place
        main, strip, whole = (self.main_at, self.main), (self.strip_at, self.strip), (0, self.deep)
        return (
            (p.group, *main, p.to_first),
            (p.group, *main, p.to_second),
            (p.first, *main, p.to_second),
            (p.first, *strip, p.to_bit(2)),
            (p.second, *strip, p.to_bit(2)),
            (p.third, *strip, p.to_bit(2)),
            (p.group, *whole, p.to_core),
            (p.first, *whole, p.to_core),
            (p.second, *whole, p.to_core),
            (p.third, *whole, p.to_core),
        )[k]

    def start(self, *ks):
        for k in ks:
            owner, at, size, device = self.plan(k)
            if k in (0, 1, 6):
                start = pl.multiple_of(at, 16) if k < 6 else 0
                pltpu.make_async_remote_copy(
                    src_ref=self.own.at[pl.ds(start, size), :], dst_ref=self.block(owner, at, size),
                    send_sem=self.send.at[k], recv_sem=self.recv.at[k], device_id=device, device_id_type=MESH,
                ).start()
            else:
                self.make(k, owner, at, size, device).start()

    def arrived(self, *ks):
        for k in ks:
            self.make(k, *self.plan(k)).wait_recv()

    def sent(self, *ks):
        for k in ks:
            self.make(k, *self.plan(k)).wait_send()

    def step_one(self):
        self.start(0, 1, 6)

    def step_two(self):
        self.arrived(0)
        self.start(2, 3)
        self.arrived(1)
        self.start(4)

    def step_three(self):
        self.arrived(2)
        self.start(5)
        self.arrived(3)
        self.start(7)
        self.arrived(4)
        self.start(8)

    def step_four(self):
        self.arrived(5)
        self.start(9)

    def step_five(self):
        self.arrived(6, 7, 8, 9)
        self.sent(*range(10))


def head_masks():
    lane = lax.broadcasted_iota(jnp.int32, (1, 2 * HEAD), 1)
    low = jnp.where(lane < HEAD, 1.0, 0.0)
    return low.astype(bf16), (1.0 - low).astype(bf16), low > 0.5


def two_heads(x, low, high):
    return jnp.concatenate([x * low, x * high], axis=0)


def pick_heads(both, first):
    rows = both.shape[0] // 2
    return jnp.where(first, both[:rows], both[rows:])


def pair_probs(q_pair, k_pair, count):
    raw = mm_nt(q_pair, k_pair) * (1.0 / math.sqrt(HEAD))
    col = lax.broadcasted_iota(jnp.int32, raw.shape, 1)
    raw = jnp.where(col < count, raw, -1e30)
    top = jnp.max(raw, axis=-1, keepdims=True)
    exponent = jnp.exp(raw - top)
    return exponent / jnp.sum(exponent, axis=-1, keepdims=True)


def attend_kernel(seqs, buf, *refs):
    counts, keep, vectors, mats, down, tokens, cot = refs[:7]
    w_attn, w_up, w_down, x, em, h1, vec, qkv, o, r, h2, stats = refs[7:19]
    wbuf, wide, tall, low_up, low_down, rows_in, parts, send, recv, vec_send, vec_recv, loads, stores, reads = refs[19:]
    rows = h1.shape[0] // seqs
    d = h1.shape[1]
    half = d // 2
    place = Place()
    core = place.core
    deep = mats.shape[0]

    takes = []
    for j in range(8):
        at = pl.ds(pl.multiple_of((2 * j + core) * half, half), half)
        takes.append(
            pltpu.make_async_copy(mats.at[:, at], wide.at[j // 4, :, pl.ds((j % 4) * half, half)], loads.at[j])
        )
    takes.append(
        pltpu.make_async_copy(down.at[pl.ds(pl.multiple_of(core * half, half), half), :], tall, loads.at[8])
    )
    for one in takes:
        one.start()
    reads_in = []
    for n in range(seqs):
        for k, src in enumerate((tokens, cot)):
            reads_in.append(pltpu.make_async_copy(src.at[n], rows_in.at[k, n], reads.at[k, n]))
    for one in reads_in:
        one.start()

    place.meet((place.to_first, place.to_second, place.to_third, place.to_core, place.to_bit(2)))

    part = vectors.shape[1]
    parts[place.group] = jnp.concatenate([vectors[...], jnp.zeros((4, part), f32)], axis=0).astype(bf16)
    for k, partner in enumerate((place.to_first, place.to_second, place.to_third)):
        pltpu.make_async_remote_copy(
            src_ref=parts.at[place.group], dst_ref=parts.at[place.group],
            send_sem=vec_send.at[k], recv_sem=vec_recv.at[k], device_id=partner, device_id_type=MESH,
        ).start()

    for one in takes[:4]:
        one.wait()
    own = wbuf.at[core, pl.ds(pl.multiple_of(place.group * deep, deep), deep), :]
    own[...] = wide[0].astype(bf16)
    attn = Gather(place, own, wbuf, send.at[0], recv.at[0])
    attn.step_one()
    for one in takes[4:]:
        one.wait()
    low_up[...] = wide[1].astype(bf16)
    low_down[...] = tall[...].astype(bf16)
    up = Gather(place, low_up, w_up, send.at[1], recv.at[1])
    downs = Gather(place, low_down, w_down, send.at[2], recv.at[2])
    keep_up = pltpu.make_async_copy(low_up, up.block(place.group, 0, deep), stores.at[0])
    keep_down = pltpu.make_async_copy(low_down, downs.block(place.group, 0, half), stores.at[1])
    keep_up.start()
    keep_down.start()

    for one in reads_in:
        one.wait()

    @pl.loop(0, seqs)
    def _(n):
        at = pl.multiple_of(n * rows, 16)
        pick = picker(keep[n], rows - buf)
        for k, dst in ((0, x), (1, em)):
            dst[pl.ds(at, buf), :] = rows_in[k, n, 0:buf, :]
            dst[pl.ds(pl.multiple_of(at + buf, 16), rows - buf), :] = mm(pick, rows_in[k, n, buf:, :]).astype(bf16)

    attn.step_two()
    for k, partner in enumerate((place.first, place.second, place.third)):
        got = pltpu.make_async_remote_copy(
            src_ref=parts.at[place.group], dst_ref=parts.at[place.group],
            send_sem=vec_send.at[k], recv_sem=vec_recv.at[k], device_id=place.to_first, device_id_type=MESH,
        )
        got.wait()
    vec[...] = jnp.zeros_like(vec)
    for s in range(4):
        vec[:, s * part : (s + 1) * part] = parts[s].astype(f32)

    @pl.loop(0, seqs)
    def _(n):
        at = pl.ds(pl.multiple_of(n * rows, 16), rows)
        normal, _ = layer_stats(x[at, :].astype(f32))
        h1[at, :] = (normal * vec[0:1, :] + vec[1:2, :]).astype(bf16)

    up.step_one()
    attn.step_three()
    attn.step_four()
    attn.step_five()
    keep_attn = pltpu.make_async_copy(wbuf, w_attn, stores.at[2])
    keep_attn.start()

    @pl.loop(0, 4)
    def _(i):
        h, t = i // 2, i % 2
        tile = half // 2
        near = pl.multiple_of(i * tile, tile)
        for j in range(3):
            w = wbuf[h, :, pl.ds(pl.multiple_of(j * half + t * tile, tile), tile)]
            got = mm(h1[...], w)
            if j != 1:
                got = got + vec[2 + j // 2 : 3 + j // 2, pl.ds(near, tile)]
            qkv[:, pl.ds(pl.multiple_of(j * d + near, tile), tile)] = got.astype(bf16)

    up.step_two()
    downs.step_one()
    low, high, first = head_masks()
    pairs = d // (2 * HEAD)
    steps = {
        4: up.step_three,
        8: up.step_four,
        12: downs.step_two,
        20: downs.step_three,
        26: downs.step_four,
    }

    @pl.loop(0, seqs * pairs)
    def _(i):
        for when, step in steps.items():
            pl.when(i == when)(step)
        n, j = i // pairs, i % pairs
        at = pl.ds(pl.multiple_of(n * rows, 16), rows)
        lanes = [pl.ds(pl.multiple_of(j * 2 * HEAD + m * d, 2 * HEAD), 2 * HEAD) for m in range(3)]
        q_pair = two_heads(qkv[at, lanes[0]], low, high)
        probs = pair_probs(q_pair, qkv[at, lanes[1]], counts[n]).astype(bf16)
        o[at, lanes[0]] = pick_heads(mm(probs, qkv[at, lanes[2]]), first).astype(bf16)

    @pl.loop(0, 4)
    def _(i):
        h, t = i // 2, i % 2
        tile = half // 2
        near = pl.ds(pl.multiple_of(i * tile, tile), tile)
        w = wbuf[h, :, pl.ds(pl.multiple_of(3 * half + t * tile, tile), tile)]
        r[:, near] = mm(o[...], w) + vec[4:5, near]

    stats[...] = jnp.zeros_like(stats)

    @pl.loop(0, seqs)
    def _(n):
        at = pl.ds(pl.multiple_of(n * rows, 16), rows)
        valid = lax.broadcasted_iota(jnp.int32, (rows, 1), 0) < counts[n]
        valid = jnp.where(valid, 1.0, 0.0)
        inputs = x[at, :].astype(f32)
        branch = r[at, :]
        resid = inputs + branch
        r[at, :] = resid
        normal, _ = layer_stats(resid)
        h2[at, :] = (normal * vec[5:6, :] + vec[6:7, :]).astype(bf16)
        stats[0:1, :] += jnp.sum(inputs * inputs * valid, axis=0, keepdims=True)
        stats[1:2, :] += jnp.sum(branch * branch * valid, axis=0, keepdims=True)

    up.step_five()
    downs.step_five()
    keep_up.wait()
    keep_down.wait()
    keep_attn.wait()


def swap_start(place, src, dst, send, recv, k):
    copy = pltpu.make_async_remote_copy(
        src_ref=src, dst_ref=dst, send_sem=send.at[k], recv_sem=recv.at[k],
        device_id=place.to_core, device_id_type=MESH,
    )
    copy.start()
    return copy


def feed_kernel(seqs, buf, *refs):
    counts, keep, h2, em, r, vec, h2_hbm, em_hbm, ups, downs = refs[:10]
    z_mine, u_mine, er, ea, out, sums, h2_got, em_got, z_got, u_got = refs[10:20]
    wup, wdown, m_acc, t_acc, z_yours, u_yours, sems, send, recv = refs[20:]
    rows = h2.shape[0] // seqs
    d = h2.shape[1]
    strip = wup.shape[2] // 4
    tile = strip // 2
    place = Place()
    copies = []
    for e in range(2):
        core = (1 - place.core) * (1 - e) + place.core * e
        copies.append(pltpu.make_async_copy(ups.at[core], wup.at[e], sems.at[e, 0]))
        copies.append(pltpu.make_async_copy(downs.at[core], wdown.at[e], sems.at[e, 1]))
    for one in copies:
        one.start()
    place.meet((place.to_core,))
    swaps = [
        swap_start(place, em_hbm, em_got, send, recv, 0),
        swap_start(place, h2_hbm, h2_got, send, recv, 1),
    ]
    sums[...] = jnp.zeros_like(sums)
    m_acc[...] = jnp.zeros_like(m_acc)
    t_acc[...] = jnp.zeros_like(t_acc)
    for e, z_out, u_out in ((0, z_yours, u_yours), (1, z_mine, u_mine)):
        core = (1 - place.core) * (1 - e) + place.core * e
        for one in copies[2 * e : 2 * e + 2]:
            one.wait()

        @pl.loop(0, 8)
        def _(i):
            s, t = i // 2, i % 2
            near = pl.ds(pl.multiple_of(i * tile, tile), tile)
            far = (pl.ds(8 + s, 1), pl.ds(pl.multiple_of(core * strip + t * tile, tile), tile))
            w_up = wup[e, :, near]
            w_down = wdown[e, near, :]
            u = mm(h2[...], w_up) + vec[far]
            phi = 0.5 * (1.0 + lax.erf(u * root_half))
            z = (u * phi).astype(bf16)
            z_out[t, :, pl.ds(pl.multiple_of(s * tile, tile), tile)] = z
            slope = phi + u * jnp.exp(-0.5 * u * u) * inverse_root_two_pi
            eu = (mm_nt(em[...], w_down) * slope).astype(bf16)
            u_out[:, near] = eu
            m_acc[...] += mm(z, w_down)
            t_acc[...] += mm_nt(eu, w_up)
            sums[far] = jnp.sum(eu.astype(f32), axis=0, keepdims=True)

        if e == 0:
            swaps.append(swap_start(place, z_yours, z_got, send, recv, 2))
            swaps.append(swap_start(place, u_yours, u_got, send, recv, 3))

    @pl.loop(0, seqs)
    def _(n):
        at = pl.ds(pl.multiple_of(n * rows, 16), rows)
        valid = lax.broadcasted_iota(jnp.int32, (rows, 1), 0) < counts[n]
        valid = jnp.where(valid, 1.0, 0.0)
        resid = r[at, :]
        m = m_acc[at, :] + vec[7:8, :]
        packed = ((resid + m) * valid).astype(bf16)
        out[n, 0:buf, :] = packed[0:buf]
        pick = picker(keep[n], rows - buf)
        out[n, buf:, :] = mm_tn(pick, packed[buf:]).astype(bf16)
        normal, inverse = layer_stats(resid)
        t = t_acc[at, :]
        low = em[at, :].astype(f32)
        back = low + norm_back(t, normal, inverse, vec[5:6, :])
        er[at, :] = back
        ea_low = back.astype(bf16)
        ea[at, :] = ea_low
        sums[4:5, :] += jnp.sum(ea_low.astype(f32), axis=0, keepdims=True)
        sums[5:6, :] += jnp.sum(t * normal, axis=0, keepdims=True)
        sums[6:7, :] += jnp.sum(t, axis=0, keepdims=True)
        sums[7:8, :] += jnp.sum(low, axis=0, keepdims=True)
        sums[12:13, :] += jnp.sum(m * m * valid, axis=0, keepdims=True)
    for one in swaps:
        one.wait()


class Timeline:
    def __init__(self):
        self.steps = []

    def add(self, when, step):
        self.steps.append((when, len(self.steps), step))
        self.steps.sort(key=lambda one: one[:2])

    def until(self, when):
        while self.steps and self.steps[0][0] <= when:
            self.steps.pop(0)[2]()

    def during(self, count, start, gap):
        due = []
        while self.steps and self.steps[0][0] < start + count * gap:
            when, _, step = self.steps.pop(0)
            due.append((min(max(int((when - start) / gap), 0), count - 1), step))

        def run(turn):
            for at, step in due:
                pl.when(turn == at)(step)

        return run


class Reduce:
    def __init__(self, place, bits, g, r1, r2, r3, r4, total, send, recv):
        self.place, self.bits, self.g, self.r1, self.r2, self.r3, self.r4 = place, bits, g, r1, r2, r3, r4
        self.total, self.send, self.recv = total, send, recv
        self.half = g.shape[1] // 2
        self.hold = r2.at[pl.ds(0, self.half)]
        self.slots = [r1.at[n // 2 % 2, pl.ds(n % 2 * self.half, self.half)] for n in range(len(bits))]

    def copy(self, k):
        p = self.place
        half = self.half
        mine, other = p.level * half, (1 - p.level) * half
        at = lambda start: pl.ds(pl.multiple_of(start, 16), half)
        plans = [
            (self.g.at[p.third], self.r1.at[1], p.to_first),
            (self.g.at[p.first], self.r1.at[0], p.to_first),
            (self.g.at[p.second], self.r2, p.to_second),
            (self.g.at[p.group, at(other)], self.r3, p.to_bit(2)),
            (self.hold, self.total.at[p.core, at(mine)], p.to_bit(2)),
            (self.hold, self.total.at[p.core, at(mine)], p.to_core),
            (self.total.at[p.core, at(other)], self.total.at[p.core, at(other)], p.to_core),
        ]
        for n, bit in enumerate(self.bits):
            plans.append((self.slots[n], self.r4.at[n], p.to_bit(bit)))
        src, dst, device = plans[k]
        return pltpu.make_async_remote_copy(
            src_ref=src, dst_ref=dst, send_sem=self.send.at[k], recv_sem=self.recv.at[k],
            device_id=device, device_id_type=MESH,
        )

    def begin(self):
        self.copy(0).start()
        self.copy(1).start()

    def pass_second(self):
        self.copy(0).wait_recv()
        at = self.place.second
        self.g[at] = (self.g[at].astype(f32) + self.r1[1].astype(f32)).astype(bf16)
        self.copy(2).start()

    def pass_replica(self):
        self.copy(1).wait_recv()
        self.copy(2).wait_recv()
        at = self.place.group
        self.g[at] = (self.g[at].astype(f32) + self.r1[0].astype(f32) + self.r2[...].astype(f32)).astype(bf16)
        self.copy(3).start()

    def pass_bit(self, n):
        p = self.place
        if n == 0:
            self.copy(3).wait_recv()
            at = pl.ds(pl.multiple_of(p.level * self.half, 16), self.half)
            value = self.g[p.group, at].astype(f32) + self.r3[...].astype(f32)
        else:
            self.copy(6 + n).wait_recv()
            value = self.slots[n - 1][...].astype(f32) + self.r4[n - 1].astype(f32)
        if n < len(self.bits):
            self.slots[n][...] = value.astype(bf16)
            self.copy(7 + n).start()
        else:
            self.hold[...] = value.astype(bf16)
            self.copy(4).start()
            self.copy(5).start()
            self.stay().start()

    def stay(self):
        p = self.place
        at = pl.ds(pl.multiple_of(p.level * self.half, 16), self.half)
        return pltpu.make_async_copy(self.hold, self.total.at[p.core, at], self.send.at[7 + len(self.bits)])

    def pass_core(self):
        self.copy(4).wait_recv()
        self.copy(6).start()

    def finish(self):
        self.copy(5).wait_recv()
        self.copy(6).wait_recv()
        for k in range(7 + len(self.bits)):
            self.copy(k).wait_send()
        self.stay().wait()


def tail_kernel(seqs, buf, bits, sizes, *refs):
    counts, keep, qkv, x, er, vec, stats, sums_feed = refs[:8]
    z_mine, z_got, em, em_got, h2, h2_got, u_mine, u_got, o, ea, h1, w_attn = refs[8:20]
    chunks = len(sizes)
    small, out = refs[20:22]
    totals = refs[22 : 22 + chunks]
    o_got, ea_got, h1_got, e_got = refs[22 + chunks : 26 + chunks]
    scratch = refs[26 + chunks :]
    wbuf, eo, e, t_acc, stage, sides, small_in = scratch[:7]
    buffers = [scratch[7 + k * chunks : 7 + (k + 1) * chunks] for k in range(5)]
    send, recv, w_sem, ea_sem, side_sems, stage_sem, swap_send, swap_recv, small_send, small_recv = scratch[7 + 5 * chunks :]
    total, d = eo.shape
    rows = total // seqs
    half, quarter = d // 2, d // 4
    place = Place()
    core = place.core

    o_weight = pltpu.make_async_copy(w_attn.at[:, :, pl.ds(3 * half, half)], wbuf.at[:, :, pl.ds(0, half)], w_sem)
    o_weight.start()
    ea_all = e.at[0, :, pl.ds(0, d)]
    take_ea = pltpu.make_async_copy(ea, ea_all, ea_sem)
    take_ea.start()

    mine_cols = pl.ds(pl.multiple_of(core * half, half), half)
    left = [(z_mine.at[0], z_got.at[0]), (z_mine.at[1], z_got.at[1]), (h2, h2_got), (h2, h2_got), (o, o_got), (h1, h1_got), (h1, h1_got)]
    right = [
        (em, em_got), (em, em_got),
        (u_mine.at[:, pl.ds(0, d)], u_got.at[:, pl.ds(0, d)]), (u_mine.at[:, pl.ds(d, d)], u_got.at[:, pl.ds(d, d)]),
        (ea.at[:, mine_cols], ea_got.at[:, mine_cols]),
        (e.at[core, :, pl.ds(0, d)], e_got.at[:, pl.ds(0, d)]), (e.at[core, :, pl.ds(d, half)], e_got.at[:, pl.ds(d, half)]),
    ]

    def side_copies(k):
        found = []
        for side, pairs in enumerate((left, right)):
            wide = sizes[k] if side else d
            for which, src in enumerate(pairs[k]):
                dst = sides.at[k % 2, side, pl.ds(which * total, total), pl.ds(0, wide)]
                found.append(pltpu.make_async_copy(src, dst, side_sems.at[k % 2, side, which]))
        return found

    def load_sides(k):
        for one in side_copies(k):
            one.start()

    load_sides(0)
    load_sides(1)
    partners = [place.to_first, place.to_second, place.to_core, place.to_bit(2)] + [place.to_bit(b) for b in bits]
    place.meet(partners)
    swaps = [
        swap_start(place, o, o_got, swap_send, swap_recv, 0),
        swap_start(place, ea, ea_got, swap_send, swap_recv, 1),
        swap_start(place, h1, h1_got, swap_send, swap_recv, 2),
    ]
    sent_e = pltpu.make_async_remote_copy(
        src_ref=e.at[1 - core], dst_ref=e_got, send_sem=swap_send.at[3], recv_sem=swap_recv.at[3],
        device_id=place.to_core, device_id_type=MESH,
    )
    reduces = [
        Reduce(place, bits, *(buffers[b][k] for b in range(5)), totals[k], send.at[k], recv.at[k]) for k in range(chunks)
    ]

    def gradient(k):
        for one in side_copies(k):
            one.wait()
        wide = sizes[k]

        @pl.loop(0, 4)
        def _(i):
            near = place.first * (1 - i // 2) + place.group * (i // 2)
            over = ((i + 1) // 2) % 2
            bit_two = (1 - core) * flip(near, 2) + core * flip(near, 1)
            owner = near * (1 - over) + bit_two * over
            cols = pl.ds(pl.multiple_of(owner * quarter, quarter), quarter)
            reduces[k].g[owner] = mm_tn(sides[k % 2, 0, :, cols], sides[k % 2, 1, :, 0:wide]).astype(bf16)

    line = Timeline()
    start = 3.0
    for k in range(chunks):
        size = sizes[k] / d
        if k == 5:
            start = max(start, 58.0)
        one = reduces[k]
        line.add(start, one.begin)
        when = start + 9.0 * size + 2
        line.add(when, one.pass_second)
        when = start + 17.0 * size + 3
        line.add(when, one.pass_replica)
        when += 7 * size + 2
        for n in range(len(bits) + 1):
            line.add(when, functools.partial(one.pass_bit, n))
            when += 10 * size + 2
        line.add(when, one.pass_core)
        line.add(when + 6 * size + 3, one.finish)
        start += 17.0 * size

    gradient(0)
    load_sides(2)
    line.until(3)
    gradient(1)
    load_sides(3)
    line.until(6)
    gradient(2)
    for one in swaps[:2]:
        one.wait()
    load_sides(4)
    line.until(9)
    gradient(3)
    line.until(12)
    gradient(4)
    swaps[2].wait()
    line.until(14)
    o_weight.wait()
    take_ea.wait()

    @pl.loop(0, 4)
    def _(s):
        near = pl.ds(pl.multiple_of(s * quarter, quarter), quarter)
        got = mm_nt(ea_all[:, 0:half], wbuf[0, near, 0:half]) + mm_nt(ea_all[:, half:], wbuf[1, near, 0:half])
        eo[:, near] = got.astype(bf16)

    in_weight = pltpu.make_async_copy(w_attn.at[:, :, pl.ds(0, 3 * half)], wbuf, w_sem)
    in_weight.start()
    line.until(17)
    low, high, first = head_masks()
    pairs = half // (2 * HEAD)
    scale = 1.0 / math.sqrt(HEAD)
    small[...] = jnp.zeros_like(small)
    turns = seqs * pairs

    due = line.during(2 * turns, 17.0, 0.9)

    @pl.loop(0, 2 * turns)
    def _(i):
        pl.when(i == turns)(sent_e.start)
        due(i)
        h = (1 - core) * (1 - i // turns) + core * (i // turns)
        n, j = (i % turns) // pairs, i % pairs
        at = pl.ds(pl.multiple_of(n * rows, 16), rows)
        far = h * half + j * 2 * HEAD
        lanes = [pl.ds(pl.multiple_of(far + m * d, 2 * HEAD), 2 * HEAD) for m in range(3)]
        k_pair = qkv[at, lanes[1]]
        q_both = two_heads(qkv[at, lanes[0]], low, high)
        probs = pair_probs(q_both, k_pair, counts[n])
        eo_both = two_heads(eo[at, lanes[0]], low, high)
        ep = mm_nt(eo_both, qkv[at, lanes[2]])
        inner = jnp.sum(probs * ep, axis=-1, keepdims=True)
        es = (probs * (ep - inner)).astype(bf16)
        ev = mm_tn(probs.astype(bf16), eo_both).astype(bf16)
        eq = (pick_heads(mm(es, k_pair), first) * scale).astype(bf16)
        ek = (mm_tn(es, q_both) * scale).astype(bf16)
        for m, value in enumerate((eq, ek, ev)):
            e[h, at, pl.ds(pl.multiple_of(m * half + j * 2 * HEAD, 2 * HEAD), 2 * HEAD)] = value
        small[2:3, lanes[0]] += jnp.sum(eq.astype(f32), axis=0, keepdims=True)
        small[3:4, lanes[0]] += jnp.sum(ev.astype(f32), axis=0, keepdims=True)

    sent_e.wait()
    load_sides(5)
    load_sides(6)
    gradient(5)
    line.until(48)
    gradient(6)
    line.until(52)
    in_weight.wait()

    due_in = line.during(4, 52.0, 1.5)

    @pl.loop(0, 4)
    def _(s):
        due_in(s)
        near = pl.ds(pl.multiple_of(s * quarter, quarter), quarter)
        t_acc[:, near] = mm_nt(e[0], wbuf[0, near, :]) + mm_nt(e[1], wbuf[1, near, :])

    due_out = line.during(seqs, 58.0, 2.5)

    @pl.loop(0, seqs)
    def _(n):
        due_out(n)
        at = pl.ds(pl.multiple_of(n * rows, 16), rows)
        normal, inverse = layer_stats(x[at, :].astype(f32))
        t = t_acc[at, :]
        grad = er[at, :] + norm_back(t, normal, inverse, vec[0:1, :])
        small[0:1, :] += jnp.sum(t * normal, axis=0, keepdims=True)
        small[1:2, :] += jnp.sum(t, axis=0, keepdims=True)
        write = pltpu.make_async_copy(stage, out.at[n], stage_sem)

        @pl.when(n > 0)
        def _():
            write.wait()

        stage[0:buf, :] = grad[0:buf]
        pick = picker(keep[n], rows - buf)
        rest = grad[buf:]
        top = rest.astype(bf16)
        rest = rest - top.astype(f32)
        middle = rest.astype(bf16)
        bottom = (rest - middle.astype(f32)).astype(bf16)
        stage[buf:, :] = mm_tn(pick, top) + mm_tn(pick, middle) + mm_tn(pick, bottom)
        write.start()

    pltpu.make_async_copy(stage, out.at[0], stage_sem).wait()

    small[4:12, :] = sums_feed[4:12, :]
    kept = counts[0]
    for n in range(1, seqs):
        kept = kept + counts[n]
    lane = lax.broadcasted_iota(jnp.int32, (1, d), 1)
    tally = jnp.where(lane == 3, kept.astype(f32), 0.0)
    for k, row in enumerate((stats[0:1, :], stats[1:2, :], sums_feed[12:13, :])):
        tally = tally + jnp.where(lane == k, jnp.sum(row, axis=1, keepdims=True), 0.0)
    small[12:13, :] = tally
    hops = [place.to_first, place.to_second] + [place.to_bit(b) for b in (1, 2, *bits)]
    small_in[0, 0] = small[...]

    def hop(k):
        return pltpu.make_async_remote_copy(
            src_ref=small_in.at[k, 0], dst_ref=small_in.at[k, 1], send_sem=small_send.at[k], recv_sem=small_recv.at[k],
            device_id=hops[k], device_id_type=MESH,
        )

    def small_step(k):
        if k > 0:
            hop(k - 1).wait()
            value = small_in[k - 1, 0] + small_in[k - 1, 1]
            if k == len(hops):
                small[...] = value
                return
            small_in[k, 0] = value
        hop(k).start()

    for k in range(len(hops) + 1):
        line.add(68.0 + 6 * k, functools.partial(small_step, k))
    line.until(1e9)


def adam_math(w, f, s, grad, rate, decay):
    first_new = beta_first * f + (1.0 - beta_first) * grad
    second_new = beta_second * s + (1.0 - beta_second) * grad * grad
    fix_first = 1.0 - beta_first**STEP
    fix_second = 1.0 - beta_second**STEP
    update = first_new / fix_first / (jnp.sqrt(second_new / fix_second) + adam_epsilon)
    return w - rate * (update + decay * w), first_new, second_new


def adam_kernel(w, f, s, grad, *rest):
    w_out, f_out, s_out, low_out = rest[-4:]
    new, first, second = adam_math(w[...], f[...], s[...], grad[0].astype(f32), rate_matrix, weight_decay)
    w_out[...] = new
    f_out[...] = first
    s_out[...] = second
    low_out[...] = new.astype(bf16)


def adam_call(state, grad, grid, block, place, grad_place, previous=None):
    spec = pl.BlockSpec(block, place)
    shape = state[0].shape
    extra = [] if previous is None else list(previous)
    size = grid[0] * grid[1] * block[0] * block[1]
    return pl.pallas_call(
        adam_kernel,
        grid=grid,
        in_specs=[spec] * 3 + [pl.BlockSpec((1, *block), grad_place)] + [ANY_SPEC] * len(extra),
        out_specs=[spec] * 4,
        out_shape=[sds(shape, f32)] * 3 + [sds(shape, bf16)],
        input_output_aliases={4 + k: k for k in range(len(extra))},
        compiler_params=params(40),
        cost_estimate=cost(20 * size, 28 * size),
    )(*state, grad, *extra)


def local(groups, replicas, *args):
    tokens, keep, cot, mats, down, vectors, f_mats, f_down, f_vectors, s_mats, s_down, s_vectors = args
    seqs, length, d = tokens.shape
    image = keep.shape[1]
    buf = length - image
    rows = -(-(buf + KEEP_MAX) // 16) * 16
    total = seqs * rows
    half = d // 2
    group = lax.axis_index("group")
    counts = (buf + jnp.sum(keep, axis=1)).astype(jnp.int32)

    keep3 = keep.reshape(seqs, 1, image)
    deep = mats.shape[0]
    w_attn, w_up, w_down, x, em, h1, vec, qkv, o, r, h2, stats = pl.pallas_call(
        functools.partial(attend_kernel, seqs, buf),
        in_specs=[SMEM_SPEC] + [VMEM_SPEC] * 2 + [ANY_SPEC] * 4,
        out_specs=[ANY_SPEC] * 3 + [VMEM_SPEC] * 9,
        out_shape=[
            sds((2, d, 2 * d), bf16),
            sds((2, d, 2 * d), bf16),
            sds((2, 2 * d, d), bf16),
            sds((total, d), bf16),
            sds((total, d), bf16),
            sds((total, d), bf16),
            sds((16, d), f32),
            sds((total, 3 * d), bf16),
            sds((total, d), bf16),
            sds((total, d), f32),
            sds((total, d), bf16),
            sds((8, d), f32),
        ],
        scratch_shapes=[
            pltpu.VMEM((2, d, 2 * d), bf16),
            pltpu.VMEM((2, deep, 2 * d), f32),
            pltpu.VMEM((half, d), f32),
            pltpu.VMEM((deep, 2 * d), bf16),
            pltpu.VMEM((half, d), bf16),
            pltpu.VMEM((2, seqs, length, d), bf16),
            pltpu.VMEM((4, 16, d // 4), bf16),
            pltpu.SemaphoreType.DMA((3, 10)),
            pltpu.SemaphoreType.DMA((3, 10)),
            pltpu.SemaphoreType.DMA((3,)),
            pltpu.SemaphoreType.DMA((3,)),
            pltpu.SemaphoreType.DMA((9,)),
            pltpu.SemaphoreType.DMA((3,)),
            pltpu.SemaphoreType.DMA((2, seqs)),
        ],
        compiler_params=params(60, collective_id=0, has_side_effects=True),
        cost_estimate=cost(2 * total * 4 * d * d * 4, 20 * total * d),
    )(counts, keep3, vectors, mats, down, tokens, cot)
    z_mine, u_mine, er, ea, block_output, sums_feed, h2_got, em_got, z_got, u_got = pl.pallas_call(
        functools.partial(feed_kernel, seqs, buf),
        in_specs=[SMEM_SPEC] + [VMEM_SPEC] * 5 + [ANY_SPEC] * 4,
        out_specs=[VMEM_SPEC] * 6 + [ANY_SPEC] * 4,
        out_shape=[
            sds((2, total, d), bf16),
            sds((total, 2 * d), bf16),
            sds((total, d), f32),
            sds((total, d), bf16),
            sds((seqs, length, d), bf16),
            sds((16, d), f32),
            sds((total, d), bf16),
            sds((total, d), bf16),
            sds((2, total, d), bf16),
            sds((total, 2 * d), bf16),
        ],
        scratch_shapes=[
            pltpu.VMEM((2, d, 2 * d), bf16),
            pltpu.VMEM((2, 2 * d, d), bf16),
            pltpu.VMEM((total, d), f32),
            pltpu.VMEM((total, d), f32),
            pltpu.VMEM((2, total, d), bf16),
            pltpu.VMEM((total, 2 * d), bf16),
            pltpu.SemaphoreType.DMA((2, 2)),
            pltpu.SemaphoreType.DMA((4,)),
            pltpu.SemaphoreType.DMA((4,)),
        ],
        compiler_params=params(60, collective_id=1, has_side_effects=True),
        cost_estimate=cost(2 * total * 16 * d * d, 60 * total * d),
    )(counts, keep3, h2, em, r, vec, h2, em, w_up, w_down)

    bits = []
    while (4 << len(bits)) < replicas:
        bits.append(4 << len(bits))
    sizes = (d, d, d, d, half, d, half)
    chunks, steps = len(sizes), 7 + len(bits)
    quarter = d // 4
    found = pl.pallas_call(
        functools.partial(tail_kernel, seqs, buf, tuple(bits), sizes),
        in_specs=[SMEM_SPEC] + [VMEM_SPEC] * 7 + [ANY_SPEC] * 12,
        out_specs=[VMEM_SPEC, ANY_SPEC] + [ANY_SPEC] * (chunks + 4),
        out_shape=[sds((16, d), f32), sds((seqs, length, d), f32)]
        + [sds((2, quarter, wide), bf16) for wide in sizes]
        + [sds((total, d), bf16)] * 3
        + [sds((total, 3 * half), bf16)],
        scratch_shapes=[
            pltpu.VMEM((2, d, 3 * half), bf16),
            pltpu.VMEM((total, d), bf16),
            pltpu.VMEM((2, total, 3 * half), bf16),
            pltpu.VMEM((total, d), f32),
            pltpu.VMEM((length, d), f32),
            pltpu.VMEM((2, 2, 2 * total, d), bf16),
            pltpu.VMEM((4 + len(bits), 2, 16, d), f32),
        ]
        + [pltpu.VMEM((4, quarter, wide), bf16) for wide in sizes]
        + [pltpu.VMEM((2, quarter, wide), bf16) for wide in sizes]
        + [pltpu.VMEM((quarter, wide), bf16) for wide in sizes]
        + [pltpu.VMEM((quarter // 2, wide), bf16) for wide in sizes]
        + [pltpu.VMEM((len(bits), quarter // 2, wide), bf16) for wide in sizes]
        + [
            pltpu.SemaphoreType.DMA((chunks, steps + 1)),
            pltpu.SemaphoreType.DMA((chunks, steps)),
            pltpu.SemaphoreType.DMA(()),
            pltpu.SemaphoreType.DMA(()),
            pltpu.SemaphoreType.DMA((2, 2, 2)),
            pltpu.SemaphoreType.DMA(()),
            pltpu.SemaphoreType.DMA((4,)),
            pltpu.SemaphoreType.DMA((4,)),
            pltpu.SemaphoreType.DMA((4 + len(bits),)),
            pltpu.SemaphoreType.DMA((4 + len(bits),)),
        ],
        compiler_params=params(61, collective_id=2, has_side_effects=True),
        cost_estimate=cost(2 * total * 16 * d * d, 100 * total * d),
    )(counts, keep3, qkv, x, er, vec, stats, sums_feed, z_mine, z_got, em, em_got, h2, h2_got, u_mine, u_got, o, ea, h1, w_attn)
    small, input_grad = found[:2]
    grads = found[2 : 2 + chunks]
    branch_rms = jnp.sqrt(small[12, 0:3] / (small[12, 3] * d))
    part = vectors.shape[1]
    grad_vectors = lax.dynamic_slice(small, (0, group * part), (12, part))

    new_down = None
    for k in range(2):
        new_down = adam_call(
            (down, f_down, s_down),
            grads[k],
            (2, 2),
            (quarter, half),
            lambda h, j, k=k: (2 * h + k, j),
            lambda h, j: (h, 0, j),
            new_down,
        )
    new_mats = None
    for k, first_strip in ((2, 4), (3, 6), (4, 3), (5, 0), (6, 2)):
        new_mats = adam_call(
            (mats, f_mats, s_mats),
            grads[k],
            (2, sizes[k] // half),
            (quarter, half),
            lambda h, j, at=first_strip: (0, 2 * (at + j) + h),
            lambda h, j: (h, 0, j),
            new_mats,
        )
    new_vectors, first_vectors, second_vectors = adam_math(
        vectors, f_vectors, s_vectors, grad_vectors, rate_vector, 0.0
    )
    return (
        block_output,
        input_grad,
        new_mats[0],
        new_down[0],
        new_vectors,
        new_mats[1],
        new_down[1],
        first_vectors,
        new_mats[2],
        new_down[2],
        second_vectors,
        new_mats[3],
        new_down[3],
        new_vectors.astype(bf16),
        branch_rms,
    )


def solution(mesh):
    rows, owned, columns = P(BOTH, None, None), P("group", None), P(None, "group")
    state = (owned, owned, columns)
    return jax.shard_map(
        functools.partial(local, mesh.shape["group"], mesh.shape["dp"]),
        mesh=mesh,
        in_specs=(rows, P(BOTH, None), rows) + state * 3,
        out_specs=(rows, rows) + state * 4 + (P(),),
        check_vma=False,
    )
```

```python
import functools
import math

import jax
import jax.numpy as jnp
from jax import lax
from jax.experimental import pallas as pl
from jax.experimental.pallas import tpu as pltpu
from jax.sharding import PartitionSpec as P

HEAD = 64
STEP = 7
KEEP_MAX = 77

norm_epsilon = 1e-06
beta_first = 0.5
beta_second = 0.5
adam_epsilon = 1e-08
rate_matrix = 0.05
rate_vector = 0.3
weight_decay = 0.05
root_half = 0.7071067811865476
inverse_root_two_pi = 0.3989422804014327

bf16 = jnp.bfloat16
f32 = jnp.float32
BOTH = ("group", "dp")
VMEM_SPEC = pl.BlockSpec(memory_space=pltpu.VMEM)
SMEM_SPEC = pl.BlockSpec(memory_space=pltpu.SMEM)
ANY_SPEC = pl.BlockSpec(memory_space=pl.ANY)
MIB = 1 << 20


def mm(a, b):
    return jnp.dot(a, b, preferred_element_type=f32)


def mm_nt(a, b):
    return lax.dot_general(a, b, (((1,), (1,)), ((), ())), preferred_element_type=f32)


def mm_tn(a, b):
    return lax.dot_general(a, b, (((0,), (0,)), ((), ())), preferred_element_type=f32)


def sds(shape, dtype):
    return jax.ShapeDtypeStruct(shape, dtype)


def params(mib, **more):
    return pltpu.CompilerParams(vmem_limit_bytes=mib * MIB, **more)


def cost(flops, nbytes):
    return pl.CostEstimate(flops=int(flops), bytes_accessed=int(nbytes), transcendentals=0)


def layer_stats(values):
    centre = jnp.mean(values, axis=-1, keepdims=True)
    centred = values - centre
    variance = jnp.mean(centred * centred, axis=-1, keepdims=True)
    inverse = lax.rsqrt(variance + norm_epsilon)
    return centred * inverse, inverse


def norm_back(grad_normed, normal, inverse, gain):
    scaled = grad_normed * gain
    mean_one = jnp.mean(scaled, axis=-1, keepdims=True)
    mean_two = jnp.mean(scaled * normal, axis=-1, keepdims=True)
    return inverse * (scaled - mean_one - normal * mean_two)


def picker(keep_row, rows):
    image = keep_row.shape[1]
    ahead = lax.broadcasted_iota(jnp.int32, (image, image), 0)
    here = lax.broadcasted_iota(jnp.int32, (image, image), 1)
    upper = jnp.where(ahead <= here, 1.0, 0.0).astype(bf16)
    kept = keep_row.astype(f32)
    place = mm(kept.astype(bf16), upper) - 1.0
    place = jnp.where(kept > 0.5, place, -1.0)
    want = lax.broadcasted_iota(jnp.int32, (rows, image), 0).astype(f32)
    return jnp.where(place == want, 1.0, 0.0).astype(bf16)


MESH = pl.DeviceIdType.MESH


def flip(value, bit):
    return value + bit - 2 * bit * ((value // bit) % 2)


class Place:
    def __init__(self):
        self.group, self.replica = lax.axis_index("group"), lax.axis_index("dp")
        self.core, self.level = self.replica % 2, (self.replica // 2) % 2
        one, two = flip(self.group, 1), flip(self.group, 2)
        self.first = (1 - self.core) * one + self.core * two
        self.second = (1 - self.core) * two + self.core * one
        self.third = flip(one, 2)
        self.to_first = (self.first, self.replica)
        self.to_second = (self.second, self.replica)
        self.to_third = (self.third, self.replica)
        self.to_core = (self.group, flip(self.replica, 1))

    def to_bit(self, bit):
        return (self.group, flip(self.replica, bit))

    def meet(self, partners):
        barrier = pltpu.get_barrier_semaphore()
        for partner in partners:
            pl.semaphore_signal(barrier, inc=1, device_id=partner, device_id_type=MESH)
        pl.semaphore_wait(barrier, len(partners))


class Timeline:
    def __init__(self):
        self.steps = []

    def add(self, when, step):
        self.steps.append((when, len(self.steps), step))
        self.steps.sort(key=lambda one: one[:2])

    def until(self, when):
        while self.steps and self.steps[0][0] <= when:
            self.steps.pop(0)[2]()

    def during(self, count, start, gap):
        due = []
        while self.steps and self.steps[0][0] < start + count * gap:
            when, _, step = self.steps.pop(0)
            due.append((min(max(int((when - start) / gap), 0), count - 1), step))

        def run(turn):
            for at, step in due:
                pl.when(turn == at)(step)

        return run


class Gather:
    def __init__(self, place, own, full, cols, send, recv):
        self.place, self.own, self.full, self.cols, self.send, self.recv = place, own, full, cols, send, recv
        deep = own.shape[0]
        self.deep, self.strip = deep, 5 * deep // 16
        self.main = deep - self.strip
        self.main_at = place.level * self.strip
        self.strip_at = place.level * self.main

    def block(self, owner, start, size, core=None):
        at = pl.multiple_of(owner * self.deep + start, 16)
        return self.full.at[self.place.core if core is None else core, pl.ds(at, size), self.cols]

    def whole(self, owner, core=None):
        return self.block(owner, 0, self.deep, core)

    def copy(self, k):
        p = self.place
        main, strip, whole = (self.main_at, self.main), (self.strip_at, self.strip), (0, self.deep)
        owner, (at, size), device = (
            (p.group, main, p.to_first),
            (p.group, main, p.to_second),
            (p.first, main, p.to_second),
            (p.first, strip, p.to_bit(2)),
            (p.second, strip, p.to_bit(2)),
            (p.third, strip, p.to_bit(2)),
            (p.group, whole, p.to_core),
            (p.first, whole, p.to_core),
            (p.second, whole, p.to_core),
            (p.third, whole, p.to_core),
        )[k]
        dst = self.block(owner, at, size)
        src = dst
        if k in (0, 1, 6):
            src = self.own.at[pl.ds(pl.multiple_of(at, 16) if k < 6 else 0, size), :]
        return pltpu.make_async_remote_copy(
            src_ref=src, dst_ref=dst, send_sem=self.send.at[k], recv_sem=self.recv.at[k],
            device_id=device, device_id_type=MESH,
        )

    def start(self, *ks):
        for k in ks:
            self.copy(k).start()

    def arrived(self, *ks):
        for k in ks:
            self.copy(k).wait_recv()

    def sent(self, *ks):
        for k in ks:
            self.copy(k).wait_send()

    def step_one(self):
        self.start(0, 1, 6)

    def step_two(self):
        self.arrived(0)
        self.start(2, 3)
        self.arrived(1)
        self.start(4)

    def step_near(self):
        self.arrived(3)
        self.start(7)
        self.arrived(4)
        self.start(8)

    def step_third(self):
        self.arrived(2)
        self.start(5)

    def step_four(self):
        self.arrived(5)
        self.start(9)

    def step_five(self):
        self.arrived(6, 7, 8, 9)
        self.sent(*range(10))

    def schedule(self, line, start, size):
        line.add(start, self.step_one)
        line.add(start + 8 * size + 2, self.step_two)
        line.add(start + 12 * size + 4, self.step_third)
        line.add(start + 14 * size + 4.5, self.step_near)
        line.add(start + 16 * size + 6, self.step_four)
        line.add(start + 17 * size + 8, self.step_five)


def head_masks():
    lane = lax.broadcasted_iota(jnp.int32, (1, 2 * HEAD), 1)
    low = jnp.where(lane < HEAD, 1.0, 0.0)
    return low.astype(bf16), (1.0 - low).astype(bf16), low > 0.5


def two_heads(x, low, high):
    return jnp.concatenate([x * low, x * high], axis=0)


def pick_heads(both, first):
    rows = both.shape[0] // 2
    return jnp.where(first, both[:rows], both[rows:])


def pair_probs(q_pair, k_pair, count):
    raw = mm_nt(q_pair, k_pair) * (1.0 / math.sqrt(HEAD))
    col = lax.broadcasted_iota(jnp.int32, raw.shape, 1)
    raw = jnp.where(col < count, raw, -1e30)
    top = jnp.max(raw, axis=-1, keepdims=True)
    exponent = jnp.exp(raw - top)
    return exponent / jnp.sum(exponent, axis=-1, keepdims=True)


def attend_kernel(seqs, buf, *refs):
    counts, keep, vectors, mats, down, tokens, cot = refs[:7]
    w_attn, w_up, w_down, own_down, x_out, em_out, h1_out, qkv_out, o_out, r_out, h2_out, vec, stats = refs[7:20]
    x, em, h1, qkv, o, r, h2, outs, wbuf, wide, tall, low_up, low_down, rows_in, parts, send, recv, vec_send, vec_recv, loads, stores, reads = refs[20:]
    rows = h1.shape[0] // seqs
    d = h1.shape[1]
    half = d // 2
    place = Place()
    core = place.core
    deep = mats.shape[0]

    takes = []
    for j in range(8):
        at = pl.ds(pl.multiple_of((2 * j + core) * half, half), half)
        takes.append(
            pltpu.make_async_copy(mats.at[:, at], wide.at[j // 4, :, pl.ds((j % 4) * half, half)], loads.at[j])
        )
    takes.append(
        pltpu.make_async_copy(down.at[pl.ds(pl.multiple_of(core * half, half), half), :], tall, loads.at[8])
    )
    for one in takes:
        one.start()
    reads_in = []
    for n in range(seqs):
        for k, src in enumerate((tokens, cot)):
            reads_in.append(pltpu.make_async_copy(src.at[n], rows_in.at[k, n], reads.at[k, n]))
    for one in reads_in:
        one.start()

    place.meet((place.to_first, place.to_second, place.to_third, place.to_core, place.to_bit(2)))

    part = vectors.shape[1]
    parts[place.group] = jnp.concatenate([vectors[...], jnp.zeros((4, part), f32)], axis=0).astype(bf16)
    for k, partner in enumerate((place.to_first, place.to_second, place.to_third)):
        pltpu.make_async_remote_copy(
            src_ref=parts.at[place.group], dst_ref=parts.at[place.group],
            send_sem=vec_send.at[k], recv_sem=vec_recv.at[k], device_id=partner, device_id_type=MESH,
        ).start()

    own_rows = pl.ds(pl.multiple_of(place.group * deep, deep), deep)
    line = Timeline()
    attn = []
    for j in range(4):
        cols = pl.ds(j * half, half)
        own = wbuf.at[core, own_rows, cols]
        takes[j].wait()
        own[...] = wide[0, :, cols].astype(bf16)
        attn.append(Gather(place, own, wbuf, cols, send.at[j], recv.at[j]))
        attn[j].schedule(line, 3.0 * j, 0.5)
        if j == 0:
            line.until(0)
    ups = []
    for j in range(2):
        cols = pl.ds(j * d, d)
        for one in takes[4 + 2 * j : 6 + 2 * j]:
            one.wait()
        low_up[j] = wide[1, :, cols].astype(bf16)
        ups.append(Gather(place, low_up.at[j], w_up, cols, send.at[4 + j], recv.at[4 + j]))
        ups[j].schedule(line, 14.0 + 10 * j, 1.0)
    takes[8].wait()
    for j in range(2):
        low_down[j] = tall[j * deep : (j + 1) * deep, :].astype(bf16)
    early = Gather(place, low_down.at[0], w_down, pl.ds(0, d), send.at[6], recv.at[6])
    early.schedule(line, 34.0, 1.0)
    keeps = [
        pltpu.make_async_copy(one.own, one.whole(place.group), stores.at[k]) for k, one in enumerate(ups + [early])
    ]
    keeps.append(pltpu.make_async_copy(low_down.at[1], own_down, stores.at[3]))
    for one in keeps:
        one.start()

    def keep_out(k, src, dst):
        one = pltpu.make_async_copy(src, dst, outs.at[k])
        one.start()
        keeps.append(one)

    for one in reads_in:
        one.wait()
    due_pack = line.during(seqs, 4.0, 1.0)

    @pl.loop(0, seqs)
    def _(n):
        due_pack(n)
        at = pl.multiple_of(n * rows, 16)
        pick = picker(keep[n], rows - buf)
        for k, dst in ((0, x), (1, em)):
            dst[pl.ds(at, buf), :] = rows_in[k, n, 0:buf, :]
            dst[pl.ds(pl.multiple_of(at + buf, 16), rows - buf), :] = mm(pick, rows_in[k, n, buf:, :]).astype(bf16)

    for k in range(3):
        pltpu.make_async_remote_copy(
            src_ref=parts.at[place.group], dst_ref=parts.at[place.group],
            send_sem=vec_send.at[k], recv_sem=vec_recv.at[k], device_id=place.to_first, device_id_type=MESH,
        ).wait()
    vec[...] = jnp.zeros_like(vec)
    for s in range(4):
        vec[:, s * part : (s + 1) * part] = parts[s].astype(f32)
    due_norm = line.during(seqs, 8.0, 0.7)

    @pl.loop(0, seqs)
    def _(n):
        due_norm(n)
        at = pl.ds(pl.multiple_of(n * rows, 16), rows)
        normal, _ = layer_stats(x[at, :].astype(f32))
        h1[at, :] = (normal * vec[0:1, :] + vec[1:2, :]).astype(bf16)

    keep_out(0, x, x_out)
    keep_out(1, em, em_out)
    keep_out(2, h1, h1_out)
    tile = half // 2
    for j in range(3):
        line.until(3.0 * j + 17 * 0.5 + 8)

        @pl.loop(0, 4)
        def _(i):
            h, t = i // 2, i % 2
            near = pl.multiple_of(i * tile, tile)
            w = wbuf[h, :, pl.ds(pl.multiple_of(j * half + t * tile, tile), tile)]
            got = mm(h1[...], w)
            if j != 1:
                got = got + vec[2 + j // 2 : 3 + j // 2, pl.ds(near, tile)]
            qkv[:, pl.ds(pl.multiple_of(j * d + near, tile), tile)] = got.astype(bf16)

    keep_out(3, qkv, qkv_out)
    low, high, first = head_masks()
    pairs = d // (2 * HEAD)
    due = line.during(seqs * pairs, 23.5, 0.6)

    @pl.loop(0, seqs * pairs)
    def _(i):
        due(i)
        n, j = i // pairs, i % pairs
        at = pl.ds(pl.multiple_of(n * rows, 16), rows)
        lanes = [pl.ds(pl.multiple_of(j * 2 * HEAD + m * d, 2 * HEAD), 2 * HEAD) for m in range(3)]
        q_pair = two_heads(qkv[at, lanes[0]], low, high)
        probs = pair_probs(q_pair, qkv[at, lanes[1]], counts[n]).astype(bf16)
        o[at, lanes[0]] = pick_heads(mm(probs, qkv[at, lanes[2]]), first).astype(bf16)

    keep_attn = pltpu.make_async_copy(wbuf, w_attn, stores.at[4])
    keep_attn.start()
    keep_out(4, o, o_out)
    due_mix = line.during(4, 43.0, 1.0)

    @pl.loop(0, 4)
    def _(i):
        due_mix(i)
        h, t = i // 2, i % 2
        near = pl.ds(pl.multiple_of(i * tile, tile), tile)
        w = wbuf[h, :, pl.ds(pl.multiple_of(3 * half + t * tile, tile), tile)]
        r[:, near] = mm(o[...], w) + vec[4:5, near]

    due_last = line.during(seqs, 47.0, 1.5)
    stats[...] = jnp.zeros_like(stats)

    @pl.loop(0, seqs)
    def _(n):
        due_last(n)
        at = pl.ds(pl.multiple_of(n * rows, 16), rows)
        valid = lax.broadcasted_iota(jnp.int32, (rows, 1), 0) < counts[n]
        valid = jnp.where(valid, 1.0, 0.0)
        inputs = x[at, :].astype(f32)
        branch = r[at, :]
        resid = inputs + branch
        r[at, :] = resid
        normal, _ = layer_stats(resid)
        h2[at, :] = (normal * vec[5:6, :] + vec[6:7, :]).astype(bf16)
        stats[0:1, :] += jnp.sum(inputs * inputs * valid, axis=0, keepdims=True)
        stats[1:2, :] += jnp.sum(branch * branch * valid, axis=0, keepdims=True)

    keep_out(5, r, r_out)
    keep_out(6, h2, h2_out)
    line.until(1e9)
    for one in keeps:
        one.wait()
    keep_attn.wait()


class Reduce:
    def __init__(self, place, bits, g, r1, r2, r3, r4, total, send, recv):
        self.place, self.bits, self.g, self.r1, self.r2, self.r3, self.r4 = place, bits, g, r1, r2, r3, r4
        self.total, self.send, self.recv = total, send, recv
        self.half = g.shape[1] // 2
        self.hold = r2.at[pl.ds(0, self.half)]
        self.slots = [r1.at[n // 2 % 2, pl.ds(n % 2 * self.half, self.half)] for n in range(len(bits))]

    def copy(self, k):
        p = self.place
        half = self.half
        mine, other = p.level * half, (1 - p.level) * half
        at = lambda start: pl.ds(pl.multiple_of(start, 16), half)
        plans = [
            lambda: (self.g.at[p.third], self.r1.at[1], p.to_first),
            lambda: (self.g.at[p.first], self.r1.at[0], p.to_first),
            lambda: (self.g.at[p.second], self.r2, p.to_second),
            lambda: (self.g.at[p.group, at(other)], self.r3, p.to_bit(2)),
            lambda: (self.hold, self.total.at[p.core, at(mine)], p.to_bit(2)),
            lambda: (self.hold, self.total.at[p.core, at(mine)], p.to_core),
            lambda: (self.total.at[p.core, at(other)], self.total.at[p.core, at(other)], p.to_core),
        ]
        for n, bit in enumerate(self.bits):
            plans.append(lambda n=n, bit=bit: (self.slots[n], self.r4.at[n], p.to_bit(bit)))
        src, dst, device = plans[k]()
        return pltpu.make_async_remote_copy(
            src_ref=src, dst_ref=dst, send_sem=self.send.at[k], recv_sem=self.recv.at[k],
            device_id=device, device_id_type=MESH,
        )

    def begin(self):
        self.copy(0).start()
        self.copy(1).start()

    def sent(self, *ks):
        for k in ks:
            self.copy(k).wait_send()

    def pass_second(self):
        self.copy(0).wait_recv()
        at = self.place.second
        self.g[at] = (self.g[at].astype(f32) + self.r1[1].astype(f32)).astype(bf16)
        self.copy(2).start()

    def settle(self):
        self.copy(1).wait_recv()
        self.copy(2).wait_recv()
        at = self.place.group
        self.g[at] = (self.g[at].astype(f32) + self.r1[0].astype(f32) + self.r2[...].astype(f32)).astype(bf16)

    def pass_replica(self):
        self.settle()
        self.copy(3).start()

    def pass_bit(self, n):
        p = self.place
        if n == 0:
            self.copy(3).wait_recv()
            at = pl.ds(pl.multiple_of(p.level * self.half, 16), self.half)
            value = self.g[p.group, at].astype(f32) + self.r3[...].astype(f32)
        else:
            self.copy(6 + n).wait_recv()
            value = self.slots[n - 1][...].astype(f32) + self.r4[n - 1].astype(f32)
        if n < len(self.bits):
            self.slots[n][...] = value.astype(bf16)
            self.copy(7 + n).start()
        else:
            self.hold[...] = value.astype(bf16)
            self.copy(4).start()
            self.copy(5).start()
            self.stay().start()

    def stay(self):
        p = self.place
        at = pl.ds(pl.multiple_of(p.level * self.half, 16), self.half)
        return pltpu.make_async_copy(self.hold, self.total.at[p.core, at], self.send.at[7 + len(self.bits)])

    def pass_core(self):
        self.copy(4).wait_recv()
        self.copy(6).start()

    def finish(self, start=0):
        self.copy(5).wait_recv()
        self.copy(6).wait_recv()
        self.sent(*range(start, 7 + len(self.bits)))
        self.stay().wait()


def block_grads(place, sides, wide, g):
    quarter = sides.shape[2] // 4

    @pl.loop(0, 4)
    def _(i):
        near = place.first * (1 - i // 2) + place.group * (i // 2)
        over = ((i + 1) // 2) % 2
        owner = near * (1 - over) + ((1 - place.core) * flip(near, 2) + place.core * flip(near, 1)) * over
        cols = pl.ds(pl.multiple_of(owner * quarter, quarter), quarter)
        g[owner] = mm_tn(sides[0, :, cols], sides[1, :, 0:wide]).astype(bf16)


def swap_start(place, src, dst, send, recv, k):
    copy = pltpu.make_async_remote_copy(
        src_ref=src, dst_ref=dst, send_sem=send.at[k], recv_sem=recv.at[k],
        device_id=place.to_core, device_id_type=MESH,
    )
    copy.start()
    return copy


def feed_kernel(seqs, buf, *refs):
    counts, keep, h2, em, r, vec, h2_hbm, em_hbm, ups, downs, own_down = refs[:11]
    er, ea, out, sums, part_sum, z_mine, z_got, u_mine, u_got, h2_got, em_got = refs[11:22]
    wup, wdown, m_acc, t_acc, z_all, u_all, sides, g, r1, r2 = refs[22:32]
    sems, send, recv, g_send, g_recv, k_sems, t_send, t_recv, r_send, r_recv = refs[32:]
    total, d = h2.shape
    rows = total // seqs
    strip = wup.shape[2] // 4
    tile = strip // 2
    place = Place()
    core = place.core
    late = Gather(place, wdown.at[1, core, pl.ds(pl.multiple_of(place.group * tile, tile), tile)], wdown.at[1], pl.ds(0, d), g_send, g_recv)
    take_own = pltpu.make_async_copy(own_down, late.own, sems.at[0])
    take_own.start()
    takes = [pltpu.make_async_copy(downs, wdown.at[0], sems.at[1])]
    takes += [pltpu.make_async_copy(ups.at[h], wup.at[h], sems.at[2 + h]) for h in range(2)]
    for one in takes:
        one.start()
    place.meet((place.to_core, place.to_second, place.to_first, place.to_bit(2)))
    take_own.wait()
    late.step_one()
    swaps = [
        swap_start(place, em_hbm, em_got, send, recv, 0),
        swap_start(place, h2_hbm, h2_got, send, recv, 1),
    ]
    reduce = Reduce(place, (), g, r1, r2, None, None, None, r_send, r_recv)
    sides[1, 0:total, :] = em[...]
    take_em = pltpu.make_async_copy(em_got, sides.at[1, pl.ds(total, total)], sems.at[4])
    sums[...] = jnp.zeros_like(sums)
    m_acc[...] = jnp.zeros_like(m_acc)
    t_acc[...] = jnp.zeros_like(t_acc)
    for one in takes:
        one.wait()

    def tile_copies(k, s, t, away):
        cols = pl.ds(pl.multiple_of(s * tile, tile), tile)
        z_to = sides.at[0, pl.ds(0 if not away else total, total), cols] if t == 0 else (z_got if away else z_mine).at[:, cols]
        pairs = (
            (z_all.at[(1 - core) if away else core, t, :, cols], z_to),
            (u_all.at[(1 - core) if away else core, t, :, cols], (u_got if away else u_mine).at[t, :, cols]),
        )
        if not away:
            return [pltpu.make_async_copy(src, dst, k_sems.at[k, n]) for n, (src, dst) in enumerate(pairs)]
        return [
            pltpu.make_async_remote_copy(
                src_ref=src, dst_ref=dst, send_sem=t_send.at[k, n], recv_sem=t_recv.at[k, n],
                device_id=place.to_core, device_id_type=MESH,
            )
            for n, (src, dst) in enumerate(pairs)
        ]

    def late_last():
        late.arrived(6, 7, 8, 9)
        late.sent(*range(10))

    def begin():
        take_em.wait()
        for k in range(4):
            tile_copies(k, 0, 0, False)[0].wait()
            tile_copies(k, 0, 0, True)[0].wait()
        block_grads(place, sides, d, g)
        reduce.begin()

    steps = ({2: swaps[0].wait, 3: late.step_two, 4: late.step_third, 5: late.step_near, 6: late.step_four, 7: late_last},
             {0: begin, 4: reduce.pass_second, 7: reduce.settle})

    for t in range(2):

        @pl.loop(0, 8)
        def _(i):
            for when, step in steps[t].items():
                pl.when(i == when)(step)
            if t == 0:
                pl.when(i == 2)(take_em.start)
            turn, away = i // 2, i % 2
            h = (1 - core) * away + core * (1 - away)
            near = place.group * (1 - turn % 2) + place.first * (turn % 2)
            over = turn // 2
            s = near * (1 - over) + ((1 - core) * flip(near, 2) + core * flip(near, 1)) * over
            cols = pl.ds(pl.multiple_of(s * strip + t * tile, tile), tile)
            far = (pl.ds(8 + s, 1), pl.ds(pl.multiple_of(h * strip + t * tile, tile), tile))
            near = pl.ds(pl.multiple_of(s * tile, tile), tile)
            w_up = wup[h, :, cols]
            w_down = wdown[t, h, near, :]
            u = mm(h2[...], w_up) + vec[far]
            phi = 0.5 * (1.0 + lax.erf(u * root_half))
            z = (u * phi).astype(bf16)
            z_all[h, t, :, near] = z
            slope = phi + u * jnp.exp(-0.5 * u * u) * inverse_root_two_pi
            eu = (mm_nt(em[...], w_down) * slope).astype(bf16)
            u_all[h, t, :, near] = eu
            m_acc[...] += mm(z, w_down)
            t_acc[...] += mm_nt(eu, w_up)
            sums[far] = jnp.sum(eu.astype(f32), axis=0, keepdims=True)
            for side in range(2):

                @pl.when(away == side)
                def _():
                    for one in tile_copies(4 * t + turn, s, t, side == 1):
                        one.start()

    share = pltpu.make_async_copy(g.at[place.group], part_sum, sems.at[0])
    share.start()

    @pl.loop(0, seqs)
    def _(n):
        at = pl.ds(pl.multiple_of(n * rows, 16), rows)
        valid = lax.broadcasted_iota(jnp.int32, (rows, 1), 0) < counts[n]
        valid = jnp.where(valid, 1.0, 0.0)
        resid = r[at, :]
        m = m_acc[at, :] + vec[7:8, :]
        packed = ((resid + m) * valid).astype(bf16)
        out[n, 0:buf, :] = packed[0:buf]
        pick = picker(keep[n], rows - buf)
        out[n, buf:, :] = mm_tn(pick, packed[buf:]).astype(bf16)
        normal, inverse = layer_stats(resid)
        t = t_acc[at, :]
        low = em[at, :].astype(f32)
        back = low + norm_back(t, normal, inverse, vec[5:6, :])
        er[at, :] = back
        ea_low = back.astype(bf16)
        ea[at, :] = ea_low
        sums[4:5, :] += jnp.sum(ea_low.astype(f32), axis=0, keepdims=True)
        sums[5:6, :] += jnp.sum(t * normal, axis=0, keepdims=True)
        sums[6:7, :] += jnp.sum(t, axis=0, keepdims=True)
        sums[7:8, :] += jnp.sum(low, axis=0, keepdims=True)
        sums[12:13, :] += jnp.sum(m * m * valid, axis=0, keepdims=True)
    swaps[1].wait()
    reduce.sent(0, 1, 2)
    share.wait()
    for k in range(8):
        for away in (False, True):
            for one in tile_copies(k, 0, k // 4, away)[0 if k >= 4 else 1 :]:
                one.wait()


def tail_kernel(seqs, buf, bits, sizes, *refs):
    counts, keep, qkv, x, er, vec, stats, sums_feed = refs[:8]
    part_sum, z_mine, z_got, em, em_got, h2, h2_got, u_mine, u_got, o, ea, h1, w_attn = refs[8:21]
    chunks = len(sizes)
    small, out = refs[21:23]
    totals = refs[23 : 23 + chunks]
    o_got, ea_got, h1_got, e_got = refs[23 + chunks : 27 + chunks]
    scratch = refs[27 + chunks :]
    wbuf, eo, e, t_acc, stage, sides, small_in = scratch[:7]
    buffers = [scratch[7 + k * chunks : 7 + (k + 1) * chunks] for k in range(5)]
    send, recv, w_sem, ea_sem, first_sem, side_sems, stage_sem, swap_send, swap_recv, small_send, small_recv = scratch[7 + 5 * chunks :]
    total, d = eo.shape
    rows = total // seqs
    half, quarter = d // 2, d // 4
    place = Place()
    core = place.core

    o_weight = pltpu.make_async_copy(w_attn.at[:, :, pl.ds(3 * half, half)], wbuf.at[:, :, pl.ds(0, half)], w_sem)
    o_weight.start()
    ea_all = e.at[0, :, pl.ds(0, d)]
    take_ea = pltpu.make_async_copy(ea, ea_all, ea_sem)
    take_ea.start()

    mine_cols = pl.ds(pl.multiple_of(core * half, half), half)
    left = [None, (z_mine, z_got), (h2, h2_got), (h2, h2_got), (o, o_got), (h1, h1_got), (h1, h1_got)]
    right = [
        None, (em, em_got),
        (u_mine.at[0], u_got.at[0]), (u_mine.at[1], u_got.at[1]),
        (ea.at[:, mine_cols], ea_got.at[:, mine_cols]),
        (e.at[core, :, pl.ds(0, d)], e_got.at[:, pl.ds(0, d)]), (e.at[core, :, pl.ds(d, half)], e_got.at[:, pl.ds(d, half)]),
    ]

    def side_copies(k):
        found = []
        for side, pairs in enumerate((left, right)):
            wide = sizes[k] if side else d
            for which, src in enumerate(pairs[k]):
                dst = sides.at[k % 2, side, pl.ds(which * total, total), pl.ds(0, wide)]
                found.append(pltpu.make_async_copy(src, dst, side_sems.at[k % 2, side, which]))
        return found

    def load_sides(k):
        for one in side_copies(k):
            one.start()

    load_sides(1)
    load_sides(2)
    partners = [place.to_first, place.to_second, place.to_core, place.to_bit(2)] + [place.to_bit(b) for b in bits]
    place.meet(partners)
    swaps = [
        swap_start(place, o, o_got, swap_send, swap_recv, 0),
        swap_start(place, ea, ea_got, swap_send, swap_recv, 1),
        swap_start(place, h1, h1_got, swap_send, swap_recv, 2),
    ]
    sent_e = pltpu.make_async_remote_copy(
        src_ref=e.at[1 - core], dst_ref=e_got, send_sem=swap_send.at[3], recv_sem=swap_recv.at[3],
        device_id=place.to_core, device_id_type=MESH,
    )
    reduces = [
        Reduce(place, bits, *(buffers[b][k] for b in range(5)), totals[k], send.at[k], recv.at[k]) for k in range(chunks)
    ]

    first_sum = pltpu.make_async_copy(part_sum, buffers[0][0].at[place.group], first_sem)
    first_sum.start()

    def gradient(k):
        for one in side_copies(k):
            one.wait()
        block_grads(place, sides.at[k % 2], sizes[k], reduces[k].g)

    line = Timeline()
    start = 3.0
    for k in range(chunks):
        size = sizes[k] / d
        if k == 5:
            start = max(start, 44.0)
        one = reduces[k]
        when = 0.0
        if k:
            line.add(start, one.begin)
            when = start + 9.0 * size + 2
            line.add(when, one.pass_second)
            when = start + 17.0 * size + 3
            line.add(when, one.pass_replica)
            start += 17.0 * size
        when += 7 * size + 2
        for n in range(len(bits) + 1):
            line.add(when, functools.partial(one.pass_bit, n))
            when += 10 * size + 2
        line.add(when, one.pass_core)
        line.add(when + 6 * size + 3, functools.partial(one.finish, 0 if k else 3))

    gradient(1)
    load_sides(3)
    first_sum.wait()
    reduces[0].copy(3).start()
    line.until(3)
    gradient(2)
    for one in swaps[:2]:
        one.wait()
    load_sides(4)
    line.until(6)
    gradient(3)
    line.until(9)
    gradient(4)
    swaps[2].wait()
    line.until(12)
    o_weight.wait()
    take_ea.wait()

    @pl.loop(0, 4)
    def _(s):
        near = pl.ds(pl.multiple_of(s * quarter, quarter), quarter)
        got = mm_nt(ea_all[:, 0:half], wbuf[0, near, 0:half]) + mm_nt(ea_all[:, half:], wbuf[1, near, 0:half])
        eo[:, near] = got.astype(bf16)

    in_weight = pltpu.make_async_copy(w_attn.at[:, :, pl.ds(0, 3 * half)], wbuf, w_sem)
    in_weight.start()
    line.until(15)
    low, high, first = head_masks()
    pairs = half // (2 * HEAD)
    scale = 1.0 / math.sqrt(HEAD)
    small[...] = jnp.zeros_like(small)
    turns = seqs * pairs

    due = line.during(2 * turns, 15.0, 0.7)

    @pl.loop(0, 2 * turns)
    def _(i):
        pl.when(i == turns)(sent_e.start)
        due(i)
        h = (1 - core) * (1 - i // turns) + core * (i // turns)
        n, j = (i % turns) // pairs, i % pairs
        at = pl.ds(pl.multiple_of(n * rows, 16), rows)
        far = h * half + j * 2 * HEAD
        lanes = [pl.ds(pl.multiple_of(far + m * d, 2 * HEAD), 2 * HEAD) for m in range(3)]
        k_pair = qkv[at, lanes[1]]
        q_both = two_heads(qkv[at, lanes[0]], low, high)
        probs = pair_probs(q_both, k_pair, counts[n])
        eo_both = two_heads(eo[at, lanes[0]], low, high)
        ep = mm_nt(eo_both, qkv[at, lanes[2]])
        inner = jnp.sum(probs * ep, axis=-1, keepdims=True)
        es = (probs * (ep - inner)).astype(bf16)
        ev = mm_tn(probs.astype(bf16), eo_both).astype(bf16)
        eq = (pick_heads(mm(es, k_pair), first) * scale).astype(bf16)
        ek = (mm_tn(es, q_both) * scale).astype(bf16)
        for m, value in enumerate((eq, ek, ev)):
            e[h, at, pl.ds(pl.multiple_of(m * half + j * 2 * HEAD, 2 * HEAD), 2 * HEAD)] = value
        small[2:3, lanes[0]] += jnp.sum(eq.astype(f32), axis=0, keepdims=True)
        small[3:4, lanes[0]] += jnp.sum(ev.astype(f32), axis=0, keepdims=True)

    sent_e.wait()
    load_sides(5)
    load_sides(6)
    gradient(5)
    line.until(42)
    gradient(6)
    line.until(45)
    in_weight.wait()

    due_in = line.during(4, 45.0, 1.2)

    @pl.loop(0, 4)
    def _(s):
        due_in(s)
        near = pl.ds(pl.multiple_of(s * quarter, quarter), quarter)
        t_acc[:, near] = mm_nt(e[0], wbuf[0, near, :]) + mm_nt(e[1], wbuf[1, near, :])

    due_out = line.during(seqs, 50.0, 3.0)

    @pl.loop(0, seqs)
    def _(n):
        due_out(n)
        at = pl.ds(pl.multiple_of(n * rows, 16), rows)
        normal, inverse = layer_stats(x[at, :].astype(f32))
        t = t_acc[at, :]
        grad = er[at, :] + norm_back(t, normal, inverse, vec[0:1, :])
        small[0:1, :] += jnp.sum(t * normal, axis=0, keepdims=True)
        small[1:2, :] += jnp.sum(t, axis=0, keepdims=True)
        write = pltpu.make_async_copy(stage, out.at[n], stage_sem)

        @pl.when(n > 0)
        def _():
            write.wait()

        stage[0:buf, :] = grad[0:buf]
        pick = picker(keep[n], rows - buf)
        rest = grad[buf:]
        top = rest.astype(bf16)
        rest = rest - top.astype(f32)
        middle = rest.astype(bf16)
        bottom = (rest - middle.astype(f32)).astype(bf16)
        stage[buf:, :] = mm_tn(pick, top) + mm_tn(pick, middle) + mm_tn(pick, bottom)
        write.start()

    pltpu.make_async_copy(stage, out.at[0], stage_sem).wait()

    small[4:12, :] = sums_feed[4:12, :]
    kept = counts[0]
    for n in range(1, seqs):
        kept = kept + counts[n]
    lane = lax.broadcasted_iota(jnp.int32, (1, d), 1)
    tally = jnp.where(lane == 3, kept.astype(f32), 0.0)
    for k, row in enumerate((stats[0:1, :], stats[1:2, :], sums_feed[12:13, :])):
        tally = tally + jnp.where(lane == k, jnp.sum(row, axis=1, keepdims=True), 0.0)
    small[12:13, :] = tally
    hops = [place.to_first, place.to_second] + [place.to_bit(b) for b in (1, 2, *bits)]
    small_in[0, 0] = small[...]

    def hop(k):
        return pltpu.make_async_remote_copy(
            src_ref=small_in.at[k, 0], dst_ref=small_in.at[k, 1], send_sem=small_send.at[k], recv_sem=small_recv.at[k],
            device_id=hops[k], device_id_type=MESH,
        )

    def small_step(k):
        if k > 0:
            hop(k - 1).wait()
            value = small_in[k - 1, 0] + small_in[k - 1, 1]
            if k == len(hops):
                small[...] = value
                return
            small_in[k, 0] = value
        hop(k).start()

    for k in range(len(hops) + 1):
        line.add(63.0 + 5 * k, functools.partial(small_step, k))
    line.until(1e9)


def adam_math(w, f, s, grad, rate, decay):
    first_new = beta_first * f + (1.0 - beta_first) * grad
    second_new = beta_second * s + (1.0 - beta_second) * grad * grad
    fix_first = 1.0 - beta_first**STEP
    fix_second = 1.0 - beta_second**STEP
    update = first_new / fix_first / (jnp.sqrt(second_new / fix_second) + adam_epsilon)
    return w - rate * (update + decay * w), first_new, second_new


def adam_kernel(w, f, s, grad, *rest):
    w_out, f_out, s_out, low_out = rest[-4:]
    new, first, second = adam_math(w[...], f[...], s[...], grad[0].astype(f32), rate_matrix, weight_decay)
    w_out[...] = new
    f_out[...] = first
    s_out[...] = second
    low_out[...] = new.astype(bf16)


def adam_call(state, grad, grid, block, place, grad_place, previous=None):
    spec = pl.BlockSpec(block, place)
    shape = state[0].shape
    extra = [] if previous is None else list(previous)
    size = grid[0] * grid[1] * block[0] * block[1]
    return pl.pallas_call(
        adam_kernel,
        grid=grid,
        in_specs=[spec] * 3 + [pl.BlockSpec((1, *block), grad_place)] + [ANY_SPEC] * len(extra),
        out_specs=[spec] * 4,
        out_shape=[sds(shape, f32)] * 3 + [sds(shape, bf16)],
        input_output_aliases={4 + k: k for k in range(len(extra))},
        compiler_params=params(40),
        cost_estimate=cost(20 * size, 28 * size),
    )(*state, grad, *extra)


def local(groups, replicas, *args):
    tokens, keep, cot, mats, down, vectors, f_mats, f_down, f_vectors, s_mats, s_down, s_vectors = args
    seqs, length, d = tokens.shape
    image = keep.shape[1]
    buf = length - image
    rows = -(-(buf + KEEP_MAX) // 16) * 16
    total = seqs * rows
    half = d // 2
    group = lax.axis_index("group")
    counts = (buf + jnp.sum(keep, axis=1)).astype(jnp.int32)

    keep3 = keep.reshape(seqs, 1, image)
    deep = mats.shape[0]
    w_attn, w_up, w_down, own_down, x, em, h1, qkv, o, r, h2, vec, stats = pl.pallas_call(
        functools.partial(attend_kernel, seqs, buf),
        in_specs=[SMEM_SPEC] + [VMEM_SPEC] * 2 + [ANY_SPEC] * 4,
        out_specs=[ANY_SPEC] * 11 + [VMEM_SPEC] * 2,
        out_shape=[
            sds((2, d, 2 * d), bf16),
            sds((2, d, 2 * d), bf16),
            sds((2, d, d), bf16),
            sds((deep, d), bf16),
            sds((total, d), bf16),
            sds((total, d), bf16),
            sds((total, d), bf16),
            sds((total, 3 * d), bf16),
            sds((total, d), bf16),
            sds((total, d), f32),
            sds((total, d), bf16),
            sds((16, d), f32),
            sds((8, d), f32),
        ],
        scratch_shapes=[
            pltpu.VMEM((total, d), bf16),
            pltpu.VMEM((total, d), bf16),
            pltpu.VMEM((total, d), bf16),
            pltpu.VMEM((total, 3 * d), bf16),
            pltpu.VMEM((total, d), bf16),
            pltpu.VMEM((total, d), f32),
            pltpu.VMEM((total, d), bf16),
            pltpu.SemaphoreType.DMA((7,)),
            pltpu.VMEM((2, d, 2 * d), bf16),
            pltpu.VMEM((2, deep, 2 * d), f32),
            pltpu.VMEM((half, d), f32),
            pltpu.VMEM((2, deep, d), bf16),
            pltpu.VMEM((2, deep, d), bf16),
            pltpu.VMEM((2, seqs, length, d), bf16),
            pltpu.VMEM((4, 16, d // 4), bf16),
            pltpu.SemaphoreType.DMA((7, 10)),
            pltpu.SemaphoreType.DMA((7, 10)),
            pltpu.SemaphoreType.DMA((3,)),
            pltpu.SemaphoreType.DMA((3,)),
            pltpu.SemaphoreType.DMA((9,)),
            pltpu.SemaphoreType.DMA((5,)),
            pltpu.SemaphoreType.DMA((2, seqs)),
        ],
        compiler_params=params(60, collective_id=0, has_side_effects=True),
        cost_estimate=cost(2 * total * 4 * d * d * 4, 20 * total * d),
    )(counts, keep3, vectors, mats, down, tokens, cot)
    quarter = d // 4
    er, ea, block_output, sums_feed, part_sum, z_mine, z_got, u_mine, u_got, h2_got, em_got = pl.pallas_call(
        functools.partial(feed_kernel, seqs, buf),
        in_specs=[SMEM_SPEC] + [VMEM_SPEC] * 5 + [ANY_SPEC] * 5,
        out_specs=[VMEM_SPEC] * 4 + [ANY_SPEC] * 7,
        out_shape=[
            sds((total, d), f32),
            sds((total, d), bf16),
            sds((seqs, length, d), bf16),
            sds((16, d), f32),
            sds((quarter, d), bf16),
            sds((total, d), bf16),
            sds((total, d), bf16),
            sds((2, total, d), bf16),
            sds((2, total, d), bf16),
            sds((total, d), bf16),
            sds((total, d), bf16),
        ],
        scratch_shapes=[
            pltpu.VMEM((2, d, 2 * d), bf16),
            pltpu.VMEM((2, 2, d, d), bf16),
            pltpu.VMEM((total, d), f32),
            pltpu.VMEM((total, d), f32),
            pltpu.VMEM((2, 2, total, d), bf16),
            pltpu.VMEM((2, 2, total, d), bf16),
            pltpu.VMEM((2, 2 * total, d), bf16),
            pltpu.VMEM((4, quarter, d), bf16),
            pltpu.VMEM((2, quarter, d), bf16),
            pltpu.VMEM((quarter, d), bf16),
            pltpu.SemaphoreType.DMA((5,)),
            pltpu.SemaphoreType.DMA((2,)),
            pltpu.SemaphoreType.DMA((2,)),
            pltpu.SemaphoreType.DMA((10,)),
            pltpu.SemaphoreType.DMA((10,)),
            pltpu.SemaphoreType.DMA((8, 2)),
            pltpu.SemaphoreType.DMA((8, 2)),
            pltpu.SemaphoreType.DMA((8, 2)),
            pltpu.SemaphoreType.DMA((7,)),
            pltpu.SemaphoreType.DMA((7,)),
        ],
        compiler_params=params(61, collective_id=1, has_side_effects=True),
        cost_estimate=cost(2 * total * 16 * d * d, 60 * total * d),
    )(counts, keep3, h2, em, r, vec, h2, em, w_up, w_down, own_down)

    bits = []
    while (4 << len(bits)) < replicas:
        bits.append(4 << len(bits))
    sizes = (d, d, d, d, half, d, half)
    chunks, steps = len(sizes), 7 + len(bits)
    found = pl.pallas_call(
        functools.partial(tail_kernel, seqs, buf, tuple(bits), sizes),
        in_specs=[SMEM_SPEC] + [VMEM_SPEC] * 7 + [ANY_SPEC] * 13,
        out_specs=[VMEM_SPEC, ANY_SPEC] + [ANY_SPEC] * (chunks + 4),
        out_shape=[sds((16, d), f32), sds((seqs, length, d), f32)]
        + [sds((2, quarter, wide), bf16) for wide in sizes]
        + [sds((total, d), bf16)] * 3
        + [sds((total, 3 * half), bf16)],
        scratch_shapes=[
            pltpu.VMEM((2, d, 3 * half), bf16),
            pltpu.VMEM((total, d), bf16),
            pltpu.VMEM((2, total, 3 * half), bf16),
            pltpu.VMEM((total, d), f32),
            pltpu.VMEM((length, d), f32),
            pltpu.VMEM((2, 2, 2 * total, d), bf16),
            pltpu.VMEM((4 + len(bits), 2, 16, d), f32),
        ]
        + [pltpu.VMEM((4, quarter, wide), bf16) for wide in sizes]
        + [pltpu.VMEM((2, quarter, wide), bf16) for wide in sizes]
        + [pltpu.VMEM((quarter, wide), bf16) for wide in sizes]
        + [pltpu.VMEM((quarter // 2, wide), bf16) for wide in sizes]
        + [pltpu.VMEM((len(bits), quarter // 2, wide), bf16) for wide in sizes]
        + [
            pltpu.SemaphoreType.DMA((chunks, steps + 1)),
            pltpu.SemaphoreType.DMA((chunks, steps)),
            pltpu.SemaphoreType.DMA(()),
            pltpu.SemaphoreType.DMA(()),
            pltpu.SemaphoreType.DMA(()),
            pltpu.SemaphoreType.DMA((2, 2, 2)),
            pltpu.SemaphoreType.DMA(()),
            pltpu.SemaphoreType.DMA((4,)),
            pltpu.SemaphoreType.DMA((4,)),
            pltpu.SemaphoreType.DMA((4 + len(bits),)),
            pltpu.SemaphoreType.DMA((4 + len(bits),)),
        ],
        compiler_params=params(61, collective_id=2, has_side_effects=True),
        cost_estimate=cost(2 * total * 16 * d * d, 100 * total * d),
    )(counts, keep3, qkv, x, er, vec, stats, sums_feed, part_sum, z_mine, z_got, em, em_got, h2, h2_got, u_mine, u_got, o, ea, h1, w_attn)
    small, input_grad = found[:2]
    grads = found[2 : 2 + chunks]
    branch_rms = jnp.sqrt(small[12, 0:3] / (small[12, 3] * d))
    part = vectors.shape[1]
    grad_vectors = lax.dynamic_slice(small, (0, group * part), (12, part))

    new_down = None
    for k in range(2):
        new_down = adam_call(
            (down, f_down, s_down),
            grads[k],
            (2, 2),
            (quarter, half),
            lambda h, j, k=k: (2 * h + k, j),
            lambda h, j: (h, 0, j),
            new_down,
        )
    new_mats = None
    for t in range(2):
        new_mats = adam_call(
            (mats, f_mats, s_mats),
            grads[2 + t],
            (2, 4),
            (quarter, quarter),
            lambda h, j, t=t: (0, 16 + 4 * j + 2 * h + t),
            lambda h, j: (h, 0, j),
            new_mats,
        )
    for k, first_strip in ((4, 3), (5, 0), (6, 2)):
        new_mats = adam_call(
            (mats, f_mats, s_mats),
            grads[k],
            (2, sizes[k] // half),
            (quarter, half),
            lambda h, j, at=first_strip: (0, 2 * (at + j) + h),
            lambda h, j: (h, 0, j),
            new_mats,
        )
    new_vectors, first_vectors, second_vectors = adam_math(
        vectors, f_vectors, s_vectors, grad_vectors, rate_vector, 0.0
    )
    return (
        block_output,
        input_grad,
        new_mats[0],
        new_down[0],
        new_vectors,
        new_mats[1],
        new_down[1],
        first_vectors,
        new_mats[2],
        new_down[2],
        second_vectors,
        new_mats[3],
        new_down[3],
        new_vectors.astype(bf16),
        branch_rms,
    )


def solution(mesh):
    rows, owned, columns = P(BOTH, None, None), P("group", None), P(None, "group")
    state = (owned, owned, columns)
    return jax.shard_map(
        functools.partial(local, mesh.shape["group"], mesh.shape["dp"]),
        mesh=mesh,
        in_specs=(rows, P(BOTH, None), rows) + state * 3,
        out_specs=(rows, rows) + state * 4 + (P(),),
        check_vma=False,
    )
```

```python
import functools
import math

import jax
import jax.numpy as jnp
from jax import lax
from jax.experimental import pallas as pl
from jax.experimental.pallas import tpu as pltpu
from jax.sharding import PartitionSpec as P

HEAD = 64
STEP = 7
KEEP_MAX = 77

norm_epsilon = 1e-06
beta_first = 0.5
beta_second = 0.5
adam_epsilon = 1e-08
rate_matrix = 0.05
rate_vector = 0.3
weight_decay = 0.05
root_half = 0.7071067811865476
inverse_root_two_pi = 0.3989422804014327

bf16 = jnp.bfloat16
f32 = jnp.float32
BOTH = ("group", "dp")
VMEM_SPEC = pl.BlockSpec(memory_space=pltpu.VMEM)
SMEM_SPEC = pl.BlockSpec(memory_space=pltpu.SMEM)
ANY_SPEC = pl.BlockSpec(memory_space=pl.ANY)
MIB = 1 << 20
GATHER = dict(attn=3.0, up=18.0, up_gap=10.0, down=38.0, two=2.0, third=4.0, near=4.5, four=6.0, five=8.0, loop=23.5, gap=0.9)
FEED = (4, 6, 7, 9, 10, 15)
TAIL = {
    0: ((0, 2), (1, -1), (1, 0)),
    2: ((2, -1), (0, 3)),
    6: ((1, 1), (2, 0)),
    7: ((3, -1),),
    8: ((1, 2),),
    10: ((0, 4),),
    13: ((4, -1), (2, 1)),
    14: ((1, 3),),
    15: ((3, 0),),
    18: ((0, 5),),
    20: ((2, 2),),
    26: ((3, 1), (2, 3)),
    32: ((4, 0), (1, 4)),
    34: ((3, 2), (5, -1), (4, 1), (5, 0), (2, 4)),
    36: ((4, 2),),
    37: ((3, 3), (5, 1), (6, -1), (1, 5)),
    38: ((4, 3),),
    40: ((5, 2),),
    41: ((3, 4),),
    42: ((1, 6), (6, 0), (5, 3), (6, 1), (9, 10), (3, 5), (9, 11), (0, 6), (9, 12), (6, 2), (9, 13), (4, 4), (6, 3), (9, 14), (5, 4), (2, 5), (9, 15), (6, 4), (5, 5), (4, 5), (3, 6), (6, 5), (9, 16), (5, 6), (2, 6), (4, 6), (6, 6)),
}


def mm(a, b):
    return jnp.dot(a, b, preferred_element_type=f32)


def mm_nt(a, b):
    return lax.dot_general(a, b, (((1,), (1,)), ((), ())), preferred_element_type=f32)


def mm_tn(a, b):
    return lax.dot_general(a, b, (((0,), (0,)), ((), ())), preferred_element_type=f32)


def sds(shape, dtype):
    return jax.ShapeDtypeStruct(shape, dtype)


def params(mib, **more):
    return pltpu.CompilerParams(vmem_limit_bytes=mib * MIB, **more)


def cost(flops, nbytes):
    return pl.CostEstimate(flops=int(flops), bytes_accessed=int(nbytes), transcendentals=0)


def layer_stats(values):
    centre = jnp.mean(values, axis=-1, keepdims=True)
    centred = values - centre
    variance = jnp.mean(centred * centred, axis=-1, keepdims=True)
    inverse = lax.rsqrt(variance + norm_epsilon)
    return centred * inverse, inverse


def norm_back(grad_normed, normal, inverse, gain):
    scaled = grad_normed * gain
    mean_one = jnp.mean(scaled, axis=-1, keepdims=True)
    mean_two = jnp.mean(scaled * normal, axis=-1, keepdims=True)
    return inverse * (scaled - mean_one - normal * mean_two)


def picker(keep_row, rows):
    image = keep_row.shape[1]
    ahead = lax.broadcasted_iota(jnp.int32, (image, image), 0)
    here = lax.broadcasted_iota(jnp.int32, (image, image), 1)
    upper = jnp.where(ahead <= here, 1.0, 0.0).astype(bf16)
    kept = keep_row.astype(f32)
    place = mm(kept.astype(bf16), upper) - 1.0
    place = jnp.where(kept > 0.5, place, -1.0)
    want = lax.broadcasted_iota(jnp.int32, (rows, image), 0).astype(f32)
    return jnp.where(place == want, 1.0, 0.0).astype(bf16)


MESH = pl.DeviceIdType.MESH


def flip(value, bit):
    return value + bit - 2 * bit * ((value // bit) % 2)


class Place:
    def __init__(self):
        self.group, self.replica = lax.axis_index("group"), lax.axis_index("dp")
        self.core, self.level = self.replica % 2, (self.replica // 2) % 2
        one, two = flip(self.group, 1), flip(self.group, 2)
        self.first = (1 - self.core) * one + self.core * two
        self.second = (1 - self.core) * two + self.core * one
        self.third = flip(one, 2)
        self.to_first = (self.first, self.replica)
        self.to_second = (self.second, self.replica)
        self.to_third = (self.third, self.replica)
        self.to_core = (self.group, flip(self.replica, 1))

    def to_bit(self, bit):
        return (self.group, flip(self.replica, bit))

    def meet(self, partners):
        barrier = pltpu.get_barrier_semaphore()
        for partner in partners:
            pl.semaphore_signal(barrier, inc=1, device_id=partner, device_id_type=MESH)
        pl.semaphore_wait(barrier, len(partners))


class Timeline:
    def __init__(self):
        self.steps = []

    def add(self, when, step):
        self.steps.append((when, len(self.steps), step))
        self.steps.sort(key=lambda one: one[:2])

    def until(self, when):
        while self.steps and self.steps[0][0] <= when:
            self.steps.pop(0)[2]()

    def during(self, count, start, gap):
        due = []
        while self.steps and self.steps[0][0] < start + count * gap:
            when, _, step = self.steps.pop(0)
            due.append((min(max(int((when - start) / gap), 0), count - 1), step))

        def run(turn):
            for at, step in due:
                pl.when(turn == at)(step)

        return run


class Gather:
    def __init__(self, place, own, full, cols, send, recv):
        self.place, self.own, self.full, self.cols, self.send, self.recv = place, own, full, cols, send, recv
        deep = own.shape[0]
        self.deep, self.strip = deep, 5 * deep // 16
        self.main = deep - self.strip
        self.main_at = place.level * self.strip
        self.strip_at = place.level * self.main

    def block(self, owner, start, size, core=None):
        at = pl.multiple_of(owner * self.deep + start, 16)
        return self.full.at[self.place.core if core is None else core, pl.ds(at, size), self.cols]

    def whole(self, owner, core=None):
        return self.block(owner, 0, self.deep, core)

    def copy(self, k):
        p = self.place
        main, strip, whole = (self.main_at, self.main), (self.strip_at, self.strip), (0, self.deep)
        owner, (at, size), device = (
            (p.group, main, p.to_first),
            (p.group, main, p.to_second),
            (p.first, main, p.to_second),
            (p.first, strip, p.to_bit(2)),
            (p.second, strip, p.to_bit(2)),
            (p.third, strip, p.to_bit(2)),
            (p.group, whole, p.to_core),
            (p.first, whole, p.to_core),
            (p.second, whole, p.to_core),
            (p.third, whole, p.to_core),
        )[k]
        dst = self.block(owner, at, size)
        src = dst
        if k in (0, 1, 6):
            src = self.own.at[pl.ds(pl.multiple_of(at, 16) if k < 6 else 0, size), :]
        return pltpu.make_async_remote_copy(
            src_ref=src, dst_ref=dst, send_sem=self.send.at[k], recv_sem=self.recv.at[k],
            device_id=device, device_id_type=MESH,
        )

    def start(self, *ks):
        for k in ks:
            self.copy(k).start()

    def arrived(self, *ks):
        for k in ks:
            self.copy(k).wait_recv()

    def sent(self, *ks):
        for k in ks:
            self.copy(k).wait_send()

    def step_one(self):
        self.start(0, 1, 6)

    def step_two(self):
        self.arrived(0)
        self.start(2, 3)
        self.arrived(1)
        self.start(4)

    def step_near(self):
        self.arrived(3)
        self.start(7)
        self.arrived(4)
        self.start(8)

    def step_third(self):
        self.arrived(2)
        self.start(5)

    def step_four(self):
        self.arrived(5)
        self.start(9)

    def step_five(self):
        self.arrived(6, 7, 8, 9)
        self.sent(*range(10))

    def schedule(self, line, start, size):
        line.add(start, self.step_one)
        line.add(start + 8 * size + GATHER["two"], self.step_two)
        line.add(start + 12 * size + GATHER["third"], self.step_third)
        line.add(start + 14 * size + GATHER["near"], self.step_near)
        line.add(start + 16 * size + GATHER["four"], self.step_four)
        line.add(start + 17 * size + GATHER["five"], self.step_five)


def head_masks():
    lane = lax.broadcasted_iota(jnp.int32, (1, 2 * HEAD), 1)
    low = jnp.where(lane < HEAD, 1.0, 0.0)
    return low.astype(bf16), (1.0 - low).astype(bf16), low > 0.5


def two_heads(x, low, high):
    return jnp.concatenate([x * low, x * high], axis=0)


def pick_heads(both, first):
    rows = both.shape[0] // 2
    return jnp.where(first, both[:rows], both[rows:])


def pair_probs(q_pair, k_pair, count):
    raw = mm_nt(q_pair, k_pair) * (1.0 / math.sqrt(HEAD))
    col = lax.broadcasted_iota(jnp.int32, raw.shape, 1)
    raw = jnp.where(col < count, raw, -1e30)
    top = jnp.max(raw, axis=-1, keepdims=True)
    exponent = jnp.exp(raw - top)
    return exponent / jnp.sum(exponent, axis=-1, keepdims=True)


def attend_kernel(seqs, buf, *refs):
    counts, keep, vectors, mats, down, tokens, cot = refs[:7]
    w_attn, w_up, w_down, own_down, x_out, em_out, h1_out, qkv_out, o_out, r_out, h2_out, vec, stats = refs[7:20]
    x, em, h1, qkv, o, r, h2, outs, wbuf, wide, tall, low_up, low_down, rows_in, parts, send, recv, vec_send, vec_recv, loads, stores, reads = refs[20:]
    rows = h1.shape[0] // seqs
    d = h1.shape[1]
    half = d // 2
    place = Place()
    core = place.core
    deep = mats.shape[0]

    takes = []
    for j in range(8):
        at = pl.ds(pl.multiple_of((2 * j + core) * half, half), half)
        takes.append(
            pltpu.make_async_copy(mats.at[:, at], wide.at[j // 4, :, pl.ds((j % 4) * half, half)], loads.at[j])
        )
    takes.append(
        pltpu.make_async_copy(down.at[pl.ds(pl.multiple_of(core * half, half), half), :], tall, loads.at[8])
    )
    for one in takes:
        one.start()
    reads_in = []
    for n in range(seqs):
        for k, src in enumerate((tokens, cot)):
            reads_in.append(pltpu.make_async_copy(src.at[n], rows_in.at[k, n], reads.at[k, n]))
    for one in reads_in:
        one.start()

    place.meet((place.to_first, place.to_second, place.to_third, place.to_core, place.to_bit(2)))

    part = vectors.shape[1]
    parts[place.group] = jnp.concatenate([vectors[...], jnp.zeros((4, part), f32)], axis=0).astype(bf16)
    for k, partner in enumerate((place.to_first, place.to_second, place.to_third)):
        pltpu.make_async_remote_copy(
            src_ref=parts.at[place.group], dst_ref=parts.at[place.group],
            send_sem=vec_send.at[k], recv_sem=vec_recv.at[k], device_id=partner, device_id_type=MESH,
        ).start()

    own_rows = pl.ds(pl.multiple_of(place.group * deep, deep), deep)
    line = Timeline()
    attn = []
    for j in range(4):
        cols = pl.ds(j * half, half)
        own = wbuf.at[core, own_rows, cols]
        takes[j].wait()
        own[...] = wide[0, :, cols].astype(bf16)
        attn.append(Gather(place, own, wbuf, cols, send.at[j], recv.at[j]))
        attn[j].schedule(line, GATHER["attn"] * j, 0.5)
        if j == 0:
            line.until(0)
    ups = []
    for j in range(2):
        cols = pl.ds(j * d, d)
        for one in takes[4 + 2 * j : 6 + 2 * j]:
            one.wait()
        low_up[j] = wide[1, :, cols].astype(bf16)
        ups.append(Gather(place, low_up.at[j], w_up, cols, send.at[4 + j], recv.at[4 + j]))
        ups[j].schedule(line, GATHER["up"] + GATHER["up_gap"] * j, 1.0)
    takes[8].wait()
    for j in range(2):
        low_down[j] = tall[j * deep : (j + 1) * deep, :].astype(bf16)
    early = Gather(place, low_down.at[0], w_down, pl.ds(0, d), send.at[6], recv.at[6])
    early.schedule(line, GATHER["down"], 1.0)
    keeps = [
        pltpu.make_async_copy(one.own, one.whole(place.group), stores.at[k]) for k, one in enumerate(ups + [early])
    ]
    keeps.append(pltpu.make_async_copy(low_down.at[1], own_down, stores.at[3]))
    for one in keeps:
        one.start()

    def keep_out(k, src, dst):
        one = pltpu.make_async_copy(src, dst, outs.at[k])
        one.start()
        keeps.append(one)

    for one in reads_in:
        one.wait()
    due_pack = line.during(seqs, 4.0, 1.0)

    @pl.loop(0, seqs)
    def _(n):
        due_pack(n)
        at = pl.multiple_of(n * rows, 16)
        pick = picker(keep[n], rows - buf)
        for k, dst in ((0, x), (1, em)):
            dst[pl.ds(at, buf), :] = rows_in[k, n, 0:buf, :]
            dst[pl.ds(pl.multiple_of(at + buf, 16), rows - buf), :] = mm(pick, rows_in[k, n, buf:, :]).astype(bf16)

    for k in range(3):
        pltpu.make_async_remote_copy(
            src_ref=parts.at[place.group], dst_ref=parts.at[place.group],
            send_sem=vec_send.at[k], recv_sem=vec_recv.at[k], device_id=place.to_first, device_id_type=MESH,
        ).wait()
    vec[...] = jnp.zeros_like(vec)
    for s in range(4):
        vec[:, s * part : (s + 1) * part] = parts[s].astype(f32)
    due_norm = line.during(seqs, 8.0, 0.7)

    @pl.loop(0, seqs)
    def _(n):
        due_norm(n)
        at = pl.ds(pl.multiple_of(n * rows, 16), rows)
        normal, _ = layer_stats(x[at, :].astype(f32))
        h1[at, :] = (normal * vec[0:1, :] + vec[1:2, :]).astype(bf16)

    keep_out(0, x, x_out)
    keep_out(1, em, em_out)
    keep_out(2, h1, h1_out)
    tile = half // 2
    for j in range(3):
        line.until(GATHER["attn"] * j + 17 * 0.5 + GATHER["five"])

        @pl.loop(0, 4)
        def _(i):
            h, t = i // 2, i % 2
            near = pl.multiple_of(i * tile, tile)
            w = wbuf[h, :, pl.ds(pl.multiple_of(j * half + t * tile, tile), tile)]
            got = mm(h1[...], w)
            if j != 1:
                got = got + vec[2 + j // 2 : 3 + j // 2, pl.ds(near, tile)]
            qkv[:, pl.ds(pl.multiple_of(j * d + near, tile), tile)] = got.astype(bf16)

    keep_out(3, qkv, qkv_out)
    low, high, first = head_masks()
    pairs = d // (2 * HEAD)
    loop_at, turn = GATHER["loop"], GATHER["gap"]
    due = line.during(seqs * pairs, loop_at, turn)
    mix_at = loop_at + seqs * pairs * turn

    @pl.loop(0, seqs * pairs)
    def _(i):
        due(i)
        n, j = i // pairs, i % pairs
        at = pl.ds(pl.multiple_of(n * rows, 16), rows)
        lanes = [pl.ds(pl.multiple_of(j * 2 * HEAD + m * d, 2 * HEAD), 2 * HEAD) for m in range(3)]
        q_pair = two_heads(qkv[at, lanes[0]], low, high)
        probs = pair_probs(q_pair, qkv[at, lanes[1]], counts[n]).astype(bf16)
        o[at, lanes[0]] = pick_heads(mm(probs, qkv[at, lanes[2]]), first).astype(bf16)

    keep_attn = pltpu.make_async_copy(wbuf, w_attn, stores.at[4])
    keep_attn.start()
    keep_out(4, o, o_out)
    due_mix = line.during(4, mix_at, 1.0)

    @pl.loop(0, 4)
    def _(i):
        due_mix(i)
        h, t = i // 2, i % 2
        near = pl.ds(pl.multiple_of(i * tile, tile), tile)
        w = wbuf[h, :, pl.ds(pl.multiple_of(3 * half + t * tile, tile), tile)]
        r[:, near] = mm(o[...], w) + vec[4:5, near]

    due_last = line.during(seqs, mix_at + 4, 1.5)
    stats[...] = jnp.zeros_like(stats)

    @pl.loop(0, seqs)
    def _(n):
        due_last(n)
        at = pl.ds(pl.multiple_of(n * rows, 16), rows)
        valid = lax.broadcasted_iota(jnp.int32, (rows, 1), 0) < counts[n]
        valid = jnp.where(valid, 1.0, 0.0)
        inputs = x[at, :].astype(f32)
        branch = r[at, :]
        resid = inputs + branch
        r[at, :] = resid
        normal, _ = layer_stats(resid)
        h2[at, :] = (normal * vec[5:6, :] + vec[6:7, :]).astype(bf16)
        stats[0:1, :] += jnp.sum(inputs * inputs * valid, axis=0, keepdims=True)
        stats[1:2, :] += jnp.sum(branch * branch * valid, axis=0, keepdims=True)

    keep_out(5, r, r_out)
    keep_out(6, h2, h2_out)
    line.until(1e9)
    for one in keeps:
        one.wait()
    keep_attn.wait()


class Reduce:
    def __init__(self, place, bits, g, r1, r2, r3, r4, total, send, recv):
        self.place, self.bits, self.g, self.r1, self.r2, self.r3, self.r4 = place, bits, g, r1, r2, r3, r4
        self.total, self.send, self.recv = total, send, recv
        self.half = g.shape[1] // 2
        self.hold = r2.at[pl.ds(0, self.half)]
        self.slots = [r1.at[n // 2 % 2, pl.ds(n % 2 * self.half, self.half)] for n in range(len(bits))]

    def copy(self, k):
        p = self.place
        half = self.half
        mine, other = p.level * half, (1 - p.level) * half
        at = lambda start: pl.ds(pl.multiple_of(start, 16), half)
        plans = [
            lambda: (self.g.at[p.third], self.r1.at[1], p.to_first),
            lambda: (self.g.at[p.first], self.r1.at[0], p.to_first),
            lambda: (self.g.at[p.second], self.r2, p.to_second),
            lambda: (self.g.at[p.group, at(other)], self.r3, p.to_bit(2)),
            lambda: (self.hold, self.total.at[p.core, at(mine)], p.to_bit(2)),
            lambda: (self.hold, self.total.at[p.core, at(mine)], p.to_core),
            lambda: (self.total.at[p.core, at(other)], self.total.at[p.core, at(other)], p.to_core),
        ]
        for n, bit in enumerate(self.bits):
            plans.append(lambda n=n, bit=bit: (self.slots[n], self.r4.at[n], p.to_bit(bit)))
        src, dst, device = plans[k]()
        return pltpu.make_async_remote_copy(
            src_ref=src, dst_ref=dst, send_sem=self.send.at[k], recv_sem=self.recv.at[k],
            device_id=device, device_id_type=MESH,
        )

    def begin(self):
        self.copy(0).start()
        self.copy(1).start()

    def sent(self, *ks):
        for k in ks:
            self.copy(k).wait_send()

    def pass_second(self):
        self.copy(0).wait_recv()
        at = self.place.second
        self.g[at] = (self.g[at].astype(f32) + self.r1[1].astype(f32)).astype(bf16)
        self.copy(2).start()

    def settle(self):
        self.copy(1).wait_recv()
        self.copy(2).wait_recv()
        at = self.place.group
        self.g[at] = (self.g[at].astype(f32) + self.r1[0].astype(f32) + self.r2[...].astype(f32)).astype(bf16)

    def pass_replica(self):
        self.settle()
        self.copy(3).start()

    def pass_bit(self, n):
        p = self.place
        if n == 0:
            self.copy(3).wait_recv()
            at = pl.ds(pl.multiple_of(p.level * self.half, 16), self.half)
            value = self.g[p.group, at].astype(f32) + self.r3[...].astype(f32)
        else:
            self.copy(6 + n).wait_recv()
            value = self.slots[n - 1][...].astype(f32) + self.r4[n - 1].astype(f32)
        if n < len(self.bits):
            self.slots[n][...] = value.astype(bf16)
            self.copy(7 + n).start()
        else:
            self.hold[...] = value.astype(bf16)
            self.copy(4).start()
            self.copy(5).start()
            self.stay().start()

    def stay(self):
        p = self.place
        at = pl.ds(pl.multiple_of(p.level * self.half, 16), self.half)
        return pltpu.make_async_copy(self.hold, self.total.at[p.core, at], self.send.at[7 + len(self.bits)])

    def pass_core(self):
        self.copy(4).wait_recv()
        self.copy(6).start()

    def finish(self, start=0):
        self.copy(5).wait_recv()
        self.copy(6).wait_recv()
        self.sent(*range(start, 7 + len(self.bits)))
        self.stay().wait()


def block_grads(place, sides, wide, g):
    quarter = sides.shape[2] // 4

    @pl.loop(0, 4)
    def _(i):
        near = place.first * (1 - i // 2) + place.group * (i // 2)
        over = ((i + 1) // 2) % 2
        owner = near * (1 - over) + ((1 - place.core) * flip(near, 2) + place.core * flip(near, 1)) * over
        cols = pl.ds(pl.multiple_of(owner * quarter, quarter), quarter)
        g[owner] = mm_tn(sides[0, :, cols], sides[1, :, 0:wide]).astype(bf16)


def swap_start(place, src, dst, send, recv, k):
    copy = pltpu.make_async_remote_copy(
        src_ref=src, dst_ref=dst, send_sem=send.at[k], recv_sem=recv.at[k],
        device_id=place.to_core, device_id_type=MESH,
    )
    copy.start()
    return copy


def feed_kernel(seqs, buf, *refs):
    counts, keep, h2, em, vec, h2_hbm, em_hbm, r_hbm, ups, downs, own_down = refs[:11]
    sums, er_hbm, ea_hbm, out_hbm, part_sum, z_mine, z_got, u_mine, u_got, h2_got, em_got = refs[11:22]
    r, er, ea, out, wup, wdown, m_acc, t_acc, z_all, u_all, sides, g, r1, r2 = refs[22:36]
    sems, w_sems, o_sems, send, recv, g_send, g_recv, k_sems, t_send, t_recv, r_send, r_recv = refs[36:]
    total, d = h2.shape
    rows = total // seqs
    strip = wup.shape[2] // 4
    tile = strip // 2
    place = Place()
    core = place.core
    late = Gather(place, wdown.at[1, core, pl.ds(pl.multiple_of(place.group * tile, tile), tile)], wdown.at[1], pl.ds(0, d), g_send, g_recv)
    take_own = pltpu.make_async_copy(own_down, late.own, sems.at[0])
    take_own.start()
    take_r = pltpu.make_async_copy(r_hbm, r, sems.at[1])

    def owner_at(turn):
        near = place.group * (1 - turn % 2) + place.first * (turn % 2)
        over = turn // 2
        return near * (1 - over) + ((1 - core) * flip(near, 2) + core * flip(near, 1)) * over

    def takes(i):
        turn, away = i // 2, i % 2
        h = (1 - core) * away + core * (1 - away)
        s = owner_at(turn)
        cols = pl.ds(pl.multiple_of(s * strip, strip), strip)
        at = pl.ds(pl.multiple_of(s * tile, tile), tile)
        return [
            pltpu.make_async_copy(ups.at[h, :, cols], wup.at[h, :, cols], w_sems.at[i, 0]),
            pltpu.make_async_copy(downs.at[h, at], wdown.at[0, h, at], w_sems.at[i, 1]),
        ]

    for i in range(8):
        for one in takes(i):
            one.start()
    take_r.start()
    place.meet((place.to_core, place.to_second, place.to_first, place.to_bit(2)))
    take_own.wait()
    late.step_one()
    swaps = [
        swap_start(place, em_hbm, em_got, send, recv, 0),
        swap_start(place, h2_hbm, h2_got, send, recv, 1),
    ]
    reduce = Reduce(place, (), g, r1, r2, None, None, None, r_send, r_recv)
    sides[1, 0:total, :] = em[...]
    take_em = pltpu.make_async_copy(em_got, sides.at[1, pl.ds(total, total)], sems.at[4])
    sums[...] = jnp.zeros_like(sums)
    m_acc[...] = jnp.zeros_like(m_acc)
    t_acc[...] = jnp.zeros_like(t_acc)

    def tile_copies(k, s, t, away):
        cols = pl.ds(pl.multiple_of(s * tile, tile), tile)
        z_to = sides.at[0, pl.ds(0 if not away else total, total), cols] if t == 0 else (z_got if away else z_mine).at[:, cols]
        pairs = (
            (z_all.at[(1 - core) if away else core, t, :, cols], z_to),
            (u_all.at[(1 - core) if away else core, t, :, cols], (u_got if away else u_mine).at[t, :, cols]),
        )
        if not away:
            return [pltpu.make_async_copy(src, dst, k_sems.at[k, n]) for n, (src, dst) in enumerate(pairs)]
        return [
            pltpu.make_async_remote_copy(
                src_ref=src, dst_ref=dst, send_sem=t_send.at[k, n], recv_sem=t_recv.at[k, n],
                device_id=place.to_core, device_id_type=MESH,
            )
            for n, (src, dst) in enumerate(pairs)
        ]

    def late_own():
        late.arrived(6)

    def late_last():
        late.arrived(7, 8, 9)
        late.sent(*range(10))

    def begin():
        take_em.wait()
        for k in range(4):
            tile_copies(k, 0, 0, False)[0].wait()
            tile_copies(k, 0, 0, True)[0].wait()
        block_grads(place, sides, d, g)
        reduce.begin()

    due = [(2, swaps[0].wait), (7, late_own), (8, begin)]
    due += zip(FEED, (late.step_two, late.step_third, late.step_near, late.step_four, late_last, reduce.pass_second))
    orders = [[(when - 8 * t, step) for when, step in due if when // 8 == t] for t in range(2)]

    for t in range(2):

        @pl.loop(0, 8)
        def _(i):
            for when, step in orders[t]:
                pl.when(i == when)(step)
            if t == 0:
                pl.when(i == 2)(take_em.start)
                for one in takes(i):
                    one.wait()
            turn, away = i // 2, i % 2
            h = (1 - core) * away + core * (1 - away)
            s = owner_at(turn)
            cols = pl.ds(pl.multiple_of(s * strip + t * tile, tile), tile)
            far = (pl.ds(8 + s, 1), pl.ds(pl.multiple_of(h * strip + t * tile, tile), tile))
            near = pl.ds(pl.multiple_of(s * tile, tile), tile)
            w_up = wup[h, :, cols]
            w_down = wdown[t, h, near, :]
            u = mm(h2[...], w_up) + vec[far]
            phi = 0.5 * (1.0 + lax.erf(u * root_half))
            z = (u * phi).astype(bf16)
            z_all[h, t, :, near] = z
            slope = phi + u * jnp.exp(-0.5 * u * u) * inverse_root_two_pi
            eu = (mm_nt(em[...], w_down) * slope).astype(bf16)
            u_all[h, t, :, near] = eu
            m_acc[...] += mm(z, w_down)
            t_acc[...] += mm_nt(eu, w_up)
            sums[far] = jnp.sum(eu.astype(f32), axis=0, keepdims=True)
            for side in range(2):

                @pl.when(away == side)
                def _():
                    for one in tile_copies(4 * t + turn, s, t, side == 1):
                        one.start()

    take_r.wait()

    def results(n):
        at = pl.ds(pl.multiple_of(n * rows, 16), rows)
        return [
            pltpu.make_async_copy(er.at[at], er_hbm.at[at], o_sems.at[n, 0]),
            pltpu.make_async_copy(ea.at[at], ea_hbm.at[at], o_sems.at[n, 1]),
            pltpu.make_async_copy(out.at[n], out_hbm.at[n], o_sems.at[n, 2]),
        ]

    @pl.loop(0, seqs)
    def _(n):
        at = pl.ds(pl.multiple_of(n * rows, 16), rows)
        valid = lax.broadcasted_iota(jnp.int32, (rows, 1), 0) < counts[n]
        valid = jnp.where(valid, 1.0, 0.0)
        resid = r[at, :]
        m = m_acc[at, :] + vec[7:8, :]
        packed = ((resid + m) * valid).astype(bf16)
        out[n, 0:buf, :] = packed[0:buf]
        pick = picker(keep[n], rows - buf)
        out[n, buf:, :] = mm_tn(pick, packed[buf:]).astype(bf16)
        normal, inverse = layer_stats(resid)
        t = t_acc[at, :]
        low = em[at, :].astype(f32)
        back = low + norm_back(t, normal, inverse, vec[5:6, :])
        er[at, :] = back
        ea_low = back.astype(bf16)
        ea[at, :] = ea_low
        sums[4:5, :] += jnp.sum(ea_low.astype(f32), axis=0, keepdims=True)
        sums[5:6, :] += jnp.sum(t * normal, axis=0, keepdims=True)
        sums[6:7, :] += jnp.sum(t, axis=0, keepdims=True)
        sums[7:8, :] += jnp.sum(low, axis=0, keepdims=True)
        sums[12:13, :] += jnp.sum(m * m * valid, axis=0, keepdims=True)
        for one in results(n):
            one.start()
    reduce.settle()
    share = pltpu.make_async_copy(g.at[place.group], part_sum, sems.at[0])
    share.start()
    for n in range(seqs):
        for one in results(n):
            one.wait()
    swaps[1].wait()
    reduce.sent(0, 1, 2)
    share.wait()
    for k in range(8):
        for away in (False, True):
            for one in tile_copies(k, 0, k // 4, away)[0 if k >= 4 else 1 :]:
                one.wait()


def tail_kernel(seqs, buf, bits, sizes, *refs):
    counts, keep, vec, stats, sums_feed, qkv_hbm, x_hbm, er_hbm = refs[:8]
    part_sum, z_mine, z_got, em, em_got, h2, h2_got, u_mine, u_got, o, ea, h1, w_attn = refs[8:21]
    chunks = len(sizes)
    small, out = refs[21:23]
    totals = refs[23 : 23 + chunks]
    o_got, ea_got, h1_got, e_got = refs[23 + chunks : 27 + chunks]
    scratch = refs[27 + chunks :]
    qkv, x, er, in_sems = scratch[:4]
    scratch = scratch[4:]
    wbuf, eo, e, t_acc, stage, sides, small_in = scratch[:7]
    buffers = [scratch[7 + k * chunks : 7 + (k + 1) * chunks] for k in range(5)]
    send, recv, w_sem, ea_sem, first_sem, side_sems, stage_sem, swap_send, swap_recv, small_send, small_recv = scratch[7 + 5 * chunks :]
    total, d = eo.shape
    rows = total // seqs
    half, quarter = d // 2, d // 4
    place = Place()
    core = place.core

    o_weight = pltpu.make_async_copy(w_attn.at[:, :, pl.ds(3 * half, half)], wbuf.at[:, :, pl.ds(0, half)], w_sem)
    o_weight.start()
    ea_all = e.at[0, :, pl.ds(0, d)]
    take_ea = pltpu.make_async_copy(ea, ea_all, ea_sem)
    take_ea.start()

    mine_cols = pl.ds(pl.multiple_of(core * half, half), half)
    left = [None, (z_mine, z_got), (h2, h2_got), (h2, h2_got), (o, o_got), (h1, h1_got), (h1, h1_got)]
    right = [
        None, (em, em_got),
        (u_mine.at[0], u_got.at[0]), (u_mine.at[1], u_got.at[1]),
        (ea.at[:, mine_cols], ea_got.at[:, mine_cols]),
        (e.at[core, :, pl.ds(0, d)], e_got.at[:, pl.ds(0, d)]), (e.at[core, :, pl.ds(d, half)], e_got.at[:, pl.ds(d, half)]),
    ]

    def side_copies(k):
        found = []
        for side, pairs in enumerate((left, right)):
            wide = sizes[k] if side else d
            for which, src in enumerate(pairs[k]):
                dst = sides.at[k % 2, side, pl.ds(which * total, total), pl.ds(0, wide)]
                found.append(pltpu.make_async_copy(src, dst, side_sems.at[k % 2, side, which]))
        return found

    def load_sides(k):
        for one in side_copies(k):
            one.start()

    load_sides(1)
    load_sides(2)
    inputs = [
        pltpu.make_async_copy(src, dst, in_sems.at[k])
        for k, (src, dst) in enumerate(((qkv_hbm, qkv), (x_hbm, x), (er_hbm, er)))
    ]
    for one in inputs:
        one.start()
    partners = [place.to_first, place.to_second, place.to_core, place.to_bit(2)] + [place.to_bit(b) for b in bits]
    place.meet(partners)
    swaps = [
        swap_start(place, o, o_got, swap_send, swap_recv, 0),
        swap_start(place, ea, ea_got, swap_send, swap_recv, 1),
        swap_start(place, h1, h1_got, swap_send, swap_recv, 2),
    ]
    sent_e = pltpu.make_async_remote_copy(
        src_ref=e.at[1 - core], dst_ref=e_got, send_sem=swap_send.at[3], recv_sem=swap_recv.at[3],
        device_id=place.to_core, device_id_type=MESH,
    )
    reduces = [
        Reduce(place, bits, *(buffers[b][k] for b in range(5)), totals[k], send.at[k], recv.at[k]) for k in range(chunks)
    ]

    first_sum = pltpu.make_async_copy(part_sum, buffers[0][0].at[place.group], first_sem)
    first_sum.start()

    def gradient(k):
        for one in side_copies(k):
            one.wait()
        block_grads(place, sides.at[k % 2], sizes[k], reduces[k].g)

    def act(k, step):
        if k == 9:
            last = step == 16
            for n in range(step - 10, len(hops) + 1 if last else step - 9):
                small_step(n)
            return
        one = reduces[k]
        if step == -1:
            gradient(k)
            if k == 1:
                load_sides(3)
            if k == 2:
                for swap in swaps[:2]:
                    swap.wait()
                load_sides(4)
        elif step == 0:
            one.begin()
        elif step == 1:
            one.pass_second()
        elif step == 2 and k == 0:
            first_sum.wait()
            one.copy(3).start()
        elif step == 2:
            one.pass_replica()
        elif step == 3:
            one.pass_bit(0)
        elif step == 4:
            for n in range(1, len(bits) + 1):
                one.pass_bit(n)
        elif step == 5:
            one.pass_core()
        else:
            one.finish(0 if k else 3)

    def due(slot, turn=None, count=1):
        for n in range(count):
            steps = TAIL.get(slot + n, ())

            def run(steps=steps):
                for k, step in steps:
                    act(k, step)

            if turn is None:
                run()
            elif steps:
                pl.when(turn == n)(run)

    due(0)
    o_weight.wait()
    take_ea.wait()
    for one in inputs:
        one.wait()

    @pl.loop(0, 4)
    def _(s):
        near = pl.ds(pl.multiple_of(s * quarter, quarter), quarter)
        got = mm_nt(ea_all[:, 0:half], wbuf[0, near, 0:half]) + mm_nt(ea_all[:, half:], wbuf[1, near, 0:half])
        eo[:, near] = got.astype(bf16)

    in_weight = pltpu.make_async_copy(w_attn.at[:, :, pl.ds(0, 3 * half)], wbuf, w_sem)
    in_weight.start()
    low, high, first = head_masks()
    pairs = half // (2 * HEAD)
    scale = 1.0 / math.sqrt(HEAD)
    small[...] = jnp.zeros_like(small)
    turns = seqs * pairs

    planned = 32

    @pl.loop(0, 2 * turns)
    def _(i):
        pl.when(i == turns)(sent_e.start)
        due(1, i, planned)
        h = (1 - core) * (1 - i // turns) + core * (i // turns)
        n, j = (i % turns) // pairs, i % pairs
        at = pl.ds(pl.multiple_of(n * rows, 16), rows)
        far = h * half + j * 2 * HEAD
        lanes = [pl.ds(pl.multiple_of(far + m * d, 2 * HEAD), 2 * HEAD) for m in range(3)]
        k_pair = qkv[at, lanes[1]]
        q_both = two_heads(qkv[at, lanes[0]], low, high)
        probs = pair_probs(q_both, k_pair, counts[n])
        eo_both = two_heads(eo[at, lanes[0]], low, high)
        ep = mm_nt(eo_both, qkv[at, lanes[2]])
        inner = jnp.sum(probs * ep, axis=-1, keepdims=True)
        es = (probs * (ep - inner)).astype(bf16)
        ev = mm_tn(probs.astype(bf16), eo_both).astype(bf16)
        eq = (pick_heads(mm(es, k_pair), first) * scale).astype(bf16)
        ek = (mm_tn(es, q_both) * scale).astype(bf16)
        for m, value in enumerate((eq, ek, ev)):
            e[h, at, pl.ds(pl.multiple_of(m * half + j * 2 * HEAD, 2 * HEAD), 2 * HEAD)] = value
        small[2:3, lanes[0]] += jnp.sum(eq.astype(f32), axis=0, keepdims=True)
        small[3:4, lanes[0]] += jnp.sum(ev.astype(f32), axis=0, keepdims=True)

    due(1 + planned)
    sent_e.wait()
    swaps[2].wait()
    load_sides(5)
    load_sides(6)
    in_weight.wait()
    @pl.loop(0, 4)
    def _(s):
        due(2 + planned, s, 4)
        near = pl.ds(pl.multiple_of(s * quarter, quarter), quarter)
        t_acc[:, near] = mm_nt(e[0], wbuf[0, near, :]) + mm_nt(e[1], wbuf[1, near, :])

    @pl.loop(0, seqs)
    def _(n):
        due(6 + planned, n, 4)
        at = pl.ds(pl.multiple_of(n * rows, 16), rows)
        normal, inverse = layer_stats(x[at, :].astype(f32))
        t = t_acc[at, :]
        grad = er[at, :] + norm_back(t, normal, inverse, vec[0:1, :])
        small[0:1, :] += jnp.sum(t * normal, axis=0, keepdims=True)
        small[1:2, :] += jnp.sum(t, axis=0, keepdims=True)
        write = pltpu.make_async_copy(stage, out.at[n], stage_sem)

        @pl.when(n > 0)
        def _():
            write.wait()

        stage[0:buf, :] = grad[0:buf]
        pick = picker(keep[n], rows - buf)
        rest = grad[buf:]
        top = rest.astype(bf16)
        rest = rest - top.astype(f32)
        middle = rest.astype(bf16)
        bottom = (rest - middle.astype(f32)).astype(bf16)
        stage[buf:, :] = mm_tn(pick, top) + mm_tn(pick, middle) + mm_tn(pick, bottom)
        write.start()

    pltpu.make_async_copy(stage, out.at[0], stage_sem).wait()

    small[4:12, :] = sums_feed[4:12, :]
    kept = counts[0]
    for n in range(1, seqs):
        kept = kept + counts[n]
    lane = lax.broadcasted_iota(jnp.int32, (1, d), 1)
    tally = jnp.where(lane == 3, kept.astype(f32), 0.0)
    for k, row in enumerate((stats[0:1, :], stats[1:2, :], sums_feed[12:13, :])):
        tally = tally + jnp.where(lane == k, jnp.sum(row, axis=1, keepdims=True), 0.0)
    small[12:13, :] = tally
    hops = [place.to_first, place.to_second] + [place.to_bit(b) for b in (1, 2, *bits)]
    small_in[0, 0] = small[...]

    def hop(k):
        return pltpu.make_async_remote_copy(
            src_ref=small_in.at[k, 0], dst_ref=small_in.at[k, 1], send_sem=small_send.at[k], recv_sem=small_recv.at[k],
            device_id=hops[k], device_id_type=MESH,
        )

    def small_step(k):
        if k > 0:
            hop(k - 1).wait()
            value = small_in[k - 1, 0] + small_in[k - 1, 1]
            if k == len(hops):
                small[...] = value
                return
            small_in[k, 0] = value
        hop(k).start()

    due(10 + planned)


def adam_math(w, f, s, grad, rate, decay):
    first_new = beta_first * f + (1.0 - beta_first) * grad
    second_new = beta_second * s + (1.0 - beta_second) * grad * grad
    fix_first = 1.0 - beta_first**STEP
    fix_second = 1.0 - beta_second**STEP
    update = first_new * (1.0 / fix_first) / (jnp.sqrt(second_new * (1.0 / fix_second)) + adam_epsilon)
    return w - rate * (update + decay * w), first_new, second_new


def adam_kernel(columns, info, *refs):
    (w, f, s, wd, fd, sd, wv, fv, sv, small, d0, d1, u0, u1, go, g1, g2) = refs[:17]
    mats, downs, vecs = refs[17:21], refs[21:25], refs[25:29]
    step = pl.program_id(0)

    def put(outs, state, grad, rate, decay):
        new, first, second = adam_math(*(one[...] for one in state), grad, rate, decay)
        for out, value in zip(outs, (new, first, second, new.astype(bf16))):
            out[...] = value

    def when(lowest, count, *parts):
        @pl.when((step >= lowest) & (step < lowest + count))
        def _():
            grad = jnp.concatenate([part[h] for h in range(2) for part in parts], axis=1)
            put(mats, (w, f, s), grad.astype(f32), rate_matrix, weight_decay)

    when(0, 2, g1)
    when(2, 1, g2)
    when(3, 1, go)
    when(4, 4, u0, u1)
    for k, part in ((0, d0), (1, d1)):

        @pl.when((step >= columns) & ((step - columns) % 2 == k))
        def _():
            put(downs, (wd, fd, sd), part[0].astype(f32), rate_matrix, weight_decay)

    @pl.when(step == 0)
    def _():
        size = wv.shape[1]
        grad = small[0:12, pl.ds(pl.multiple_of(info[0] * size, size), size)]
        put(vecs, (wv, fv, sv), grad, rate_vector, 0.0)


def adam_call(group, mats, downs, vecs, small, grads):
    deep, wide = mats[0].shape
    tile = downs[0].shape[1]
    columns, rest = wide // tile, downs[0].shape[0] // deep
    clip = lambda value, most: jnp.clip(value, 0, most - 1)
    block = (deep, tile)
    mat = pl.BlockSpec(block, lambda i, info: (0, clip(i, columns)))
    row = lambda i: clip(i - columns, rest)
    down = pl.BlockSpec(block, lambda i, info: (row(i), 0))
    vec = pl.BlockSpec(vecs[0].shape, lambda i, info: (0, 0))
    small_spec = pl.BlockSpec(small.shape, lambda i, info: (0, 0))
    down_grad = pl.BlockSpec((1, *block), lambda i, info: (row(i) // 2, 0, 0))
    halves = lambda start, count, width: pl.BlockSpec((2, deep, width), lambda i, info: (0, 0, clip(i - start, count)))
    shapes = []
    for state in (mats, downs, vecs):
        shapes += [sds(state[0].shape, f32)] * 3 + [sds(state[0].shape, bf16)]
    size = sum(one[0].size for one in (mats, downs))
    return pl.pallas_call(
        functools.partial(adam_kernel, columns),
        grid_spec=pltpu.PrefetchScalarGridSpec(
            num_scalar_prefetch=1,
            grid=(columns + rest,),
            in_specs=[mat] * 3 + [down] * 3 + [vec] * 3 + [small_spec] + [down_grad] * 2
            + [halves(4, 4, tile // 4)] * 2 + [halves(3, 1, tile // 2), halves(0, 2, tile // 2), halves(2, 1, tile // 2)],
            out_specs=[mat] * 4 + [down] * 4 + [vec] * 4,
        ),
        out_shape=shapes,
        compiler_params=params(60),
        cost_estimate=cost(20 * size, 28 * size),
    )(group, *mats, *downs, *vecs, small, *grads)


def local(groups, replicas, *args):
    tokens, keep, cot, mats, down, vectors, f_mats, f_down, f_vectors, s_mats, s_down, s_vectors = args
    seqs, length, d = tokens.shape
    image = keep.shape[1]
    buf = length - image
    rows = -(-(buf + KEEP_MAX) // 16) * 16
    total = seqs * rows
    half = d // 2
    group = lax.axis_index("group")
    counts = (buf + jnp.sum(keep, axis=1)).astype(jnp.int32)

    keep3 = keep.reshape(seqs, 1, image)
    deep = mats.shape[0]
    w_attn, w_up, w_down, own_down, x, em, h1, qkv, o, r, h2, vec, stats = pl.pallas_call(
        functools.partial(attend_kernel, seqs, buf),
        in_specs=[SMEM_SPEC] + [VMEM_SPEC] * 2 + [ANY_SPEC] * 4,
        out_specs=[ANY_SPEC] * 11 + [VMEM_SPEC] * 2,
        out_shape=[
            sds((2, d, 2 * d), bf16),
            sds((2, d, 2 * d), bf16),
            sds((2, d, d), bf16),
            sds((deep, d), bf16),
            sds((total, d), bf16),
            sds((total, d), bf16),
            sds((total, d), bf16),
            sds((total, 3 * d), bf16),
            sds((total, d), bf16),
            sds((total, d), f32),
            sds((total, d), bf16),
            sds((16, d), f32),
            sds((8, d), f32),
        ],
        scratch_shapes=[
            pltpu.VMEM((total, d), bf16),
            pltpu.VMEM((total, d), bf16),
            pltpu.VMEM((total, d), bf16),
            pltpu.VMEM((total, 3 * d), bf16),
            pltpu.VMEM((total, d), bf16),
            pltpu.VMEM((total, d), f32),
            pltpu.VMEM((total, d), bf16),
            pltpu.SemaphoreType.DMA((7,)),
            pltpu.VMEM((2, d, 2 * d), bf16),
            pltpu.VMEM((2, deep, 2 * d), f32),
            pltpu.VMEM((half, d), f32),
            pltpu.VMEM((2, deep, d), bf16),
            pltpu.VMEM((2, deep, d), bf16),
            pltpu.VMEM((2, seqs, length, d), bf16),
            pltpu.VMEM((4, 16, d // 4), bf16),
            pltpu.SemaphoreType.DMA((7, 10)),
            pltpu.SemaphoreType.DMA((7, 10)),
            pltpu.SemaphoreType.DMA((3,)),
            pltpu.SemaphoreType.DMA((3,)),
            pltpu.SemaphoreType.DMA((9,)),
            pltpu.SemaphoreType.DMA((5,)),
            pltpu.SemaphoreType.DMA((2, seqs)),
        ],
        compiler_params=params(60, collective_id=0, has_side_effects=True),
        cost_estimate=cost(2 * total * 4 * d * d * 4, 20 * total * d),
    )(counts, keep3, vectors, mats, down, tokens, cot)
    quarter = d // 4
    sums_feed, er, ea, block_output, part_sum, z_mine, z_got, u_mine, u_got, h2_got, em_got = pl.pallas_call(
        functools.partial(feed_kernel, seqs, buf),
        in_specs=[SMEM_SPEC] + [VMEM_SPEC] * 4 + [ANY_SPEC] * 6,
        out_specs=[VMEM_SPEC] + [ANY_SPEC] * 10,
        out_shape=[
            sds((16, d), f32),
            sds((total, d), f32),
            sds((total, d), bf16),
            sds((seqs, length, d), bf16),
            sds((quarter, d), bf16),
            sds((total, d), bf16),
            sds((total, d), bf16),
            sds((2, total, d), bf16),
            sds((2, total, d), bf16),
            sds((total, d), bf16),
            sds((total, d), bf16),
        ],
        scratch_shapes=[
            pltpu.VMEM((total, d), f32),
            pltpu.VMEM((total, d), f32),
            pltpu.VMEM((total, d), bf16),
            pltpu.VMEM((seqs, length, d), bf16),
            pltpu.VMEM((2, d, 2 * d), bf16),
            pltpu.VMEM((2, 2, d, d), bf16),
            pltpu.VMEM((total, d), f32),
            pltpu.VMEM((total, d), f32),
            pltpu.VMEM((2, 2, total, d), bf16),
            pltpu.VMEM((2, 2, total, d), bf16),
            pltpu.VMEM((2, 2 * total, d), bf16),
            pltpu.VMEM((4, quarter, d), bf16),
            pltpu.VMEM((2, quarter, d), bf16),
            pltpu.VMEM((quarter, d), bf16),
            pltpu.SemaphoreType.DMA((5,)),
            pltpu.SemaphoreType.DMA((8, 2)),
            pltpu.SemaphoreType.DMA((seqs, 3)),
            pltpu.SemaphoreType.DMA((2,)),
            pltpu.SemaphoreType.DMA((2,)),
            pltpu.SemaphoreType.DMA((10,)),
            pltpu.SemaphoreType.DMA((10,)),
            pltpu.SemaphoreType.DMA((8, 2)),
            pltpu.SemaphoreType.DMA((8, 2)),
            pltpu.SemaphoreType.DMA((8, 2)),
            pltpu.SemaphoreType.DMA((7,)),
            pltpu.SemaphoreType.DMA((7,)),
        ],
        compiler_params=params(61, collective_id=1, has_side_effects=True),
        cost_estimate=cost(2 * total * 16 * d * d, 60 * total * d),
    )(counts, keep3, h2, em, vec, h2, em, r, w_up, w_down, own_down)

    bits = []
    while (4 << len(bits)) < replicas:
        bits.append(4 << len(bits))
    sizes = (d, d, d, d, half, d, half)
    chunks, steps = len(sizes), 7 + len(bits)
    found = pl.pallas_call(
        functools.partial(tail_kernel, seqs, buf, tuple(bits), sizes),
        in_specs=[SMEM_SPEC] + [VMEM_SPEC] * 4 + [ANY_SPEC] * 16,
        out_specs=[VMEM_SPEC, ANY_SPEC] + [ANY_SPEC] * (chunks + 4),
        out_shape=[sds((16, d), f32), sds((seqs, length, d), f32)]
        + [sds((2, quarter, wide), bf16) for wide in sizes]
        + [sds((total, d), bf16)] * 3
        + [sds((total, 3 * half), bf16)],
        scratch_shapes=[
            pltpu.VMEM((total, 3 * d), bf16),
            pltpu.VMEM((total, d), bf16),
            pltpu.VMEM((total, d), f32),
            pltpu.SemaphoreType.DMA((3,)),
            pltpu.VMEM((2, d, 3 * half), bf16),
            pltpu.VMEM((total, d), bf16),
            pltpu.VMEM((2, total, 3 * half), bf16),
            pltpu.VMEM((total, d), f32),
            pltpu.VMEM((length, d), f32),
            pltpu.VMEM((2, 2, 2 * total, d), bf16),
            pltpu.VMEM((4 + len(bits), 2, 16, d), f32),
        ]
        + [pltpu.VMEM((4, quarter, wide), bf16) for wide in sizes]
        + [pltpu.VMEM((2, quarter, wide), bf16) for wide in sizes]
        + [pltpu.VMEM((quarter, wide), bf16) for wide in sizes]
        + [pltpu.VMEM((quarter // 2, wide), bf16) for wide in sizes]
        + [pltpu.VMEM((len(bits), quarter // 2, wide), bf16) for wide in sizes]
        + [
            pltpu.SemaphoreType.DMA((chunks, steps + 1)),
            pltpu.SemaphoreType.DMA((chunks, steps)),
            pltpu.SemaphoreType.DMA(()),
            pltpu.SemaphoreType.DMA(()),
            pltpu.SemaphoreType.DMA(()),
            pltpu.SemaphoreType.DMA((2, 2, 2)),
            pltpu.SemaphoreType.DMA(()),
            pltpu.SemaphoreType.DMA((4,)),
            pltpu.SemaphoreType.DMA((4,)),
            pltpu.SemaphoreType.DMA((4 + len(bits),)),
            pltpu.SemaphoreType.DMA((4 + len(bits),)),
        ],
        compiler_params=params(61, collective_id=2, has_side_effects=True),
        cost_estimate=cost(2 * total * 16 * d * d, 100 * total * d),
    )(counts, keep3, vec, stats, sums_feed, qkv, x, er, part_sum, z_mine, z_got, em, em_got, h2, h2_got, u_mine, u_got, o, ea, h1, w_attn)
    small, input_grad = found[:2]
    grads = found[2 : 2 + chunks]
    branch_rms = jnp.sqrt(small[12, 0:3] / (small[12, 3] * d))
    new = adam_call(
        group.astype(jnp.int32).reshape(1),
        (mats, f_mats, s_mats),
        (down, f_down, s_down),
        (vectors, f_vectors, s_vectors),
        small,
        grads,
    )
    by_kind = [new[4 * part + kind] for kind in range(4) for part in range(3)]
    return (block_output, input_grad, *by_kind, branch_rms)


def solution(mesh):
    rows, owned, columns = P(BOTH, None, None), P("group", None), P(None, "group")
    state = (owned, owned, columns)
    return jax.shard_map(
        functools.partial(local, mesh.shape["group"], mesh.shape["dp"]),
        mesh=mesh,
        in_specs=(rows, P(BOTH, None), rows) + state * 3,
        out_specs=(rows, rows) + state * 4 + (P(),),
        check_vma=False,
    )
```

```python
import functools
import math

import jax
import jax.numpy as jnp
from jax import lax
from jax.experimental import pallas as pl
from jax.experimental.pallas import tpu as pltpu
from jax.sharding import PartitionSpec as P

HEAD = 64
STEP = 7
KEEP_MAX = 77

norm_epsilon = 1e-06
beta_first = 0.5
beta_second = 0.5
adam_epsilon = 1e-08
rate_matrix = 0.05
rate_vector = 0.3
weight_decay = 0.05
root_half = 0.7071067811865476
inverse_root_two_pi = 0.3989422804014327

bf16 = jnp.bfloat16
f32 = jnp.float32
BOTH = ("group", "dp")
VMEM_SPEC = pl.BlockSpec(memory_space=pltpu.VMEM)
ANY_SPEC = pl.BlockSpec(memory_space=pl.ANY)
MIB = 1 << 20
GATHER = dict(attn=3.0, up=18.0, up_gap=10.0, down=38.0, two=2.0, third=4.0, near=4.5, four=6.0, five=8.0, loop=23.5, gap=0.9)
FEED = (4, 6, 7, 9, 10, 15)
TAIL = {
    0: ((0, 2), (1, -1), (1, 0)),
    2: ((2, -1),),
    3: ((1, 1), (3, -1)),
    4: ((3, 0),),
    6: ((4, -1),),
    7: ((2, 0),),
    11: ((0, 3), (1, 2)),
    21: ((3, 1),),
    26: ((1, 3), (0, 4)),
    30: ((2, 1),),
    34: ((5, -1), (5, 0)),
    35: ((3, 2),),
    40: ((2, 2),),
    41: ((3, 3), (5, 1), (1, 4)),
    42: ((4, 0), (6, -1), (5, 2), (2, 3), (9, 10), (3, 4), (6, 0), (4, 1), (5, 3), (6, 1), (2, 4), (9, 11), (0, 5), (6, 2), (5, 4), (1, 5), (6, 3), (4, 2), (3, 5), (9, 12), (4, 3), (9, 13), (2, 5), (6, 4), (9, 14), (5, 5), (2, 6), (9, 15), (4, 4), (9, 16), (0, 6), (5, 6), (6, 5), (4, 5), (4, 6), (1, 6), (3, 6), (6, 6)),
}


def mm(a, b):
    return jnp.dot(a, b, preferred_element_type=f32)


def mm_nt(a, b):
    return lax.dot_general(a, b, (((1,), (1,)), ((), ())), preferred_element_type=f32)


def mm_tn(a, b):
    return lax.dot_general(a, b, (((0,), (0,)), ((), ())), preferred_element_type=f32)


def sds(shape, dtype):
    return jax.ShapeDtypeStruct(shape, dtype)


def params(mib, **more):
    return pltpu.CompilerParams(vmem_limit_bytes=mib * MIB, **more)


def cost(flops, nbytes):
    return pl.CostEstimate(flops=int(flops), bytes_accessed=int(nbytes), transcendentals=0)


def layer_stats(values):
    centre = jnp.mean(values, axis=-1, keepdims=True)
    centred = values - centre
    variance = jnp.mean(centred * centred, axis=-1, keepdims=True)
    inverse = lax.rsqrt(variance + norm_epsilon)
    return centred * inverse, inverse


def norm_back(grad_normed, normal, inverse, gain):
    scaled = grad_normed * gain
    mean_one = jnp.mean(scaled, axis=-1, keepdims=True)
    mean_two = jnp.mean(scaled * normal, axis=-1, keepdims=True)
    return inverse * (scaled - mean_one - normal * mean_two)


def picker(keep_row, rows):
    image = keep_row.shape[1]
    ahead = lax.broadcasted_iota(jnp.int32, (image, image), 0)
    here = lax.broadcasted_iota(jnp.int32, (image, image), 1)
    upper = jnp.where(ahead <= here, 1.0, 0.0).astype(bf16)
    kept = keep_row.astype(f32)
    place = mm(kept.astype(bf16), upper) - 1.0
    place = jnp.where(kept > 0.5, place, -1.0)
    want = lax.broadcasted_iota(jnp.int32, (rows, image), 0).astype(f32)
    return jnp.where(place == want, 1.0, 0.0).astype(bf16)


MESH = pl.DeviceIdType.MESH


def flip(value, bit):
    return value + bit - 2 * bit * ((value // bit) % 2)


class Place:
    def __init__(self):
        self.group, self.replica = lax.axis_index("group"), lax.axis_index("dp")
        self.core, self.level = self.replica % 2, (self.replica // 2) % 2
        self.inner = (self.level + self.replica // 4) % 2
        one, two = flip(self.group, 1), flip(self.group, 2)
        self.first = (1 - self.core) * one + self.core * two
        self.second = (1 - self.core) * two + self.core * one
        self.third = flip(one, 2)
        self.to_first = (self.first, self.replica)
        self.to_second = (self.second, self.replica)
        self.to_third = (self.third, self.replica)
        self.to_core = (self.group, flip(self.replica, 1))

    @property
    def to_middle(self):
        return (self.group, flip(flip(self.replica, 2), 4))

    def to_bit(self, bit):
        return (self.group, flip(self.replica, bit))

    def meet(self, partners):
        barrier = pltpu.get_barrier_semaphore()
        for partner in partners:
            pl.semaphore_signal(barrier, inc=1, device_id=partner, device_id_type=MESH)
        pl.semaphore_wait(barrier, len(partners))


class Timeline:
    def __init__(self):
        self.steps = []

    def add(self, when, step):
        self.steps.append((when, len(self.steps), step))
        self.steps.sort(key=lambda one: one[:2])

    def until(self, when):
        while self.steps and self.steps[0][0] <= when:
            self.steps.pop(0)[2]()

    def during(self, count, start, gap):
        due = []
        while self.steps and self.steps[0][0] < start + count * gap:
            when, _, step = self.steps.pop(0)
            due.append((min(max(int((when - start) / gap), 0), count - 1), step))

        def run(turn):
            for at, step in due:
                pl.when(turn == at)(step)

        return run


class Gather:
    def __init__(self, place, own, full, cols, send, recv):
        self.place, self.own, self.full, self.cols, self.send, self.recv = place, own, full, cols, send, recv
        deep = own.shape[0]
        self.deep, self.strip = deep, 5 * deep // 16
        self.main = deep - self.strip
        self.main_at = place.level * self.strip
        self.strip_at = place.level * self.main

    def block(self, owner, start, size, core=None):
        at = pl.multiple_of(owner * self.deep + start, 16)
        return self.full.at[self.place.core if core is None else core, pl.ds(at, size), self.cols]

    def whole(self, owner, core=None):
        return self.block(owner, 0, self.deep, core)

    def copy(self, k):
        p = self.place
        main, strip, whole = (self.main_at, self.main), (self.strip_at, self.strip), (0, self.deep)
        owner, (at, size), device = (
            (p.group, main, p.to_first),
            (p.group, main, p.to_second),
            (p.first, main, p.to_second),
            (p.first, strip, p.to_bit(2)),
            (p.second, strip, p.to_bit(2)),
            (p.third, strip, p.to_bit(2)),
            (p.group, whole, p.to_core),
            (p.first, whole, p.to_core),
            (p.second, whole, p.to_core),
            (p.third, whole, p.to_core),
        )[k]
        dst = self.block(owner, at, size)
        src = dst
        if k in (0, 1, 6):
            src = self.own.at[pl.ds(pl.multiple_of(at, 16) if k < 6 else 0, size), :]
        return pltpu.make_async_remote_copy(
            src_ref=src, dst_ref=dst, send_sem=self.send.at[k], recv_sem=self.recv.at[k],
            device_id=device, device_id_type=MESH,
        )

    def start(self, *ks):
        for k in ks:
            self.copy(k).start()

    def arrived(self, *ks):
        for k in ks:
            self.copy(k).wait_recv()

    def sent(self, *ks):
        for k in ks:
            self.copy(k).wait_send()

    def step_one(self):
        self.start(0, 1, 6)

    def step_two(self):
        self.arrived(0)
        self.start(2, 3)
        self.arrived(1)
        self.start(4)

    def step_near(self):
        self.arrived(3)
        self.start(7)
        self.arrived(4)
        self.start(8)

    def step_third(self):
        self.arrived(2)
        self.start(5)

    def step_four(self):
        self.arrived(5)
        self.start(9)

    def step_five(self):
        self.arrived(6, 7, 8, 9)
        self.sent(*range(10))

    def schedule(self, line, start, size):
        line.add(start, self.step_one)
        line.add(start + 8 * size + GATHER["two"], self.step_two)
        line.add(start + 12 * size + GATHER["third"], self.step_third)
        line.add(start + 14 * size + GATHER["near"], self.step_near)
        line.add(start + 16 * size + GATHER["four"], self.step_four)
        line.add(start + 17 * size + GATHER["five"], self.step_five)


def head_masks():
    lane = lax.broadcasted_iota(jnp.int32, (1, 2 * HEAD), 1)
    low = jnp.where(lane < HEAD, 1.0, 0.0)
    return low.astype(bf16), (1.0 - low).astype(bf16), low > 0.5


def two_heads(x, low, high):
    return jnp.concatenate([x * low, x * high], axis=0)


def pick_heads(both, first):
    rows = both.shape[0] // 2
    return jnp.where(first, both[:rows], both[rows:])


def pair_probs(q_pair, k_pair, counts, n):
    raw = mm_nt(q_pair, k_pair) * (1.0 / math.sqrt(HEAD))
    col = lax.broadcasted_iota(jnp.int32, raw.shape, 1)
    raw = jnp.where(col < counts[pl.ds(n, 1), :][:, 0 : raw.shape[1]], raw, -1e30)
    top = jnp.max(raw, axis=-1, keepdims=True)
    exponent = jnp.exp(raw - top)
    return exponent / jnp.sum(exponent, axis=-1, keepdims=True)


def attend_kernel(seqs, buf, *refs):
    keep, vectors, mats, down, tokens, cot = refs[:6]
    w_attn, w_up, w_down, own_down, x_out, em_out, h1_out, qkv_out, o_out, r_out, h2_out, vec, stats, counts = refs[6:20]
    x, em, h1, qkv, o, r, h2, outs, wbuf, wide, tall, low_up, low_down, rows_in, parts, send, recv, vec_send, vec_recv, loads, stores, reads = refs[20:]
    rows = h1.shape[0] // seqs
    d = h1.shape[1]
    half = d // 2
    place = Place()
    core = place.core
    deep = mats.shape[0]

    takes = []
    for j in range(8):
        at = pl.ds(pl.multiple_of((2 * j + core) * half, half), half)
        takes.append(
            pltpu.make_async_copy(mats.at[:, at], wide.at[j // 4, :, pl.ds((j % 4) * half, half)], loads.at[j])
        )
    takes.append(
        pltpu.make_async_copy(down.at[pl.ds(pl.multiple_of(core * half, half), half), :], tall, loads.at[8])
    )
    for one in takes:
        one.start()
    reads_in = []
    for n in range(seqs):
        for k, src in enumerate((tokens, cot)):
            reads_in.append(pltpu.make_async_copy(src.at[n], rows_in.at[k, n], reads.at[k, n]))
    for one in reads_in:
        one.start()

    place.meet((place.to_first, place.to_second, place.to_third, place.to_core, place.to_bit(2)))

    part = vectors.shape[1]
    parts[place.group] = jnp.concatenate([vectors[...], jnp.zeros((4, part), f32)], axis=0).astype(bf16)
    for k, partner in enumerate((place.to_first, place.to_second, place.to_third)):
        pltpu.make_async_remote_copy(
            src_ref=parts.at[place.group], dst_ref=parts.at[place.group],
            send_sem=vec_send.at[k], recv_sem=vec_recv.at[k], device_id=partner, device_id_type=MESH,
        ).start()

    own_rows = pl.ds(pl.multiple_of(place.group * deep, deep), deep)
    line = Timeline()
    attn = []
    for j in range(4):
        cols = pl.ds(j * half, half)
        own = wbuf.at[core, own_rows, cols]
        takes[j].wait()
        own[...] = wide[0, :, cols].astype(bf16)
        attn.append(Gather(place, own, wbuf, cols, send.at[j], recv.at[j]))
        attn[j].schedule(line, GATHER["attn"] * j, 0.5)
        if j == 0:
            line.until(0)
    ups = []
    for j in range(2):
        cols = pl.ds(j * d, d)
        for one in takes[4 + 2 * j : 6 + 2 * j]:
            one.wait()
        low_up[j] = wide[1, :, cols].astype(bf16)
        ups.append(Gather(place, low_up.at[j], w_up, cols, send.at[4 + j], recv.at[4 + j]))
        ups[j].schedule(line, GATHER["up"] + GATHER["up_gap"] * j, 1.0)
    takes[8].wait()
    for j in range(2):
        low_down[j] = tall[j * deep : (j + 1) * deep, :].astype(bf16)
    early = Gather(place, low_down.at[0], w_down, pl.ds(0, d), send.at[6], recv.at[6])
    early.schedule(line, GATHER["down"], 1.0)
    keeps = [
        pltpu.make_async_copy(one.own, one.whole(place.group), stores.at[k]) for k, one in enumerate(ups + [early])
    ]
    keeps.append(pltpu.make_async_copy(low_down.at[1], own_down, stores.at[3]))
    for one in keeps:
        one.start()

    def keep_out(k, src, dst):
        one = pltpu.make_async_copy(src, dst, outs.at[k])
        one.start()
        keeps.append(one)

    kept = jnp.sum(keep[...], axis=1, keepdims=True) + buf
    counts[0:seqs, :] = jnp.broadcast_to(kept, keep.shape)
    counts[2 * seqs : 3 * seqs, :] = keep[...]

    for one in reads_in:
        one.wait()
    due_pack = line.during(seqs, 4.0, 1.0)

    @pl.loop(0, seqs)
    def _(n):
        due_pack(n)
        at = pl.multiple_of(n * rows, 16)
        pick = picker(counts[pl.ds(2 * seqs + n, 1), :], rows - buf)
        for k, dst in ((0, x), (1, em)):
            dst[pl.ds(at, buf), :] = rows_in[k, n, 0:buf, :]
            dst[pl.ds(pl.multiple_of(at + buf, 16), rows - buf), :] = mm(pick, rows_in[k, n, buf:, :]).astype(bf16)

    for k in range(3):
        pltpu.make_async_remote_copy(
            src_ref=parts.at[place.group], dst_ref=parts.at[place.group],
            send_sem=vec_send.at[k], recv_sem=vec_recv.at[k], device_id=place.to_first, device_id_type=MESH,
        ).wait()
    vec[...] = jnp.zeros_like(vec)
    for s in range(4):
        vec[:, s * part : (s + 1) * part] = parts[s].astype(f32)
    due_norm = line.during(seqs, 8.0, 0.7)

    @pl.loop(0, seqs)
    def _(n):
        due_norm(n)
        at = pl.ds(pl.multiple_of(n * rows, 16), rows)
        normal, _ = layer_stats(x[at, :].astype(f32))
        h1[at, :] = (normal * vec[0:1, :] + vec[1:2, :]).astype(bf16)

    keep_out(0, x, x_out)
    keep_out(1, em, em_out)
    keep_out(2, h1, h1_out)
    tile = half // 2
    for j in range(3):
        line.until(GATHER["attn"] * j + 17 * 0.5 + GATHER["five"])

        @pl.loop(0, 4)
        def _(i):
            h, t = i // 2, i % 2
            near = pl.multiple_of(i * tile, tile)
            w = wbuf[h, :, pl.ds(pl.multiple_of(j * half + t * tile, tile), tile)]
            got = mm(h1[...], w)
            if j != 1:
                got = got + vec[2 + j // 2 : 3 + j // 2, pl.ds(near, tile)]
            qkv[:, pl.ds(pl.multiple_of(j * d + near, tile), tile)] = got.astype(bf16)

    keep_out(3, qkv, qkv_out)
    low, high, first = head_masks()
    pairs = d // (2 * HEAD)
    loop_at, turn = GATHER["loop"], GATHER["gap"]
    due = line.during(seqs * pairs, loop_at, turn)
    mix_at = loop_at + seqs * pairs * turn

    @pl.loop(0, seqs * pairs)
    def _(i):
        due(i)
        n, j = i // pairs, i % pairs
        at = pl.ds(pl.multiple_of(n * rows, 16), rows)
        lanes = [pl.ds(pl.multiple_of(j * 2 * HEAD + m * d, 2 * HEAD), 2 * HEAD) for m in range(3)]
        q_pair = two_heads(qkv[at, lanes[0]], low, high)
        probs = pair_probs(q_pair, qkv[at, lanes[1]], counts, n).astype(bf16)
        o[at, lanes[0]] = pick_heads(mm(probs, qkv[at, lanes[2]]), first).astype(bf16)

    keep_attn = pltpu.make_async_copy(wbuf, w_attn, stores.at[4])
    keep_attn.start()
    keep_out(4, o, o_out)
    due_mix = line.during(4, mix_at, 1.0)

    @pl.loop(0, 4)
    def _(i):
        due_mix(i)
        h, t = i // 2, i % 2
        near = pl.ds(pl.multiple_of(i * tile, tile), tile)
        w = wbuf[h, :, pl.ds(pl.multiple_of(3 * half + t * tile, tile), tile)]
        r[:, near] = mm(o[...], w) + vec[4:5, near]

    due_last = line.during(seqs, mix_at + 4, 1.5)
    stats[...] = jnp.zeros_like(stats)

    @pl.loop(0, seqs)
    def _(n):
        due_last(n)
        at = pl.ds(pl.multiple_of(n * rows, 16), rows)
        valid = lax.broadcasted_iota(jnp.int32, (rows, 1), 0) < counts[pl.ds(n, 1), :][:, 0:1]
        valid = jnp.where(valid, 1.0, 0.0)
        inputs = x[at, :].astype(f32)
        branch = r[at, :]
        resid = inputs + branch
        r[at, :] = resid
        normal, _ = layer_stats(resid)
        h2[at, :] = (normal * vec[5:6, :] + vec[6:7, :]).astype(bf16)
        stats[0:1, :] += jnp.sum(inputs * inputs * valid, axis=0, keepdims=True)
        stats[1:2, :] += jnp.sum(branch * branch * valid, axis=0, keepdims=True)

    keep_out(5, r, r_out)
    keep_out(6, h2, h2_out)
    line.until(1e9)
    for one in keeps:
        one.wait()
    keep_attn.wait()


class Reduce:
    def __init__(self, place, bits, g, r1, r2, r3, r4, far, total, send, recv, home=None):
        self.place, self.bits, self.g, self.r1, self.r2, self.r3, self.r4 = place, bits, g, r1, r2, r3, r4
        self.far, self.total, self.send, self.recv = far, total, send, recv
        self.home = place.group if home is None else home

    def copy(self, k):
        p = self.place
        plans = [
            lambda: (self.g.at[p.third], self.r1.at[1], p.to_first),
            lambda: (self.g.at[p.first], self.r1.at[0], p.to_first),
            lambda: (self.g.at[p.second], self.r2, p.to_second),
            lambda: (self.g.at[self.home], self.r3, p.to_bit(2)),
            lambda: (self.r2, self.total.at[p.core], p.to_bit(2)),
            lambda: (self.r2, self.total.at[p.core], p.to_core),
            lambda: (self.total.at[p.core], self.total.at[p.core], p.to_core),
            lambda: (self.r1.at[0], self.r4, p.to_middle),
        ]
        for n, bit in enumerate(self.bits):
            plans.append(lambda n=n, bit=bit: (self.far.at[n, 0], self.far.at[n, 1], p.to_bit(bit)))
        src, dst, device = plans[k]()
        return pltpu.make_async_remote_copy(
            src_ref=src, dst_ref=dst, send_sem=self.send.at[k], recv_sem=self.recv.at[k],
            device_id=device, device_id_type=MESH,
        )

    def begin(self):
        self.copy(0).start()
        self.copy(1).start()

    def sent(self, *ks):
        for k in ks:
            self.copy(k).wait_send()

    def pass_second(self):
        self.copy(0).wait_recv()
        at = self.place.second
        self.g[at] = (self.g[at].astype(f32) + self.r1[1].astype(f32)).astype(bf16)
        self.copy(2).start()

    def settle(self):
        self.copy(1).wait_recv()
        self.copy(2).wait_recv()
        at = self.place.group
        self.g[at] = (self.g[at].astype(f32) + self.r1[0].astype(f32) + self.r2[...].astype(f32)).astype(bf16)

    def pass_in(self):
        pl.when(self.place.inner == 0)(self.copy(3).start)

    def pass_middle(self):
        @pl.when(self.place.inner == 1)
        def _():
            self.copy(3).wait_recv()
            value = self.g[self.home].astype(f32) + self.r3[...].astype(f32)
            self.r1[0] = value.astype(bf16)
            self.copy(7).start()

    def pass_out(self):
        @pl.when(self.place.inner == 1)
        def _():
            self.copy(7).wait_recv()
            self.r2[...] = (self.r1[0].astype(f32) + self.r4[...].astype(f32)).astype(bf16)
            for n in range(len(self.bits)):
                pltpu.sync_copy(self.r2, self.far.at[n, 0])
                self.copy(8 + n).start()
                self.copy(8 + n).wait()
                pltpu.sync_copy(self.far.at[n, 1], self.r3)
                self.r2[...] = (self.r2[...].astype(f32) + self.r3[...].astype(f32)).astype(bf16)
            self.copy(4).start()
            self.copy(5).start()
            self.stay().start()

    def stay(self):
        return pltpu.make_async_copy(self.r2, self.total.at[self.place.core], self.send.at[8 + len(self.bits)])

    def pass_core(self):
        @pl.when(self.place.inner == 0)
        def _():
            self.copy(4).wait_recv()
            self.copy(6).start()

    def finish(self, whole=True):
        if whole:
            self.sent(0, 1, 2)

        @pl.when(self.place.inner == 1)
        def _():
            self.copy(5).wait_recv()
            self.sent(4, 5, 7)
            self.stay().wait()

        @pl.when(self.place.inner == 0)
        def _():
            self.copy(6).wait_recv()
            self.sent(3, 6)


def block_grads(place, sides, wide, g):
    quarter = sides.shape[2] // 4

    @pl.loop(0, 4)
    def _(i):
        near = place.first * (1 - i // 2) + place.group * (i // 2)
        over = ((i + 1) // 2) % 2
        owner = near * (1 - over) + ((1 - place.core) * flip(near, 2) + place.core * flip(near, 1)) * over
        cols = pl.ds(pl.multiple_of(owner * quarter, quarter), quarter)
        g[owner] = mm_tn(sides[0, :, cols], sides[1, :, 0:wide]).astype(bf16)


def swap_start(place, src, dst, send, recv, k):
    copy = pltpu.make_async_remote_copy(
        src_ref=src, dst_ref=dst, send_sem=send.at[k], recv_sem=recv.at[k],
        device_id=place.to_core, device_id_type=MESH,
    )
    copy.start()
    return copy


def feed_kernel(seqs, buf, *refs):
    counts, h2, em, vec, h2_hbm, em_hbm, r_hbm, ups, downs, own_down = refs[:10]
    sums, er_hbm, ea_hbm, out_hbm, part_sum, z_mine, z_got, u_mine, u_got, h2_got, em_got = refs[10:21]
    r, er, ea, out, wup, wdown, m_acc, t_acc, z_all, u_all, sides, g, r1, r2 = refs[21:35]
    sems, w_sems, o_sems, send, recv, g_send, g_recv, k_sems, t_send, t_recv, r_send, r_recv = refs[35:]
    total, d = h2.shape
    rows = total // seqs
    strip = wup.shape[2] // 4
    tile = strip // 2
    place = Place()
    core = place.core
    late = Gather(place, wdown.at[1, core, pl.ds(pl.multiple_of(place.group * tile, tile), tile)], wdown.at[1], pl.ds(0, d), g_send, g_recv)
    take_own = pltpu.make_async_copy(own_down, late.own, sems.at[0])
    take_own.start()
    take_r = pltpu.make_async_copy(r_hbm, r, sems.at[1])

    def owner_at(turn):
        near = place.group * (1 - turn % 2) + place.first * (turn % 2)
        over = turn // 2
        return near * (1 - over) + ((1 - core) * flip(near, 2) + core * flip(near, 1)) * over

    def takes(i):
        turn, away = i // 2, i % 2
        h = (1 - core) * away + core * (1 - away)
        s = owner_at(turn)
        cols = pl.ds(pl.multiple_of(s * strip, strip), strip)
        at = pl.ds(pl.multiple_of(s * tile, tile), tile)
        return [
            pltpu.make_async_copy(ups.at[h, :, cols], wup.at[h, :, cols], w_sems.at[i, 0]),
            pltpu.make_async_copy(downs.at[h, at], wdown.at[0, h, at], w_sems.at[i, 1]),
        ]

    for i in range(8):
        for one in takes(i):
            one.start()
    take_r.start()
    place.meet((place.to_core, place.to_second, place.to_first, place.to_bit(2)))
    take_own.wait()
    late.step_one()
    swaps = [
        swap_start(place, em_hbm, em_got, send, recv, 0),
        swap_start(place, h2_hbm, h2_got, send, recv, 1),
    ]
    reduce = Reduce(place, (), g, r1, r2, None, None, None, None, r_send, r_recv)
    sides[1, 0:total, :] = em[...]
    take_em = pltpu.make_async_copy(em_got, sides.at[1, pl.ds(total, total)], sems.at[4])
    sums[...] = jnp.zeros_like(sums)
    m_acc[...] = jnp.zeros_like(m_acc)
    t_acc[...] = jnp.zeros_like(t_acc)

    def tile_copies(k, s, t, away):
        cols = pl.ds(pl.multiple_of(s * tile, tile), tile)
        z_to = sides.at[0, pl.ds(0 if not away else total, total), cols] if t == 0 else (z_got if away else z_mine).at[:, cols]
        pairs = (
            (z_all.at[(1 - core) if away else core, t, :, cols], z_to),
            (u_all.at[(1 - core) if away else core, t, :, cols], (u_got if away else u_mine).at[t, :, cols]),
        )
        if not away:
            return [pltpu.make_async_copy(src, dst, k_sems.at[k, n]) for n, (src, dst) in enumerate(pairs)]
        return [
            pltpu.make_async_remote_copy(
                src_ref=src, dst_ref=dst, send_sem=t_send.at[k, n], recv_sem=t_recv.at[k, n],
                device_id=place.to_core, device_id_type=MESH,
            )
            for n, (src, dst) in enumerate(pairs)
        ]

    def late_own():
        late.arrived(6)

    def late_last():
        late.arrived(7, 8, 9)
        late.sent(*range(10))

    def begin():
        take_em.wait()
        for k in range(4):
            tile_copies(k, 0, 0, False)[0].wait()
            tile_copies(k, 0, 0, True)[0].wait()
        block_grads(place, sides, d, g)
        reduce.begin()

    due = [(2, swaps[0].wait), (7, late_own), (8, begin)]
    due += zip(FEED, (late.step_two, late.step_third, late.step_near, late.step_four, late_last, reduce.pass_second))
    orders = [[(when - 8 * t, step) for when, step in due if when // 8 == t] for t in range(2)]

    for t in range(2):

        @pl.loop(0, 8)
        def _(i):
            for when, step in orders[t]:
                pl.when(i == when)(step)
            if t == 0:
                pl.when(i == 2)(take_em.start)
                for one in takes(i):
                    one.wait()
            turn, away = i // 2, i % 2
            h = (1 - core) * away + core * (1 - away)
            s = owner_at(turn)
            cols = pl.ds(pl.multiple_of(s * strip + t * tile, tile), tile)
            far = (pl.ds(8 + s, 1), pl.ds(pl.multiple_of(h * strip + t * tile, tile), tile))
            near = pl.ds(pl.multiple_of(s * tile, tile), tile)
            w_up = wup[h, :, cols]
            w_down = wdown[t, h, near, :]
            u = mm(h2[...], w_up) + vec[far]
            phi = 0.5 * (1.0 + lax.erf(u * root_half))
            z = (u * phi).astype(bf16)
            z_all[h, t, :, near] = z
            slope = phi + u * jnp.exp(-0.5 * u * u) * inverse_root_two_pi
            eu = (mm_nt(em[...], w_down) * slope).astype(bf16)
            u_all[h, t, :, near] = eu
            m_acc[...] += mm(z, w_down)
            t_acc[...] += mm_nt(eu, w_up)
            sums[far] = jnp.sum(eu.astype(f32), axis=0, keepdims=True)
            for side in range(2):

                @pl.when(away == side)
                def _():
                    for one in tile_copies(4 * t + turn, s, t, side == 1):
                        one.start()

    take_r.wait()

    def results(n):
        at = pl.ds(pl.multiple_of(n * rows, 16), rows)
        return [
            pltpu.make_async_copy(er.at[at], er_hbm.at[at], o_sems.at[n, 0]),
            pltpu.make_async_copy(ea.at[at], ea_hbm.at[at], o_sems.at[n, 1]),
            pltpu.make_async_copy(out.at[n], out_hbm.at[n], o_sems.at[n, 2]),
        ]

    @pl.loop(0, seqs)
    def _(n):
        at = pl.ds(pl.multiple_of(n * rows, 16), rows)
        valid = lax.broadcasted_iota(jnp.int32, (rows, 1), 0) < counts[pl.ds(n, 1), :][:, 0:1]
        valid = jnp.where(valid, 1.0, 0.0)
        resid = r[at, :]
        m = m_acc[at, :] + vec[7:8, :]
        packed = ((resid + m) * valid).astype(bf16)
        out[n, 0:buf, :] = packed[0:buf]
        pick = picker(counts[pl.ds(2 * seqs + n, 1), :], rows - buf)
        out[n, buf:, :] = mm_tn(pick, packed[buf:]).astype(bf16)
        normal, inverse = layer_stats(resid)
        t = t_acc[at, :]
        low = em[at, :].astype(f32)
        back = low + norm_back(t, normal, inverse, vec[5:6, :])
        er[at, :] = back
        ea_low = back.astype(bf16)
        ea[at, :] = ea_low
        sums[4:5, :] += jnp.sum(ea_low.astype(f32), axis=0, keepdims=True)
        sums[5:6, :] += jnp.sum(t * normal, axis=0, keepdims=True)
        sums[6:7, :] += jnp.sum(t, axis=0, keepdims=True)
        sums[7:8, :] += jnp.sum(low, axis=0, keepdims=True)
        sums[12:13, :] += jnp.sum(m * m * valid, axis=0, keepdims=True)
        for one in results(n):
            one.start()
    reduce.settle()
    share = pltpu.make_async_copy(g.at[place.group], part_sum, sems.at[0])
    share.start()
    for n in range(seqs):
        for one in results(n):
            one.wait()
    swaps[1].wait()
    reduce.sent(0, 1, 2)
    share.wait()
    for k in range(8):
        for away in (False, True):
            for one in tile_copies(k, 0, k // 4, away)[0 if k >= 4 else 1 :]:
                one.wait()


def tail_kernel(seqs, buf, bits, sizes, *refs):
    counts, vec, stats, sums_feed, qkv_hbm, x_hbm, er_hbm = refs[:7]
    part_sum, z_mine, z_got, em, em_got, h2, h2_got, u_mine, u_got, o, ea, h1, w_attn = refs[7:20]
    chunks = len(sizes)
    small, out = refs[20:22]
    totals = refs[22 : 22 + chunks]
    o_got, ea_got, h1_got, e_got = refs[22 + chunks : 26 + chunks]
    outs = 26 + chunks + (chunks if bits else 0)
    far = refs[26 + chunks : outs] or [None] * chunks
    scratch = refs[outs:]
    qkv, er, in_sems = scratch[:3]
    scratch = scratch[3:]
    wbuf, eo, e, t_acc, stage, sides, small_in = scratch[:7]
    buffers = [scratch[7 + k * chunks : 7 + (k + 1) * chunks] for k in range(5)]
    send, recv, w_sem, ea_sem, first_sem, side_sems, stage_sem, swap_send, swap_recv, small_send, small_recv = scratch[7 + 5 * chunks :]
    total, d = eo.shape
    rows = total // seqs
    half, quarter = d // 2, d // 4
    place = Place()
    core = place.core

    o_weight = pltpu.make_async_copy(w_attn.at[:, :, pl.ds(3 * half, half)], wbuf.at[:, :, pl.ds(0, half)], w_sem)
    o_weight.start()
    ea_all = e.at[0, :, pl.ds(0, d)]
    take_ea = pltpu.make_async_copy(ea, ea_all, ea_sem)
    take_ea.start()

    mine_cols = pl.ds(pl.multiple_of(core * half, half), half)
    left = [None, (z_mine, z_got), (h2, h2_got), (h2, h2_got), (o, o_got), (h1, h1_got), (h1, h1_got)]
    right = [
        None, (em, em_got),
        (u_mine.at[0], u_got.at[0]), (u_mine.at[1], u_got.at[1]),
        (ea.at[:, mine_cols], ea_got.at[:, mine_cols]),
        (e.at[core, :, pl.ds(0, d)], e_got.at[:, pl.ds(0, d)]), (e.at[core, :, pl.ds(d, half)], e_got.at[:, pl.ds(d, half)]),
    ]

    def side_copies(k):
        found = []
        for side, pairs in enumerate((left, right)):
            wide = sizes[k] if side else d
            for which, src in enumerate(pairs[k]):
                dst = sides.at[k % 2, side, pl.ds(which * total, total), pl.ds(0, wide)]
                found.append(pltpu.make_async_copy(src, dst, side_sems.at[k % 2, side, which]))
        return found

    def load_sides(k):
        for one in side_copies(k):
            one.start()

    load_sides(1)
    load_sides(2)
    inputs = [
        pltpu.make_async_copy(src, dst, in_sems.at[k])
        for k, (src, dst) in enumerate(((qkv_hbm, qkv), (er_hbm, er)))
    ]
    for one in inputs:
        one.start()
    partners = [place.to_first, place.to_second, place.to_core, place.to_bit(2), place.to_bit(4), place.to_middle]
    partners += [place.to_bit(b) for b in bits]
    place.meet(partners)
    swaps = [
        swap_start(place, o, o_got, swap_send, swap_recv, 0),
        swap_start(place, ea, ea_got, swap_send, swap_recv, 1),
        swap_start(place, h1, h1_got, swap_send, swap_recv, 2),
    ]
    sent_e = pltpu.make_async_remote_copy(
        src_ref=e.at[1 - core], dst_ref=e_got, send_sem=swap_send.at[3], recv_sem=swap_recv.at[3],
        device_id=place.to_core, device_id_type=MESH,
    )
    reduces = [
        Reduce(place, bits, *(buffers[b][k] for b in range(5)), far[k], totals[k], send.at[k], recv.at[k], None if k else 0) for k in range(chunks)
    ]

    first_sum = pltpu.make_async_copy(part_sum, buffers[0][0].at[0], first_sem)
    first_sum.start()

    def gradient(k):
        for one in side_copies(k):
            one.wait()
        block_grads(place, sides.at[k % 2], sizes[k], reduces[k].g)

    def act(k, step):
        if k == 9:
            last = step == 16
            for n in range(step - 10, len(hops) + 1 if last else step - 9):
                small_step(n)
            return
        one = reduces[k]
        if step == -1:
            gradient(k)
            if k == 1:
                load_sides(3)
            if k == 2:
                for swap in swaps[:2]:
                    swap.wait()
                load_sides(4)
        elif step == 0:
            one.begin()
        elif step == 1:
            one.pass_second()
        elif step == 2:
            if k == 0:
                first_sum.wait()
            else:
                one.settle()
            one.pass_in()
        elif step == 3:
            one.pass_middle()
        elif step == 4:
            one.pass_out()
        elif step == 5:
            one.pass_core()
        else:
            one.finish(k > 0)

    def due(slot, turn=None, count=1):
        for n in range(count):
            steps = TAIL.get(slot + n, ())

            def run(steps=steps):
                for k, step in steps:
                    act(k, step)

            if turn is None:
                run()
            elif steps:
                pl.when(turn == n)(run)

    due(0)
    o_weight.wait()
    take_ea.wait()
    for one in inputs:
        one.wait()

    @pl.loop(0, 4)
    def _(s):
        near = pl.ds(pl.multiple_of(s * quarter, quarter), quarter)
        got = mm_nt(ea_all[:, 0:half], wbuf[0, near, 0:half]) + mm_nt(ea_all[:, half:], wbuf[1, near, 0:half])
        eo[:, near] = got.astype(bf16)

    in_weight = pltpu.make_async_copy(w_attn.at[:, :, pl.ds(0, 3 * half)], wbuf, w_sem)
    in_weight.start()
    low, high, first = head_masks()
    pairs = half // (2 * HEAD)
    scale = 1.0 / math.sqrt(HEAD)
    small[...] = jnp.zeros_like(small)
    turns = seqs * pairs

    planned = 32

    @pl.loop(0, 2 * turns)
    def _(i):
        pl.when(i == turns)(sent_e.start)
        due(1, i, planned)
        h = (1 - core) * (1 - i // turns) + core * (i // turns)
        n, j = (i % turns) // pairs, i % pairs
        at = pl.ds(pl.multiple_of(n * rows, 16), rows)
        far = h * half + j * 2 * HEAD
        lanes = [pl.ds(pl.multiple_of(far + m * d, 2 * HEAD), 2 * HEAD) for m in range(3)]
        k_pair = qkv[at, lanes[1]]
        q_both = two_heads(qkv[at, lanes[0]], low, high)
        probs = pair_probs(q_both, k_pair, counts, n)
        eo_both = two_heads(eo[at, lanes[0]], low, high)
        ep = mm_nt(eo_both, qkv[at, lanes[2]])
        inner = jnp.sum(probs * ep, axis=-1, keepdims=True)
        es = (probs * (ep - inner)).astype(bf16)
        ev = mm_tn(probs.astype(bf16), eo_both).astype(bf16)
        eq = (pick_heads(mm(es, k_pair), first) * scale).astype(bf16)
        ek = (mm_tn(es, q_both) * scale).astype(bf16)
        for m, value in enumerate((eq, ek, ev)):
            e[h, at, pl.ds(pl.multiple_of(m * half + j * 2 * HEAD, 2 * HEAD), 2 * HEAD)] = value
        small[2:3, lanes[0]] += jnp.sum(eq.astype(f32), axis=0, keepdims=True)
        small[3:4, lanes[0]] += jnp.sum(ev.astype(f32), axis=0, keepdims=True)

    due(1 + planned)
    take_x = pltpu.make_async_copy(x_hbm, eo, in_sems.at[2])
    take_x.start()
    x = eo
    sent_e.wait()
    swaps[2].wait()
    load_sides(5)
    load_sides(6)
    in_weight.wait()
    take_x.wait()
    @pl.loop(0, 4)
    def _(s):
        due(2 + planned, s, 4)
        near = pl.ds(pl.multiple_of(s * quarter, quarter), quarter)
        t_acc[:, near] = mm_nt(e[0], wbuf[0, near, :]) + mm_nt(e[1], wbuf[1, near, :])

    @pl.loop(0, seqs)
    def _(n):
        due(6 + planned, n, 4)
        at = pl.ds(pl.multiple_of(n * rows, 16), rows)
        normal, inverse = layer_stats(x[at, :].astype(f32))
        t = t_acc[at, :]
        grad = er[at, :] + norm_back(t, normal, inverse, vec[0:1, :])
        small[0:1, :] += jnp.sum(t * normal, axis=0, keepdims=True)
        small[1:2, :] += jnp.sum(t, axis=0, keepdims=True)
        write = pltpu.make_async_copy(stage, out.at[n], stage_sem)

        @pl.when(n > 0)
        def _():
            write.wait()

        stage[0:buf, :] = grad[0:buf]
        pick = picker(counts[pl.ds(2 * seqs + n, 1), :], rows - buf)
        rest = grad[buf:]
        top = rest.astype(bf16)
        rest = rest - top.astype(f32)
        middle = rest.astype(bf16)
        bottom = (rest - middle.astype(f32)).astype(bf16)
        stage[buf:, :] = mm_tn(pick, top) + mm_tn(pick, middle) + mm_tn(pick, bottom)
        write.start()

    pltpu.make_async_copy(stage, out.at[0], stage_sem).wait()

    small[4:12, :] = sums_feed[4:12, :]
    kept = jnp.sum(counts[0:seqs, 0:1], axis=0, keepdims=True)
    lane = lax.broadcasted_iota(jnp.int32, (1, d), 1)
    tally = jnp.where(lane == 3, kept.astype(f32), 0.0)
    for k, row in enumerate((stats[0:1, :], stats[1:2, :], sums_feed[12:13, :])):
        tally = tally + jnp.where(lane == k, jnp.sum(row, axis=1, keepdims=True), 0.0)
    small[12:13, :] = tally
    hops = [place.to_first, place.to_second] + [place.to_bit(b) for b in (1, 2, 4, *bits)]
    small_in[0, 0] = small[...]

    def hop(k):
        return pltpu.make_async_remote_copy(
            src_ref=small_in.at[k, 0], dst_ref=small_in.at[k, 1], send_sem=small_send.at[k], recv_sem=small_recv.at[k],
            device_id=hops[k], device_id_type=MESH,
        )

    def small_step(k):
        if k > 0:
            hop(k - 1).wait()
            value = small_in[k - 1, 0] + small_in[k - 1, 1]
            if k == len(hops):
                small[...] = value
                return
            small_in[k, 0] = value
        hop(k).start()

    due(10 + planned)


def adam_math(w, f, s, grad, rate, decay):
    first_new = beta_first * f + (1.0 - beta_first) * grad
    second_new = beta_second * s + (1.0 - beta_second) * grad * grad
    fix_first = 1.0 - beta_first**STEP
    fix_second = 1.0 - beta_second**STEP
    update = first_new * (1.0 / fix_first) / (jnp.sqrt(second_new * (1.0 / fix_second)) + adam_epsilon)
    return w - rate * (update + decay * w), first_new, second_new


def adam_kernel(columns, info, *refs):
    (w, f, s, wd, fd, sd, wv, fv, sv, small, d0, d1, u0, u1, go, g1, g2) = refs[:17]
    mats, downs, vecs = refs[17:21], refs[21:25], refs[25:29]
    step = pl.program_id(0)

    def put(outs, state, grad, rate, decay):
        new, first, second = adam_math(*(one[...] for one in state), grad, rate, decay)
        for out, value in zip(outs, (new, first, second, new.astype(bf16))):
            out[...] = value

    def when(lowest, count, *parts):
        @pl.when((step >= lowest) & (step < lowest + count))
        def _():
            grad = jnp.concatenate([part[h] for h in range(2) for part in parts], axis=1)
            put(mats, (w, f, s), grad.astype(f32), rate_matrix, weight_decay)

    when(0, 2, g1)
    when(2, 1, g2)
    when(3, 1, go)
    when(4, 4, u0, u1)
    for k, part in ((0, d0), (1, d1)):

        @pl.when((step >= columns) & ((step - columns) % 2 == k))
        def _():
            put(downs, (wd, fd, sd), part[0].astype(f32), rate_matrix, weight_decay)

    @pl.when(step == 0)
    def _():
        size = wv.shape[1]
        grad = small[0:12, pl.ds(pl.multiple_of(info[0] * size, size), size)]
        put(vecs, (wv, fv, sv), grad, rate_vector, 0.0)


def adam_call(group, mats, downs, vecs, small, grads):
    deep, wide = mats[0].shape
    tile = downs[0].shape[1]
    columns, rest = wide // tile, downs[0].shape[0] // deep
    clip = lambda value, most: jnp.clip(value, 0, most - 1)
    block = (deep, tile)
    mat = pl.BlockSpec(block, lambda i, info: (0, clip(i, columns)))
    row = lambda i: clip(i - columns, rest)
    down = pl.BlockSpec(block, lambda i, info: (row(i), 0))
    vec = pl.BlockSpec(vecs[0].shape, lambda i, info: (0, 0))
    small_spec = pl.BlockSpec(small.shape, lambda i, info: (0, 0))
    down_grad = pl.BlockSpec((1, *block), lambda i, info: (row(i) // 2, 0, 0))
    halves = lambda start, count, width: pl.BlockSpec((2, deep, width), lambda i, info: (0, 0, clip(i - start, count)))
    shapes = []
    for state in (mats, downs, vecs):
        shapes += [sds(state[0].shape, f32)] * 3 + [sds(state[0].shape, bf16)]
    size = sum(one[0].size for one in (mats, downs))
    return pl.pallas_call(
        functools.partial(adam_kernel, columns),
        grid_spec=pltpu.PrefetchScalarGridSpec(
            num_scalar_prefetch=1,
            grid=(columns + rest,),
            in_specs=[mat] * 3 + [down] * 3 + [vec] * 3 + [small_spec] + [down_grad] * 2
            + [halves(4, 4, tile // 4)] * 2 + [halves(3, 1, tile // 2), halves(0, 2, tile // 2), halves(2, 1, tile // 2)],
            out_specs=[mat] * 4 + [down] * 4 + [vec] * 4,
        ),
        out_shape=shapes,
        compiler_params=params(60),
        cost_estimate=cost(20 * size, 28 * size),
    )(group, *mats, *downs, *vecs, small, *grads)


def local(groups, replicas, *args):
    tokens, keep, cot, mats, down, vectors, f_mats, f_down, f_vectors, s_mats, s_down, s_vectors = args
    seqs, length, d = tokens.shape
    image = keep.shape[1]
    buf = length - image
    rows = -(-(buf + KEEP_MAX) // 16) * 16
    total = seqs * rows
    half = d // 2
    group = lax.axis_index("group")

    deep = mats.shape[0]
    w_attn, w_up, w_down, own_down, x, em, h1, qkv, o, r, h2, vec, stats, counts = pl.pallas_call(
        functools.partial(attend_kernel, seqs, buf),
        in_specs=[VMEM_SPEC] * 2 + [ANY_SPEC] * 4,
        out_specs=[ANY_SPEC] * 11 + [VMEM_SPEC] * 3,
        out_shape=[
            sds((2, d, 2 * d), bf16),
            sds((2, d, 2 * d), bf16),
            sds((2, d, d), bf16),
            sds((deep, d), bf16),
            sds((total, d), bf16),
            sds((total, d), bf16),
            sds((total, d), bf16),
            sds((total, 3 * d), bf16),
            sds((total, d), bf16),
            sds((total, d), f32),
            sds((total, d), bf16),
            sds((16, d), f32),
            sds((8, d), f32),
            sds((4 * seqs, image), jnp.int32),
        ],
        scratch_shapes=[
            pltpu.VMEM((total, d), bf16),
            pltpu.VMEM((total, d), bf16),
            pltpu.VMEM((total, d), bf16),
            pltpu.VMEM((total, 3 * d), bf16),
            pltpu.VMEM((total, d), bf16),
            pltpu.VMEM((total, d), f32),
            pltpu.VMEM((total, d), bf16),
            pltpu.SemaphoreType.DMA((7,)),
            pltpu.VMEM((2, d, 2 * d), bf16),
            pltpu.VMEM((2, deep, 2 * d), f32),
            pltpu.VMEM((half, d), f32),
            pltpu.VMEM((2, deep, d), bf16),
            pltpu.VMEM((2, deep, d), bf16),
            pltpu.VMEM((2, seqs, length, d), bf16),
            pltpu.VMEM((4, 16, d // 4), bf16),
            pltpu.SemaphoreType.DMA((7, 10)),
            pltpu.SemaphoreType.DMA((7, 10)),
            pltpu.SemaphoreType.DMA((3,)),
            pltpu.SemaphoreType.DMA((3,)),
            pltpu.SemaphoreType.DMA((9,)),
            pltpu.SemaphoreType.DMA((5,)),
            pltpu.SemaphoreType.DMA((2, seqs)),
        ],
        compiler_params=params(60, collective_id=0, has_side_effects=True),
        cost_estimate=cost(2 * total * 4 * d * d * 4, 20 * total * d),
    )(keep, vectors, mats, down, tokens, cot)
    quarter = d // 4
    sums_feed, er, ea, block_output, part_sum, z_mine, z_got, u_mine, u_got, h2_got, em_got = pl.pallas_call(
        functools.partial(feed_kernel, seqs, buf),
        in_specs=[VMEM_SPEC] * 4 + [ANY_SPEC] * 6,
        out_specs=[VMEM_SPEC] + [ANY_SPEC] * 10,
        out_shape=[
            sds((16, d), f32),
            sds((total, d), f32),
            sds((total, d), bf16),
            sds((seqs, length, d), bf16),
            sds((quarter, d), bf16),
            sds((total, d), bf16),
            sds((total, d), bf16),
            sds((2, total, d), bf16),
            sds((2, total, d), bf16),
            sds((total, d), bf16),
            sds((total, d), bf16),
        ],
        scratch_shapes=[
            pltpu.VMEM((total, d), f32),
            pltpu.VMEM((total, d), f32),
            pltpu.VMEM((total, d), bf16),
            pltpu.VMEM((seqs, length, d), bf16),
            pltpu.VMEM((2, d, 2 * d), bf16),
            pltpu.VMEM((2, 2, d, d), bf16),
            pltpu.VMEM((total, d), f32),
            pltpu.VMEM((total, d), f32),
            pltpu.VMEM((2, 2, total, d), bf16),
            pltpu.VMEM((2, 2, total, d), bf16),
            pltpu.VMEM((2, 2 * total, d), bf16),
            pltpu.VMEM((4, quarter, d), bf16),
            pltpu.VMEM((2, quarter, d), bf16),
            pltpu.VMEM((quarter, d), bf16),
            pltpu.SemaphoreType.DMA((5,)),
            pltpu.SemaphoreType.DMA((8, 2)),
            pltpu.SemaphoreType.DMA((seqs, 3)),
            pltpu.SemaphoreType.DMA((2,)),
            pltpu.SemaphoreType.DMA((2,)),
            pltpu.SemaphoreType.DMA((10,)),
            pltpu.SemaphoreType.DMA((10,)),
            pltpu.SemaphoreType.DMA((8, 2)),
            pltpu.SemaphoreType.DMA((8, 2)),
            pltpu.SemaphoreType.DMA((8, 2)),
            pltpu.SemaphoreType.DMA((7,)),
            pltpu.SemaphoreType.DMA((7,)),
        ],
        compiler_params=params(61, collective_id=1, has_side_effects=True),
        cost_estimate=cost(2 * total * 16 * d * d, 60 * total * d),
    )(counts, h2, em, vec, h2, em, r, w_up, w_down, own_down)

    bits = []
    while (8 << len(bits)) < replicas:
        bits.append(8 << len(bits))
    sizes = (d, d, d, d, half, d, half)
    chunks, steps = len(sizes), 8 + len(bits)
    found = pl.pallas_call(
        functools.partial(tail_kernel, seqs, buf, tuple(bits), sizes),
        in_specs=[VMEM_SPEC] * 4 + [ANY_SPEC] * 16,
        out_specs=[VMEM_SPEC, ANY_SPEC] + [ANY_SPEC] * (chunks + 4 + (chunks if bits else 0)),
        out_shape=[sds((16, d), f32), sds((seqs, length, d), f32)]
        + [sds((2, quarter, wide), bf16) for wide in sizes]
        + [sds((total, d), bf16)] * 3
        + [sds((total, 3 * half), bf16)]
        + [sds((len(bits), 2, quarter, wide), bf16) for wide in sizes if bits],
        scratch_shapes=[
            pltpu.VMEM((total, 3 * d), bf16),
            pltpu.VMEM((total, d), f32),
            pltpu.SemaphoreType.DMA((3,)),
            pltpu.VMEM((2, d, 3 * half), bf16),
            pltpu.VMEM((total, d), bf16),
            pltpu.VMEM((2, total, 3 * half), bf16),
            pltpu.VMEM((total, d), f32),
            pltpu.VMEM((length, d), f32),
            pltpu.VMEM((2, 2, 2 * total, d), bf16),
            pltpu.VMEM((5 + len(bits), 2, 16, d), f32),
        ]
        + [pltpu.VMEM((4 if k else 1, quarter, wide), bf16) for k, wide in enumerate(sizes)]
        + [pltpu.VMEM((2 if k else 1, quarter, wide), bf16) for k, wide in enumerate(sizes)]
        + [pltpu.VMEM((quarter, wide), bf16) for wide in sizes]
        + [pltpu.VMEM((quarter, wide), bf16) for wide in sizes] * 2
        + [
            pltpu.SemaphoreType.DMA((chunks, steps + 1)),
            pltpu.SemaphoreType.DMA((chunks, steps)),
            pltpu.SemaphoreType.DMA(()),
            pltpu.SemaphoreType.DMA(()),
            pltpu.SemaphoreType.DMA(()),
            pltpu.SemaphoreType.DMA((2, 2, 2)),
            pltpu.SemaphoreType.DMA(()),
            pltpu.SemaphoreType.DMA((4,)),
            pltpu.SemaphoreType.DMA((4,)),
            pltpu.SemaphoreType.DMA((5 + len(bits),)),
            pltpu.SemaphoreType.DMA((5 + len(bits),)),
        ],
        compiler_params=params(61, collective_id=2, has_side_effects=True),
        cost_estimate=cost(2 * total * 16 * d * d, 100 * total * d),
    )(counts, vec, stats, sums_feed, qkv, x, er, part_sum, z_mine, z_got, em, em_got, h2, h2_got, u_mine, u_got, o, ea, h1, w_attn)
    small, input_grad = found[:2]
    grads = found[2 : 2 + chunks]
    branch_rms = jnp.sqrt(small[12, 0:3] / (small[12, 3] * d))
    new = adam_call(
        group.astype(jnp.int32).reshape(1),
        (mats, f_mats, s_mats),
        (down, f_down, s_down),
        (vectors, f_vectors, s_vectors),
        small,
        grads,
    )
    by_kind = [new[4 * part + kind] for kind in range(4) for part in range(3)]
    return (block_output, input_grad, *by_kind, branch_rms)


def solution(mesh):
    rows, owned, columns = P(BOTH, None, None), P("group", None), P(None, "group")
    state = (owned, owned, columns)
    return jax.shard_map(
        functools.partial(local, mesh.shape["group"], mesh.shape["dp"]),
        mesh=mesh,
        in_specs=(rows, P(BOTH, None), rows) + state * 3,
        out_specs=(rows, rows) + state * 4 + (P(),),
        check_vma=False,
    )
```

```python
import functools
import math

import jax
import jax.numpy as jnp
from jax import lax
from jax.experimental import pallas as pl
from jax.experimental.pallas import tpu as pltpu
from jax.sharding import PartitionSpec as P

HEAD = 64
STEP = 7
KEEP_MAX = 77

norm_epsilon = 1e-06
beta_first = 0.5
beta_second = 0.5
adam_epsilon = 1e-08
rate_matrix = 0.05
rate_vector = 0.3
weight_decay = 0.05
root_half = 0.7071067811865476
inverse_root_two_pi = 0.3989422804014327

bf16 = jnp.bfloat16
f32 = jnp.float32
BOTH = ("group", "dp")
VMEM_SPEC = pl.BlockSpec(memory_space=pltpu.VMEM)
ANY_SPEC = pl.BlockSpec(memory_space=pl.ANY)
MIB = 1 << 20
GATHER = dict(attn=3.0, up=18.0, up_gap=10.0, down=38.0, two=2.0, third=4.0, near=4.5, four=6.0, five=8.0, loop=23.5, gap=0.9)
FEED = (6, 8, 9, 10, 11, 15)
TAIL = {
    0: ((0, 2), (1, -1), (1, 0)),
    2: ((2, -1),),
    3: ((1, 1), (3, -1)),
    4: ((3, 0),),
    6: ((4, -1),),
    7: ((2, 0),),
    11: ((0, 3), (1, 2)),
    21: ((3, 1),),
    26: ((1, 3), (0, 4)),
    30: ((2, 1),),
    34: ((5, -1), (5, 0)),
    35: ((3, 2),),
    40: ((2, 2),),
    41: ((3, 3), (5, 1), (1, 4)),
    42: ((4, 0), (6, -1), (5, 2), (2, 3), (9, 10), (3, 4), (6, 0), (4, 1), (5, 3), (6, 1), (2, 4), (9, 11), (0, 5), (6, 2), (5, 4), (1, 5), (6, 3), (4, 2), (3, 5), (9, 12), (4, 3), (9, 13), (2, 5), (6, 4), (9, 14), (5, 5), (2, 6), (9, 15), (4, 4), (9, 16), (0, 6), (5, 6), (6, 5), (4, 5), (4, 6), (1, 6), (3, 6), (6, 6)),
}


def mm(a, b):
    return jnp.dot(a, b, preferred_element_type=f32)


def mm_nt(a, b):
    return lax.dot_general(a, b, (((1,), (1,)), ((), ())), preferred_element_type=f32)


def mm_tn(a, b):
    return lax.dot_general(a, b, (((0,), (0,)), ((), ())), preferred_element_type=f32)


def sds(shape, dtype):
    return jax.ShapeDtypeStruct(shape, dtype)


def params(mib, **more):
    return pltpu.CompilerParams(vmem_limit_bytes=mib * MIB, **more)


def cost(flops, nbytes):
    return pl.CostEstimate(flops=int(flops), bytes_accessed=int(nbytes), transcendentals=0)


def layer_stats(values):
    centre = jnp.mean(values, axis=-1, keepdims=True)
    centred = values - centre
    variance = jnp.mean(centred * centred, axis=-1, keepdims=True)
    inverse = lax.rsqrt(variance + norm_epsilon)
    return centred * inverse, inverse


def norm_back(grad_normed, normal, inverse, gain):
    scaled = grad_normed * gain
    mean_one = jnp.mean(scaled, axis=-1, keepdims=True)
    mean_two = jnp.mean(scaled * normal, axis=-1, keepdims=True)
    return inverse * (scaled - mean_one - normal * mean_two)


def picker(keep_row, rows):
    image = keep_row.shape[1]
    ahead = lax.broadcasted_iota(jnp.int32, (image, image), 0)
    here = lax.broadcasted_iota(jnp.int32, (image, image), 1)
    upper = jnp.where(ahead <= here, 1.0, 0.0).astype(bf16)
    kept = keep_row.astype(f32)
    place = mm(kept.astype(bf16), upper) - 1.0
    place = jnp.where(kept > 0.5, place, -1.0)
    want = lax.broadcasted_iota(jnp.int32, (rows, image), 0).astype(f32)
    return jnp.where(place == want, 1.0, 0.0).astype(bf16)


MESH = pl.DeviceIdType.MESH


def flip(value, bit):
    return value + bit - 2 * bit * ((value // bit) % 2)


class Place:
    def __init__(self):
        self.group, self.replica = lax.axis_index("group"), lax.axis_index("dp")
        self.core, self.level = self.replica % 2, (self.replica // 2) % 2
        self.inner = (self.level + self.replica // 4) % 2
        one, two = flip(self.group, 1), flip(self.group, 2)
        self.first = (1 - self.core) * one + self.core * two
        self.second = (1 - self.core) * two + self.core * one
        self.third = flip(one, 2)
        self.to_first = (self.first, self.replica)
        self.to_second = (self.second, self.replica)
        self.to_third = (self.third, self.replica)
        self.to_core = (self.group, flip(self.replica, 1))

    @property
    def to_middle(self):
        return (self.group, flip(flip(self.replica, 2), 4))

    def to_bit(self, bit):
        return (self.group, flip(self.replica, bit))

    def meet(self, partners):
        barrier = pltpu.get_barrier_semaphore()
        for partner in partners:
            pl.semaphore_signal(barrier, inc=1, device_id=partner, device_id_type=MESH)
        pl.semaphore_wait(barrier, len(partners))


class Timeline:
    def __init__(self):
        self.steps = []

    def add(self, when, step):
        self.steps.append((when, len(self.steps), step))
        self.steps.sort(key=lambda one: one[:2])

    def until(self, when):
        while self.steps and self.steps[0][0] <= when:
            self.steps.pop(0)[2]()

    def during(self, count, start, gap):
        due = []
        while self.steps and self.steps[0][0] < start + count * gap:
            when, _, step = self.steps.pop(0)
            due.append((min(max(int((when - start) / gap), 0), count - 1), step))

        def run(turn):
            for at, step in due:
                pl.when(turn == at)(step)

        return run


class Gather:
    def __init__(self, place, own, full, cols, send, recv):
        self.place, self.own, self.full, self.cols, self.send, self.recv = place, own, full, cols, send, recv
        deep = own.shape[0]
        self.deep, self.strip = deep, 5 * deep // 16
        self.main = deep - self.strip
        self.main_at = place.level * self.strip
        self.strip_at = place.level * self.main

    def block(self, owner, start, size, core=None):
        at = pl.multiple_of(owner * self.deep + start, 16)
        return self.full.at[self.place.core if core is None else core, pl.ds(at, size), self.cols]

    def whole(self, owner, core=None):
        return self.block(owner, 0, self.deep, core)

    def copy(self, k):
        p = self.place
        main, strip, whole = (self.main_at, self.main), (self.strip_at, self.strip), (0, self.deep)
        owner, (at, size), device = (
            (p.group, main, p.to_first),
            (p.group, main, p.to_second),
            (p.first, main, p.to_second),
            (p.first, strip, p.to_bit(2)),
            (p.second, strip, p.to_bit(2)),
            (p.third, strip, p.to_bit(2)),
            (p.group, whole, p.to_core),
            (p.first, whole, p.to_core),
            (p.second, whole, p.to_core),
            (p.third, whole, p.to_core),
        )[k]
        dst = self.block(owner, at, size)
        src = dst
        if k in (0, 1, 6):
            src = self.own.at[pl.ds(pl.multiple_of(at, 16) if k < 6 else 0, size), :]
        return pltpu.make_async_remote_copy(
            src_ref=src, dst_ref=dst, send_sem=self.send.at[k], recv_sem=self.recv.at[k],
            device_id=device, device_id_type=MESH,
        )

    def start(self, *ks):
        for k in ks:
            self.copy(k).start()

    def arrived(self, *ks):
        for k in ks:
            self.copy(k).wait_recv()

    def sent(self, *ks):
        for k in ks:
            self.copy(k).wait_send()

    def step_one(self):
        self.start(0, 1, 6)

    def step_two(self):
        self.arrived(0)
        self.start(2, 3)
        self.arrived(1)
        self.start(4)

    def step_near(self):
        self.arrived(3)
        self.start(7)
        self.arrived(4)
        self.start(8)

    def step_third(self):
        self.arrived(2)
        self.start(5)

    def step_four(self):
        self.arrived(5)
        self.start(9)

    def step_five(self):
        self.arrived(6, 7, 8, 9)
        self.sent(*range(10))

    def schedule(self, line, start, size):
        line.add(start, self.step_one)
        line.add(start + 8 * size + GATHER["two"], self.step_two)
        line.add(start + 12 * size + GATHER["third"], self.step_third)
        line.add(start + 14 * size + GATHER["near"], self.step_near)
        line.add(start + 16 * size + GATHER["four"], self.step_four)
        line.add(start + 17 * size + GATHER["five"], self.step_five)


def head_masks():
    lane = lax.broadcasted_iota(jnp.int32, (1, 2 * HEAD), 1)
    low = jnp.where(lane < HEAD, 1.0, 0.0)
    return low.astype(bf16), (1.0 - low).astype(bf16), low > 0.5


def two_heads(x, low, high):
    return jnp.concatenate([x * low, x * high], axis=0)


def pick_heads(both, first):
    rows = both.shape[0] // 2
    return jnp.where(first, both[:rows], both[rows:])


def pair_probs(q_pair, k_pair, counts, n):
    raw = mm_nt(q_pair, k_pair) * (1.0 / math.sqrt(HEAD))
    col = lax.broadcasted_iota(jnp.int32, raw.shape, 1)
    raw = jnp.where(col < counts[pl.ds(n, 1), :][:, 0 : raw.shape[1]], raw, -1e30)
    top = jnp.max(raw, axis=-1, keepdims=True)
    exponent = jnp.exp(raw - top)
    return exponent / jnp.sum(exponent, axis=-1, keepdims=True)


def attend_kernel(seqs, buf, *refs):
    keep, vectors, mats, down, tokens, cot = refs[:6]
    w_attn, w_up, w_down, own_down, x_out, em_out, h1_out, qkv_out, o_out, r_out, h2_out, vec, stats, counts = refs[6:20]
    x, em, h1, qkv, o, r, h2, outs, wbuf, wide, tall, low_up, low_down, rows_in, parts, send, recv, vec_send, vec_recv, loads, stores, reads = refs[20:]
    rows = h1.shape[0] // seqs
    d = h1.shape[1]
    half = d // 2
    place = Place()
    core = place.core
    deep = mats.shape[0]

    takes = []
    for j in range(8):
        at = pl.ds(pl.multiple_of((2 * j + core) * half, half), half)
        takes.append(
            pltpu.make_async_copy(mats.at[:, at], wide.at[j // 4, :, pl.ds((j % 4) * half, half)], loads.at[j])
        )
    takes.append(
        pltpu.make_async_copy(down.at[pl.ds(pl.multiple_of(core * half, half), half), :], tall, loads.at[8])
    )
    for one in takes:
        one.start()
    reads_in = []
    for n in range(seqs):
        for k, src in enumerate((tokens, cot)):
            reads_in.append(pltpu.make_async_copy(src.at[n], rows_in.at[k, n], reads.at[k, n]))
    for one in reads_in:
        one.start()

    place.meet((place.to_first, place.to_second, place.to_third, place.to_core, place.to_bit(2)))

    part = vectors.shape[1]
    parts[place.group] = jnp.concatenate([vectors[...], jnp.zeros((4, part), f32)], axis=0).astype(bf16)
    for k, partner in enumerate((place.to_first, place.to_second, place.to_third)):
        pltpu.make_async_remote_copy(
            src_ref=parts.at[place.group], dst_ref=parts.at[place.group],
            send_sem=vec_send.at[k], recv_sem=vec_recv.at[k], device_id=partner, device_id_type=MESH,
        ).start()

    own_rows = pl.ds(pl.multiple_of(place.group * deep, deep), deep)
    line = Timeline()
    attn = []
    for j in range(4):
        cols = pl.ds(j * half, half)
        own = wbuf.at[core, own_rows, cols]
        takes[j].wait()
        own[...] = wide[0, :, cols].astype(bf16)
        attn.append(Gather(place, own, wbuf, cols, send.at[j], recv.at[j]))
        attn[j].schedule(line, GATHER["attn"] * j, 0.5)
        if j == 0:
            line.until(0)
    ups = []
    for j in range(2):
        cols = pl.ds(j * d, d)
        for one in takes[4 + 2 * j : 6 + 2 * j]:
            one.wait()
        low_up[j] = wide[1, :, cols].astype(bf16)
        ups.append(Gather(place, low_up.at[j], w_up, cols, send.at[4 + j], recv.at[4 + j]))
        ups[j].schedule(line, GATHER["up"] + GATHER["up_gap"] * j, 1.0)
    takes[8].wait()
    for j in range(2):
        low_down[j] = tall[j * deep : (j + 1) * deep, :].astype(bf16)
    early = Gather(place, low_down.at[0], w_down, pl.ds(0, d), send.at[6], recv.at[6])
    early.schedule(line, GATHER["down"], 1.0)
    keeps = [
        pltpu.make_async_copy(one.own, one.whole(place.group), stores.at[k]) for k, one in enumerate(ups + [early])
    ]
    keeps.append(pltpu.make_async_copy(low_down.at[1], own_down, stores.at[3]))
    for one in keeps:
        one.start()

    def keep_out(k, src, dst):
        one = pltpu.make_async_copy(src, dst, outs.at[k])
        one.start()
        keeps.append(one)

    kept = jnp.sum(keep[...], axis=1, keepdims=True) + buf
    counts[0:seqs, :] = jnp.broadcast_to(kept, keep.shape)
    counts[2 * seqs : 3 * seqs, :] = keep[...]

    for one in reads_in:
        one.wait()
    due_pack = line.during(seqs, 4.0, 1.0)

    @pl.loop(0, seqs)
    def _(n):
        due_pack(n)
        at = pl.multiple_of(n * rows, 16)
        pick = picker(counts[pl.ds(2 * seqs + n, 1), :], rows - buf)
        for k, dst in ((0, x), (1, em)):
            dst[pl.ds(at, buf), :] = rows_in[k, n, 0:buf, :]
            dst[pl.ds(pl.multiple_of(at + buf, 16), rows - buf), :] = mm(pick, rows_in[k, n, buf:, :]).astype(bf16)

    for k in range(3):
        pltpu.make_async_remote_copy(
            src_ref=parts.at[place.group], dst_ref=parts.at[place.group],
            send_sem=vec_send.at[k], recv_sem=vec_recv.at[k], device_id=place.to_first, device_id_type=MESH,
        ).wait()
    vec[...] = jnp.zeros_like(vec)
    for s in range(4):
        vec[:, s * part : (s + 1) * part] = parts[s].astype(f32)
    due_norm = line.during(seqs, 8.0, 0.7)

    @pl.loop(0, seqs)
    def _(n):
        due_norm(n)
        at = pl.ds(pl.multiple_of(n * rows, 16), rows)
        normal, _ = layer_stats(x[at, :].astype(f32))
        h1[at, :] = (normal * vec[0:1, :] + vec[1:2, :]).astype(bf16)

    keep_out(0, x, x_out)
    keep_out(1, em, em_out)
    keep_out(2, h1, h1_out)
    tile = half // 2
    for j in range(3):
        line.until(GATHER["attn"] * j + 17 * 0.5 + GATHER["five"])

        @pl.loop(0, 4)
        def _(i):
            h, t = i // 2, i % 2
            near = pl.multiple_of(i * tile, tile)
            w = wbuf[h, :, pl.ds(pl.multiple_of(j * half + t * tile, tile), tile)]
            got = mm(h1[...], w)
            if j != 1:
                got = got + vec[2 + j // 2 : 3 + j // 2, pl.ds(near, tile)]
            qkv[:, pl.ds(pl.multiple_of(j * d + near, tile), tile)] = got.astype(bf16)

    keep_out(3, qkv, qkv_out)
    low, high, first = head_masks()
    pairs = d // (2 * HEAD)
    loop_at, turn = GATHER["loop"], GATHER["gap"]
    due = line.during(seqs * pairs, loop_at, turn)
    mix_at = loop_at + seqs * pairs * turn

    @pl.loop(0, seqs * pairs)
    def _(i):
        due(i)
        n, j = i // pairs, i % pairs
        at = pl.ds(pl.multiple_of(n * rows, 16), rows)
        lanes = [pl.ds(pl.multiple_of(j * 2 * HEAD + m * d, 2 * HEAD), 2 * HEAD) for m in range(3)]
        q_pair = two_heads(qkv[at, lanes[0]], low, high)
        probs = pair_probs(q_pair, qkv[at, lanes[1]], counts, n).astype(bf16)
        o[at, lanes[0]] = pick_heads(mm(probs, qkv[at, lanes[2]]), first).astype(bf16)

    keep_attn = pltpu.make_async_copy(wbuf, w_attn, stores.at[4])
    keep_attn.start()
    keep_out(4, o, o_out)
    due_mix = line.during(4, mix_at, 1.0)

    @pl.loop(0, 4)
    def _(i):
        due_mix(i)
        h, t = i // 2, i % 2
        near = pl.ds(pl.multiple_of(i * tile, tile), tile)
        w = wbuf[h, :, pl.ds(pl.multiple_of(3 * half + t * tile, tile), tile)]
        r[:, near] = mm(o[...], w) + vec[4:5, near]

    due_last = line.during(seqs, mix_at + 4, 1.5)
    stats[...] = jnp.zeros_like(stats)

    @pl.loop(0, seqs)
    def _(n):
        due_last(n)
        at = pl.ds(pl.multiple_of(n * rows, 16), rows)
        valid = lax.broadcasted_iota(jnp.int32, (rows, 1), 0) < counts[pl.ds(n, 1), :][:, 0:1]
        valid = jnp.where(valid, 1.0, 0.0)
        inputs = x[at, :].astype(f32)
        branch = r[at, :]
        resid = inputs + branch
        r[at, :] = resid
        normal, _ = layer_stats(resid)
        h2[at, :] = (normal * vec[5:6, :] + vec[6:7, :]).astype(bf16)
        stats[0:1, :] += jnp.sum(inputs * inputs * valid, axis=0, keepdims=True)
        stats[1:2, :] += jnp.sum(branch * branch * valid, axis=0, keepdims=True)

    keep_out(5, r, r_out)
    keep_out(6, h2, h2_out)
    line.until(1e9)
    for one in keeps:
        one.wait()
    keep_attn.wait()


class Reduce:
    def __init__(self, place, bits, g, r1, r2, r3, r4, far, total, send, recv, home=None):
        self.place, self.bits, self.g, self.r1, self.r2, self.r3, self.r4 = place, bits, g, r1, r2, r3, r4
        self.far, self.total, self.send, self.recv = far, total, send, recv
        self.home = place.group if home is None else home

    def copy(self, k):
        p = self.place
        plans = [
            lambda: (self.g.at[p.third], self.r1.at[1], p.to_first),
            lambda: (self.g.at[p.first], self.r1.at[0], p.to_first),
            lambda: (self.g.at[p.second], self.r2, p.to_second),
            lambda: (self.g.at[self.home], self.r3, p.to_bit(2)),
            lambda: (self.r2, self.total.at[p.core], p.to_bit(2)),
            lambda: (self.r2, self.total.at[p.core], p.to_core),
            lambda: (self.total.at[p.core], self.total.at[p.core], p.to_core),
            lambda: (self.r1.at[0], self.r4, p.to_middle),
        ]
        for n, bit in enumerate(self.bits):
            plans.append(lambda n=n, bit=bit: (self.far.at[n, 0], self.far.at[n, 1], p.to_bit(bit)))
        src, dst, device = plans[k]()
        return pltpu.make_async_remote_copy(
            src_ref=src, dst_ref=dst, send_sem=self.send.at[k], recv_sem=self.recv.at[k],
            device_id=device, device_id_type=MESH,
        )

    def begin(self):
        self.copy(0).start()
        self.copy(1).start()

    def sent(self, *ks):
        for k in ks:
            self.copy(k).wait_send()

    def pass_second(self):
        self.copy(0).wait_recv()
        at = self.place.second
        self.g[at] = (self.g[at].astype(f32) + self.r1[1].astype(f32)).astype(bf16)
        self.copy(2).start()

    def settle(self):
        self.copy(1).wait_recv()
        self.copy(2).wait_recv()
        at = self.place.group
        self.g[at] = (self.g[at].astype(f32) + self.r1[0].astype(f32) + self.r2[...].astype(f32)).astype(bf16)

    def pass_in(self):
        pl.when(self.place.inner == 0)(self.copy(3).start)

    def pass_middle(self):
        @pl.when(self.place.inner == 1)
        def _():
            self.copy(3).wait_recv()
            value = self.g[self.home].astype(f32) + self.r3[...].astype(f32)
            self.r1[0] = value.astype(bf16)
            self.copy(7).start()

    def pass_out(self):
        @pl.when(self.place.inner == 1)
        def _():
            self.copy(7).wait_recv()
            self.r2[...] = (self.r1[0].astype(f32) + self.r4[...].astype(f32)).astype(bf16)
            for n in range(len(self.bits)):
                pltpu.sync_copy(self.r2, self.far.at[n, 0])
                self.copy(8 + n).start()
                self.copy(8 + n).wait()
                pltpu.sync_copy(self.far.at[n, 1], self.r3)
                self.r2[...] = (self.r2[...].astype(f32) + self.r3[...].astype(f32)).astype(bf16)
            self.copy(4).start()
            self.copy(5).start()
            self.stay().start()

    def stay(self):
        return pltpu.make_async_copy(self.r2, self.total.at[self.place.core], self.send.at[8 + len(self.bits)])

    def pass_core(self):
        @pl.when(self.place.inner == 0)
        def _():
            self.copy(4).wait_recv()
            self.copy(6).start()

    def finish(self, whole=True):
        if whole:
            self.sent(0, 1, 2)

        @pl.when(self.place.inner == 1)
        def _():
            self.copy(5).wait_recv()
            self.sent(4, 5, 7)
            self.stay().wait()

        @pl.when(self.place.inner == 0)
        def _():
            self.copy(6).wait_recv()
            self.sent(3, 6)


def block_grads(place, sides, wide, g):
    quarter = sides.shape[2] // 4

    @pl.loop(0, 4)
    def _(i):
        near = place.first * (1 - i // 2) + place.group * (i // 2)
        over = ((i + 1) // 2) % 2
        owner = near * (1 - over) + ((1 - place.core) * flip(near, 2) + place.core * flip(near, 1)) * over
        cols = pl.ds(pl.multiple_of(owner * quarter, quarter), quarter)
        g[owner] = mm_tn(sides[0, :, cols], sides[1, :, 0:wide]).astype(bf16)


def swap_start(place, src, dst, send, recv, k):
    copy = pltpu.make_async_remote_copy(
        src_ref=src, dst_ref=dst, send_sem=send.at[k], recv_sem=recv.at[k],
        device_id=place.to_core, device_id_type=MESH,
    )
    copy.start()
    return copy


def feed_kernel(seqs, buf, *refs):
    counts, h2, em, vec, h2_hbm, em_hbm, r_hbm, ups, downs, own_down = refs[:10]
    sums, er_hbm, ea_hbm, out_hbm, part_sum, z_mine, z_got, u_mine, u_got, h2_got, em_got = refs[10:21]
    r, er, ea, out, wup, wdown, m_acc, t_acc, z_all, u_all, sides, g, r1, r2 = refs[21:35]
    sems, w_sems, o_sems, send, recv, g_send, g_recv, k_sems, t_send, t_recv, r_send, r_recv = refs[35:]
    total, d = h2.shape
    rows = total // seqs
    strip = wup.shape[2] // 4
    tile = strip // 2
    place = Place()
    core = place.core
    late = Gather(place, wdown.at[1, core, pl.ds(pl.multiple_of(place.group * tile, tile), tile)], wdown.at[1], pl.ds(0, d), g_send, g_recv)
    take_own = pltpu.make_async_copy(own_down, late.own, sems.at[0])
    take_own.start()
    take_r = pltpu.make_async_copy(r_hbm, r, sems.at[1])

    def owner_at(turn):
        near = place.group * (1 - turn % 2) + place.first * (turn % 2)
        over = turn // 2
        return near * (1 - over) + ((1 - core) * flip(near, 2) + core * flip(near, 1)) * over

    def takes(i):
        turn, away = i // 2, i % 2
        h = (1 - core) * away + core * (1 - away)
        s = owner_at(turn)
        cols = pl.ds(pl.multiple_of(s * strip, strip), strip)
        at = pl.ds(pl.multiple_of(s * tile, tile), tile)
        return [
            pltpu.make_async_copy(ups.at[h, :, cols], wup.at[h, :, cols], w_sems.at[i, 0]),
            pltpu.make_async_copy(downs.at[h, at], wdown.at[0, h, at], w_sems.at[i, 1]),
        ]

    for i in range(8):
        for one in takes(i):
            one.start()
    take_r.start()
    place.meet((place.to_core, place.to_second, place.to_first, place.to_bit(2)))
    take_own.wait()
    late.step_one()
    swaps = [
        swap_start(place, em_hbm, em_got, send, recv, 0),
        swap_start(place, h2_hbm, h2_got, send, recv, 1),
    ]
    reduce = Reduce(place, (), g, r1, r2, None, None, None, None, r_send, r_recv)
    sides[1, 0:total, :] = em[...]
    take_em = pltpu.make_async_copy(em_got, sides.at[1, pl.ds(total, total)], sems.at[4])
    sums[...] = jnp.zeros_like(sums)
    m_acc[...] = jnp.zeros_like(m_acc)
    t_acc[...] = jnp.zeros_like(t_acc)

    def tile_copies(k, s, t, away):
        cols = pl.ds(pl.multiple_of(s * tile, tile), tile)
        z_to = sides.at[0, pl.ds(0 if not away else total, total), cols] if t == 0 else (z_got if away else z_mine).at[:, cols]
        pairs = (
            (z_all.at[(1 - core) if away else core, t, :, cols], z_to),
            (u_all.at[(1 - core) if away else core, t, :, cols], (u_got if away else u_mine).at[t, :, cols]),
        )
        if not away:
            return [pltpu.make_async_copy(src, dst, k_sems.at[k, n]) for n, (src, dst) in enumerate(pairs)]
        return [
            pltpu.make_async_remote_copy(
                src_ref=src, dst_ref=dst, send_sem=t_send.at[k, n], recv_sem=t_recv.at[k, n],
                device_id=place.to_core, device_id_type=MESH,
            )
            for n, (src, dst) in enumerate(pairs)
        ]

    def late_own():
        late.arrived(6)

    def late_last():
        late.arrived(7, 8, 9)
        late.sent(*range(10))

    def begin():
        take_em.wait()
        for k in range(4):
            tile_copies(k, 0, 0, False)[0].wait()
            tile_copies(k, 0, 0, True)[0].wait()
        block_grads(place, sides, d, g)
        reduce.begin()

    due = [(2, swaps[0].wait), (7, late_own), (8, begin)]
    due += zip(FEED, (late.step_two, late.step_third, late.step_near, late.step_four, late_last, reduce.pass_second))
    orders = [[(when // 2 - 4 * t, step) for when, step in due if when // 8 == t] for t in range(2)]

    for t in range(2):

        @pl.loop(0, 4)
        def _(turn):
            for when, step in orders[t]:
                pl.when(turn == when)(step)
            if t == 0:
                pl.when(turn == 1)(take_em.start)
                for away in range(2):
                    for one in takes(2 * turn + away):
                        one.wait()
            s = owner_at(turn)
            cols = pl.ds(pl.multiple_of(s * strip + t * tile, tile), tile)
            near = pl.ds(pl.multiple_of(s * tile, tile), tile)
            parts = []
            for away in range(2):
                h = (1 - core) * away + core * (1 - away)
                far = (pl.ds(8 + s, 1), pl.ds(pl.multiple_of(h * strip + t * tile, tile), tile))
                w_up = wup[h, :, cols]
                w_down = wdown[t, h, near, :]
                u = mm(h2[...], w_up) + vec[far]
                phi = 0.5 * (1.0 + lax.erf(u * root_half))
                z = (u * phi).astype(bf16)
                z_all[h, t, :, near] = z
                slope = phi + u * jnp.exp(-0.5 * u * u) * inverse_root_two_pi
                eu = (mm_nt(em[...], w_down) * slope).astype(bf16)
                u_all[h, t, :, near] = eu
                sums[far] = jnp.sum(eu.astype(f32), axis=0, keepdims=True)
                for one in tile_copies(4 * t + turn, s, t, away == 1):
                    one.start()
                parts.append((z, eu, w_up, w_down))
            z_pair, u_pair = (jnp.concatenate([part[k] for part in parts], axis=1) for k in range(2))
            m_acc[...] += mm(z_pair, jnp.concatenate([part[3] for part in parts], axis=0))
            t_acc[...] += mm_nt(u_pair, jnp.concatenate([part[2] for part in parts], axis=1))

    take_r.wait()

    def results(n):
        at = pl.ds(pl.multiple_of(n * rows, 16), rows)
        return [
            pltpu.make_async_copy(er.at[at], er_hbm.at[at], o_sems.at[n, 0]),
            pltpu.make_async_copy(ea.at[at], ea_hbm.at[at], o_sems.at[n, 1]),
            pltpu.make_async_copy(out.at[n], out_hbm.at[n], o_sems.at[n, 2]),
        ]

    @pl.loop(0, seqs)
    def _(n):
        at = pl.ds(pl.multiple_of(n * rows, 16), rows)
        valid = lax.broadcasted_iota(jnp.int32, (rows, 1), 0) < counts[pl.ds(n, 1), :][:, 0:1]
        valid = jnp.where(valid, 1.0, 0.0)
        resid = r[at, :]
        m = m_acc[at, :] + vec[7:8, :]
        packed = ((resid + m) * valid).astype(bf16)
        out[n, 0:buf, :] = packed[0:buf]
        pick = picker(counts[pl.ds(2 * seqs + n, 1), :], rows - buf)
        out[n, buf:, :] = mm_tn(pick, packed[buf:]).astype(bf16)
        normal, inverse = layer_stats(resid)
        t = t_acc[at, :]
        low = em[at, :].astype(f32)
        back = low + norm_back(t, normal, inverse, vec[5:6, :])
        er[at, :] = back
        ea_low = back.astype(bf16)
        ea[at, :] = ea_low
        sums[4:5, :] += jnp.sum(ea_low.astype(f32), axis=0, keepdims=True)
        sums[5:6, :] += jnp.sum(t * normal, axis=0, keepdims=True)
        sums[6:7, :] += jnp.sum(t, axis=0, keepdims=True)
        sums[7:8, :] += jnp.sum(low, axis=0, keepdims=True)
        sums[12:13, :] += jnp.sum(m * m * valid, axis=0, keepdims=True)
        for one in results(n):
            one.start()
    reduce.settle()
    share = pltpu.make_async_copy(g.at[place.group], part_sum, sems.at[0])
    share.start()
    for n in range(seqs):
        for one in results(n):
            one.wait()
    swaps[1].wait()
    reduce.sent(0, 1, 2)
    share.wait()
    for k in range(8):
        for away in (False, True):
            for one in tile_copies(k, 0, k // 4, away)[0 if k >= 4 else 1 :]:
                one.wait()


def tail_kernel(seqs, buf, bits, sizes, *refs):
    counts, vec, stats, sums_feed, qkv_hbm, x_hbm, er_hbm = refs[:7]
    part_sum, z_mine, z_got, em, em_got, h2, h2_got, u_mine, u_got, o, ea, h1, w_attn = refs[7:20]
    chunks = len(sizes)
    small, out = refs[20:22]
    totals = refs[22 : 22 + chunks]
    o_got, ea_got, h1_got, e_got = refs[22 + chunks : 26 + chunks]
    outs = 26 + chunks + (chunks if bits else 0)
    far = refs[26 + chunks : outs] or [None] * chunks
    scratch = refs[outs:]
    qkv, er, in_sems = scratch[:3]
    scratch = scratch[3:]
    wbuf, eo, e, t_acc, stage, sides, small_in = scratch[:7]
    buffers = [scratch[7 + k * chunks : 7 + (k + 1) * chunks] for k in range(5)]
    send, recv, w_sem, ea_sem, first_sem, side_sems, stage_sem, swap_send, swap_recv, small_send, small_recv = scratch[7 + 5 * chunks :]
    total, d = eo.shape
    rows = total // seqs
    half, quarter = d // 2, d // 4
    place = Place()
    core = place.core

    o_weight = pltpu.make_async_copy(w_attn.at[:, :, pl.ds(3 * half, half)], wbuf.at[:, :, pl.ds(0, half)], w_sem)
    o_weight.start()
    ea_all = e.at[0, :, pl.ds(0, d)]
    take_ea = pltpu.make_async_copy(ea, ea_all, ea_sem)
    take_ea.start()

    mine_cols = pl.ds(pl.multiple_of(core * half, half), half)
    left = [None, (z_mine, z_got), (h2, h2_got), (h2, h2_got), (o, o_got), (h1, h1_got), (h1, h1_got)]
    right = [
        None, (em, em_got),
        (u_mine.at[0], u_got.at[0]), (u_mine.at[1], u_got.at[1]),
        (ea.at[:, mine_cols], ea_got.at[:, mine_cols]),
        (e.at[core, :, pl.ds(0, d)], e_got.at[:, pl.ds(0, d)]), (e.at[core, :, pl.ds(d, half)], e_got.at[:, pl.ds(d, half)]),
    ]

    def side_copies(k):
        found = []
        for side, pairs in enumerate((left, right)):
            wide = sizes[k] if side else d
            for which, src in enumerate(pairs[k]):
                dst = sides.at[k % 2, side, pl.ds(which * total, total), pl.ds(0, wide)]
                found.append(pltpu.make_async_copy(src, dst, side_sems.at[k % 2, side, which]))
        return found

    def load_sides(k):
        for one in side_copies(k):
            one.start()

    load_sides(1)
    load_sides(2)
    inputs = [
        pltpu.make_async_copy(src, dst, in_sems.at[k])
        for k, (src, dst) in enumerate(((qkv_hbm, qkv), (er_hbm, er)))
    ]
    for one in inputs:
        one.start()
    partners = [place.to_first, place.to_second, place.to_core, place.to_bit(2), place.to_bit(4), place.to_middle]
    partners += [place.to_bit(b) for b in bits]
    place.meet(partners)
    swaps = [
        swap_start(place, o, o_got, swap_send, swap_recv, 0),
        swap_start(place, ea, ea_got, swap_send, swap_recv, 1),
        swap_start(place, h1, h1_got, swap_send, swap_recv, 2),
    ]
    sent_e = pltpu.make_async_remote_copy(
        src_ref=e.at[1 - core], dst_ref=e_got, send_sem=swap_send.at[3], recv_sem=swap_recv.at[3],
        device_id=place.to_core, device_id_type=MESH,
    )
    reduces = [
        Reduce(place, bits, *(buffers[b][k] for b in range(5)), far[k], totals[k], send.at[k], recv.at[k], None if k else 0) for k in range(chunks)
    ]

    first_sum = pltpu.make_async_copy(part_sum, buffers[0][0].at[0], first_sem)
    first_sum.start()

    def gradient(k):
        for one in side_copies(k):
            one.wait()
        block_grads(place, sides.at[k % 2], sizes[k], reduces[k].g)

    def act(k, step):
        if k == 9:
            last = step == 16
            for n in range(step - 10, len(hops) + 1 if last else step - 9):
                small_step(n)
            return
        one = reduces[k]
        if step == -1:
            gradient(k)
            if k == 1:
                load_sides(3)
            if k == 2:
                for swap in swaps[:2]:
                    swap.wait()
                load_sides(4)
        elif step == 0:
            one.begin()
        elif step == 1:
            one.pass_second()
        elif step == 2:
            if k == 0:
                first_sum.wait()
            else:
                one.settle()
            one.pass_in()
        elif step == 3:
            one.pass_middle()
        elif step == 4:
            one.pass_out()
        elif step == 5:
            one.pass_core()
        else:
            one.finish(k > 0)

    def due(slot, turn=None, count=1):
        for n in range(count):
            steps = TAIL.get(slot + n, ())

            def run(steps=steps):
                for k, step in steps:
                    act(k, step)

            if turn is None:
                run()
            elif steps:
                pl.when(turn == n)(run)

    due(0)
    o_weight.wait()
    take_ea.wait()
    for one in inputs:
        one.wait()

    @pl.loop(0, 4)
    def _(s):
        near = pl.ds(pl.multiple_of(s * quarter, quarter), quarter)
        got = mm_nt(ea_all[:, 0:half], wbuf[0, near, 0:half]) + mm_nt(ea_all[:, half:], wbuf[1, near, 0:half])
        eo[:, near] = got.astype(bf16)

    in_weight = pltpu.make_async_copy(w_attn.at[:, :, pl.ds(0, 3 * half)], wbuf, w_sem)
    in_weight.start()
    low, high, first = head_masks()
    pairs = half // (2 * HEAD)
    scale = 1.0 / math.sqrt(HEAD)
    small[...] = jnp.zeros_like(small)
    turns = seqs * pairs

    planned = 32

    @pl.loop(0, 2 * turns)
    def _(i):
        pl.when(i == turns)(sent_e.start)
        due(1, i, planned)
        h = (1 - core) * (1 - i // turns) + core * (i // turns)
        n, j = (i % turns) // pairs, i % pairs
        at = pl.ds(pl.multiple_of(n * rows, 16), rows)
        far = h * half + j * 2 * HEAD
        lanes = [pl.ds(pl.multiple_of(far + m * d, 2 * HEAD), 2 * HEAD) for m in range(3)]
        k_pair = qkv[at, lanes[1]]
        q_both = two_heads(qkv[at, lanes[0]], low, high)
        probs = pair_probs(q_both, k_pair, counts, n)
        eo_both = two_heads(eo[at, lanes[0]], low, high)
        ep = mm_nt(eo_both, qkv[at, lanes[2]])
        inner = jnp.sum(probs * ep, axis=-1, keepdims=True)
        es = (probs * (ep - inner)).astype(bf16)
        ev = mm_tn(probs.astype(bf16), eo_both).astype(bf16)
        eq = (pick_heads(mm(es, k_pair), first) * scale).astype(bf16)
        ek = (mm_tn(es, q_both) * scale).astype(bf16)
        for m, value in enumerate((eq, ek, ev)):
            e[h, at, pl.ds(pl.multiple_of(m * half + j * 2 * HEAD, 2 * HEAD), 2 * HEAD)] = value
        small[2:3, lanes[0]] += jnp.sum(eq.astype(f32), axis=0, keepdims=True)
        small[3:4, lanes[0]] += jnp.sum(ev.astype(f32), axis=0, keepdims=True)

    due(1 + planned)
    take_x = pltpu.make_async_copy(x_hbm, eo, in_sems.at[2])
    take_x.start()
    x = eo
    sent_e.wait()
    swaps[2].wait()
    load_sides(5)
    load_sides(6)
    in_weight.wait()
    take_x.wait()
    @pl.loop(0, 4)
    def _(s):
        due(2 + planned, s, 4)
        near = pl.ds(pl.multiple_of(s * quarter, quarter), quarter)
        t_acc[:, near] = mm_nt(e[0], wbuf[0, near, :]) + mm_nt(e[1], wbuf[1, near, :])

    @pl.loop(0, seqs)
    def _(n):
        due(6 + planned, n, 4)
        at = pl.ds(pl.multiple_of(n * rows, 16), rows)
        normal, inverse = layer_stats(x[at, :].astype(f32))
        t = t_acc[at, :]
        grad = er[at, :] + norm_back(t, normal, inverse, vec[0:1, :])
        small[0:1, :] += jnp.sum(t * normal, axis=0, keepdims=True)
        small[1:2, :] += jnp.sum(t, axis=0, keepdims=True)
        write = pltpu.make_async_copy(stage, out.at[n], stage_sem)

        @pl.when(n > 0)
        def _():
            write.wait()

        stage[0:buf, :] = grad[0:buf]
        pick = picker(counts[pl.ds(2 * seqs + n, 1), :], rows - buf)
        rest = grad[buf:]
        top = rest.astype(bf16)
        rest = rest - top.astype(f32)
        middle = rest.astype(bf16)
        bottom = (rest - middle.astype(f32)).astype(bf16)
        stage[buf:, :] = mm_tn(pick, top) + mm_tn(pick, middle) + mm_tn(pick, bottom)
        write.start()

    pltpu.make_async_copy(stage, out.at[0], stage_sem).wait()

    small[4:12, :] = sums_feed[4:12, :]
    kept = jnp.sum(counts[0:seqs, 0:1], axis=0, keepdims=True)
    lane = lax.broadcasted_iota(jnp.int32, (1, d), 1)
    tally = jnp.where(lane == 3, kept.astype(f32), 0.0)
    for k, row in enumerate((stats[0:1, :], stats[1:2, :], sums_feed[12:13, :])):
        tally = tally + jnp.where(lane == k, jnp.sum(row, axis=1, keepdims=True), 0.0)
    small[12:13, :] = tally
    hops = [place.to_first, place.to_second] + [place.to_bit(b) for b in (1, 2, 4, *bits)]
    small_in[0, 0] = small[...]

    def hop(k):
        return pltpu.make_async_remote_copy(
            src_ref=small_in.at[k, 0], dst_ref=small_in.at[k, 1], send_sem=small_send.at[k], recv_sem=small_recv.at[k],
            device_id=hops[k], device_id_type=MESH,
        )

    def small_step(k):
        if k > 0:
            hop(k - 1).wait()
            value = small_in[k - 1, 0] + small_in[k - 1, 1]
            if k == len(hops):
                small[...] = value
                return
            small_in[k, 0] = value
        hop(k).start()

    due(10 + planned)


def adam_math(w, f, s, grad, rate, decay):
    first_new = beta_first * f + (1.0 - beta_first) * grad
    second_new = beta_second * s + (1.0 - beta_second) * grad * grad
    fix_first = 1.0 - beta_first**STEP
    fix_second = 1.0 - beta_second**STEP
    update = first_new * (1.0 / fix_first) / (jnp.sqrt(second_new * (1.0 / fix_second)) + adam_epsilon)
    return w - rate * (update + decay * w), first_new, second_new


def adam_kernel(columns, info, *refs):
    (w, f, s, wd, fd, sd, wv, fv, sv, small, d0, d1, u0, u1, go, g1, g2) = refs[:17]
    mats, downs, vecs = refs[17:21], refs[21:25], refs[25:29]
    step = pl.program_id(0)

    def put(outs, state, grad, rate, decay):
        new, first, second = adam_math(*(one[...] for one in state), grad, rate, decay)
        for out, value in zip(outs, (new, first, second, new.astype(bf16))):
            out[...] = value

    def when(lowest, count, *parts):
        @pl.when((step >= lowest) & (step < lowest + count))
        def _():
            grad = jnp.concatenate([part[h] for h in range(2) for part in parts], axis=1)
            put(mats, (w, f, s), grad.astype(f32), rate_matrix, weight_decay)

    when(0, 2, g1)
    when(2, 1, g2)
    when(3, 1, go)
    when(4, 4, u0, u1)
    for k, part in ((0, d0), (1, d1)):

        @pl.when((step >= columns) & ((step - columns) % 2 == k))
        def _():
            put(downs, (wd, fd, sd), part[0].astype(f32), rate_matrix, weight_decay)

    @pl.when(step == 0)
    def _():
        size = wv.shape[1]
        grad = small[0:12, pl.ds(pl.multiple_of(info[0] * size, size), size)]
        put(vecs, (wv, fv, sv), grad, rate_vector, 0.0)


def adam_call(group, mats, downs, vecs, small, grads):
    deep, wide = mats[0].shape
    tile = downs[0].shape[1]
    columns, rest = wide // tile, downs[0].shape[0] // deep
    clip = lambda value, most: jnp.clip(value, 0, most - 1)
    block = (deep, tile)
    mat = pl.BlockSpec(block, lambda i, info: (0, clip(i, columns)))
    row = lambda i: clip(i - columns, rest)
    down = pl.BlockSpec(block, lambda i, info: (row(i), 0))
    vec = pl.BlockSpec(vecs[0].shape, lambda i, info: (0, 0))
    small_spec = pl.BlockSpec(small.shape, lambda i, info: (0, 0))
    down_grad = pl.BlockSpec((1, *block), lambda i, info: (row(i) // 2, 0, 0))
    halves = lambda start, count, width: pl.BlockSpec((2, deep, width), lambda i, info: (0, 0, clip(i - start, count)))
    shapes = []
    for state in (mats, downs, vecs):
        shapes += [sds(state[0].shape, f32)] * 3 + [sds(state[0].shape, bf16)]
    size = sum(one[0].size for one in (mats, downs))
    return pl.pallas_call(
        functools.partial(adam_kernel, columns),
        grid_spec=pltpu.PrefetchScalarGridSpec(
            num_scalar_prefetch=1,
            grid=(columns + rest,),
            in_specs=[mat] * 3 + [down] * 3 + [vec] * 3 + [small_spec] + [down_grad] * 2
            + [halves(4, 4, tile // 4)] * 2 + [halves(3, 1, tile // 2), halves(0, 2, tile // 2), halves(2, 1, tile // 2)],
            out_specs=[mat] * 4 + [down] * 4 + [vec] * 4,
        ),
        out_shape=shapes,
        compiler_params=params(60),
        cost_estimate=cost(20 * size, 28 * size),
    )(group, *mats, *downs, *vecs, small, *grads)


def local(groups, replicas, *args):
    tokens, keep, cot, mats, down, vectors, f_mats, f_down, f_vectors, s_mats, s_down, s_vectors = args
    seqs, length, d = tokens.shape
    image = keep.shape[1]
    buf = length - image
    rows = -(-(buf + KEEP_MAX) // 16) * 16
    total = seqs * rows
    half = d // 2
    group = lax.axis_index("group")

    deep = mats.shape[0]
    w_attn, w_up, w_down, own_down, x, em, h1, qkv, o, r, h2, vec, stats, counts = pl.pallas_call(
        functools.partial(attend_kernel, seqs, buf),
        in_specs=[VMEM_SPEC] * 2 + [ANY_SPEC] * 4,
        out_specs=[ANY_SPEC] * 11 + [VMEM_SPEC] * 3,
        out_shape=[
            sds((2, d, 2 * d), bf16),
            sds((2, d, 2 * d), bf16),
            sds((2, d, d), bf16),
            sds((deep, d), bf16),
            sds((total, d), bf16),
            sds((total, d), bf16),
            sds((total, d), bf16),
            sds((total, 3 * d), bf16),
            sds((total, d), bf16),
            sds((total, d), f32),
            sds((total, d), bf16),
            sds((16, d), f32),
            sds((8, d), f32),
            sds((4 * seqs, image), jnp.int32),
        ],
        scratch_shapes=[
            pltpu.VMEM((total, d), bf16),
            pltpu.VMEM((total, d), bf16),
            pltpu.VMEM((total, d), bf16),
            pltpu.VMEM((total, 3 * d), bf16),
            pltpu.VMEM((total, d), bf16),
            pltpu.VMEM((total, d), f32),
            pltpu.VMEM((total, d), bf16),
            pltpu.SemaphoreType.DMA((7,)),
            pltpu.VMEM((2, d, 2 * d), bf16),
            pltpu.VMEM((2, deep, 2 * d), f32),
            pltpu.VMEM((half, d), f32),
            pltpu.VMEM((2, deep, d), bf16),
            pltpu.VMEM((2, deep, d), bf16),
            pltpu.VMEM((2, seqs, length, d), bf16),
            pltpu.VMEM((4, 16, d // 4), bf16),
            pltpu.SemaphoreType.DMA((7, 10)),
            pltpu.SemaphoreType.DMA((7, 10)),
            pltpu.SemaphoreType.DMA((3,)),
            pltpu.SemaphoreType.DMA((3,)),
            pltpu.SemaphoreType.DMA((9,)),
            pltpu.SemaphoreType.DMA((5,)),
            pltpu.SemaphoreType.DMA((2, seqs)),
        ],
        compiler_params=params(60, collective_id=0, has_side_effects=True),
        cost_estimate=cost(2 * total * 4 * d * d * 4, 20 * total * d),
    )(keep, vectors, mats, down, tokens, cot)
    quarter = d // 4
    sums_feed, er, ea, block_output, part_sum, z_mine, z_got, u_mine, u_got, h2_got, em_got = pl.pallas_call(
        functools.partial(feed_kernel, seqs, buf),
        in_specs=[VMEM_SPEC] * 4 + [ANY_SPEC] * 6,
        out_specs=[VMEM_SPEC] + [ANY_SPEC] * 10,
        out_shape=[
            sds((16, d), f32),
            sds((total, d), f32),
            sds((total, d), bf16),
            sds((seqs, length, d), bf16),
            sds((quarter, d), bf16),
            sds((total, d), bf16),
            sds((total, d), bf16),
            sds((2, total, d), bf16),
            sds((2, total, d), bf16),
            sds((total, d), bf16),
            sds((total, d), bf16),
        ],
        scratch_shapes=[
            pltpu.VMEM((total, d), f32),
            pltpu.VMEM((total, d), f32),
            pltpu.VMEM((total, d), bf16),
            pltpu.VMEM((seqs, length, d), bf16),
            pltpu.VMEM((2, d, 2 * d), bf16),
            pltpu.VMEM((2, 2, d, d), bf16),
            pltpu.VMEM((total, d), f32),
            pltpu.VMEM((total, d), f32),
            pltpu.VMEM((2, 2, total, d), bf16),
            pltpu.VMEM((2, 2, total, d), bf16),
            pltpu.VMEM((2, 2 * total, d), bf16),
            pltpu.VMEM((4, quarter, d), bf16),
            pltpu.VMEM((2, quarter, d), bf16),
            pltpu.VMEM((quarter, d), bf16),
            pltpu.SemaphoreType.DMA((5,)),
            pltpu.SemaphoreType.DMA((8, 2)),
            pltpu.SemaphoreType.DMA((seqs, 3)),
            pltpu.SemaphoreType.DMA((2,)),
            pltpu.SemaphoreType.DMA((2,)),
            pltpu.SemaphoreType.DMA((10,)),
            pltpu.SemaphoreType.DMA((10,)),
            pltpu.SemaphoreType.DMA((8, 2)),
            pltpu.SemaphoreType.DMA((8, 2)),
            pltpu.SemaphoreType.DMA((8, 2)),
            pltpu.SemaphoreType.DMA((7,)),
            pltpu.SemaphoreType.DMA((7,)),
        ],
        compiler_params=params(61, collective_id=1, has_side_effects=True),
        cost_estimate=cost(2 * total * 16 * d * d, 60 * total * d),
    )(counts, h2, em, vec, h2, em, r, w_up, w_down, own_down)

    bits = []
    while (8 << len(bits)) < replicas:
        bits.append(8 << len(bits))
    sizes = (d, d, d, d, half, d, half)
    chunks, steps = len(sizes), 8 + len(bits)
    found = pl.pallas_call(
        functools.partial(tail_kernel, seqs, buf, tuple(bits), sizes),
        in_specs=[VMEM_SPEC] * 4 + [ANY_SPEC] * 16,
        out_specs=[VMEM_SPEC, ANY_SPEC] + [ANY_SPEC] * (chunks + 4 + (chunks if bits else 0)),
        out_shape=[sds((16, d), f32), sds((seqs, length, d), f32)]
        + [sds((2, quarter, wide), bf16) for wide in sizes]
        + [sds((total, d), bf16)] * 3
        + [sds((total, 3 * half), bf16)]
        + [sds((len(bits), 2, quarter, wide), bf16) for wide in sizes if bits],
        scratch_shapes=[
            pltpu.VMEM((total, 3 * d), bf16),
            pltpu.VMEM((total, d), f32),
            pltpu.SemaphoreType.DMA((3,)),
            pltpu.VMEM((2, d, 3 * half), bf16),
            pltpu.VMEM((total, d), bf16),
            pltpu.VMEM((2, total, 3 * half), bf16),
            pltpu.VMEM((total, d), f32),
            pltpu.VMEM((length, d), f32),
            pltpu.VMEM((2, 2, 2 * total, d), bf16),
            pltpu.VMEM((5 + len(bits), 2, 16, d), f32),
        ]
        + [pltpu.VMEM((4 if k else 1, quarter, wide), bf16) for k, wide in enumerate(sizes)]
        + [pltpu.VMEM((2 if k else 1, quarter, wide), bf16) for k, wide in enumerate(sizes)]
        + [pltpu.VMEM((quarter, wide), bf16) for wide in sizes]
        + [pltpu.VMEM((quarter, wide), bf16) for wide in sizes] * 2
        + [
            pltpu.SemaphoreType.DMA((chunks, steps + 1)),
            pltpu.SemaphoreType.DMA((chunks, steps)),
            pltpu.SemaphoreType.DMA(()),
            pltpu.SemaphoreType.DMA(()),
            pltpu.SemaphoreType.DMA(()),
            pltpu.SemaphoreType.DMA((2, 2, 2)),
            pltpu.SemaphoreType.DMA(()),
            pltpu.SemaphoreType.DMA((4,)),
            pltpu.SemaphoreType.DMA((4,)),
            pltpu.SemaphoreType.DMA((5 + len(bits),)),
            pltpu.SemaphoreType.DMA((5 + len(bits),)),
        ],
        compiler_params=params(61, collective_id=2, has_side_effects=True),
        cost_estimate=cost(2 * total * 16 * d * d, 100 * total * d),
    )(counts, vec, stats, sums_feed, qkv, x, er, part_sum, z_mine, z_got, em, em_got, h2, h2_got, u_mine, u_got, o, ea, h1, w_attn)
    small, input_grad = found[:2]
    grads = found[2 : 2 + chunks]
    branch_rms = jnp.sqrt(small[12, 0:3] / (small[12, 3] * d))
    new = adam_call(
        group.astype(jnp.int32).reshape(1),
        (mats, f_mats, s_mats),
        (down, f_down, s_down),
        (vectors, f_vectors, s_vectors),
        small,
        grads,
    )
    by_kind = [new[4 * part + kind] for kind in range(4) for part in range(3)]
    return (block_output, input_grad, *by_kind, branch_rms)


def solution(mesh):
    rows, owned, columns = P(BOTH, None, None), P("group", None), P(None, "group")
    state = (owned, owned, columns)
    return jax.shard_map(
        functools.partial(local, mesh.shape["group"], mesh.shape["dp"]),
        mesh=mesh,
        in_specs=(rows, P(BOTH, None), rows) + state * 3,
        out_specs=(rows, rows) + state * 4 + (P(),),
        check_vma=False,
    )
```
